128 devices in a mesh: pos: 8 (over x, core), head: 8 (over y_lo, z), chan: 2 (over y_hi).
Axes of the slice: x: 4, y: 4 (y_hi: 2, y_lo: 2; y = y_hi * 2 + y_lo), z: 4, core: 2. Of those that a mesh axis runs over, the one named last changes fastest.
Arguments:
- inputs_saved: bfloat16 [3, 32768, 1536], P(None, ('pos', 'head'), 'chan'), may hold values from -6 to 6
- conv_weight: bfloat16 [3, 3, 1536, 768], P(None, None, 'chan'), may hold values from -0.09375 to 0.09375
- expand_weight: bfloat16 [3, 768, 1536], P(None, None, 'chan'), may hold values from -0.21875 to 0.21875
- head_weight: bfloat16 [4096, 1536], P(('pos', 'head')), may hold values from -1.796875 to 1.796875
- batch_of: int32 [4096], P(('pos', 'head')), may hold values from 0 to 7
- erase_left: bfloat16 [1536, 64], replicated, may hold values from -0.15625 to 0.15625
- erase_right: bfloat16 [1536, 64], replicated, may hold values from -2.09375 to 2.09375
- bin_gradient: bfloat16 [4096, 32], P(('pos', 'head')), may hold values from -6 to 6
- cover_bins: int32 [4096, 32], P(('pos', 'head')), may hold values from 0 to 32767, as said below
Outputs:
- input_grad: bfloat16 [32768, 1536], P(('pos', 'head'), 'chan')
The draws below stay inside these ranges and needn't reach their ends.
Inputs may be any that keep to these rules, and one draw needn't show every extreme that they name: `cover_bins`: of the 2048 entries of the experiments held by one device of pos and head, at most 64 name positions of any one device; in every draw some device's positions are named by exactly 64 entries of every device. Positions may repeat within an experiment.
All inputs are finite; a program needn't handle non-finite values.
Results may differ from the reference program's by a relative error of at most 0.0095.
Values may be sent and summed in bfloat16 or wider, within the bound.
No kernel may reach another device: no remote copies, remote signals or barrier semaphores. Data moves between devices by JAX's collectives and lax.ppermute only.
A program may use at most 128 MiB of HBM per device.

```python
import jax
import jax.numpy as jnp
from jax import lax

C = 1536
C2 = 768
KW = 3
LAYERS = 3
BASE_DILATION = 4
BIN_DEV = 512
E_DEV = 64
COV = 32
NB = 8
RANK = 8
GROUP = 64
POSITIONS = 32768
EXPERIMENTS = 4096
ENTRIES = 2048
CAP = 64


def draw_cover_bins(key, part):
    hottest = jax.random.randint(jax.random.fold_in(key, 11), (), 0, GROUP)
    quarter = GROUP // 4
    placing = jnp.arange(GROUP)
    counted = jnp.where(placing < quarter, CAP, jnp.where(placing < 2 * quarter, CAP // 2, CAP // 4))
    bounds = jnp.cumsum(counted)
    slot_of = jnp.searchsorted(bounds, jnp.arange(ENTRIES), side='right')
    order_key = jax.random.fold_in(key, 12)

    def arrange(source):
        shuffled = jax.random.permutation(jax.random.fold_in(order_key, source), GROUP)
        where_hot = jnp.argmax(shuffled == hottest)
        leading = shuffled[0]
        shuffled = shuffled.at[where_hot].set(leading)
        return shuffled.at[0].set(hottest)
    orders = jax.vmap(arrange)(jnp.arange(GROUP))
    targets = orders[:, slot_of]
    offsets = jax.random.randint(jax.random.fold_in(key, 13), (GROUP, ENTRIES), 0, BIN_DEV)
    return (targets * BIN_DEV + offsets).reshape(EXPERIMENTS, COV).astype(jnp.int32)


def plant(result, stream_key, least, top_value):
    extent = result.shape
    place = [jax.random.randint(jax.random.fold_in(stream_key, axis), (), 0, extent[axis]) for axis in range(len(extent))]
    result = result.at[tuple(place)].set(least)
    longest = extent.index(max(extent))
    place[longest] = (place[longest] + 1) % extent[longest]
    return result.at[tuple(place)].set(top_value)


def block_scale(own_key, shape, cuts, smallest, high):
    level = 1.0
    for axis_at, parts in cuts:
        heights = jax.random.uniform(jax.random.fold_in(jax.random.fold_in(own_key, 6), axis_at), (parts,), jnp.float32, smallest / len(cuts), high / len(cuts))
        level = level * jnp.repeat(jnp.exp(heights), shape[axis_at] // parts).reshape((-1,) + (1,) * (len(shape) - 1 - axis_at))
    return level


def bell_draw(own_key, shape, deviation, bound, cuts=(), kind=jnp.bfloat16):
    factor_of = block_scale(own_key, shape, cuts, -0.22, 0.18) if cuts else 1.0
    result = jax.random.normal(own_key, shape, jnp.float32) * deviation * factor_of
    return jnp.minimum(jnp.maximum(result, -bound), bound).astype(kind)


def setup_inputs(seed: int = 0) -> dict:
    streams_of = jax.random.split(jax.random.key(seed), 10)
    return {
        "inputs_saved": bell_draw(streams_of[0], (LAYERS, POSITIONS, C), 1.0, 6.0, ((1, 64), (2, 2))),
        "conv_weight": bell_draw(streams_of[1], (LAYERS, KW, C, C2), (KW * C) ** -0.5, 0.09375, ((2, 2),)),
        "expand_weight": bell_draw(streams_of[2], (LAYERS, C2, C), C2 ** -0.5, 0.21875, ((2, 2),)),
        "head_weight": bell_draw(streams_of[3], (EXPERIMENTS, C), 0.3, 1.796875, ((0, 64),)),
        "batch_of": plant(jax.random.randint(streams_of[4], (EXPERIMENTS,), 0, NB), jax.random.fold_in(streams_of[4], 1), 0, NB - 1).astype(jnp.int32),
        "erase_left": bell_draw(streams_of[5], (C, NB * RANK), C ** -0.5, 0.15625),
        "erase_right": bell_draw(streams_of[6], (C, NB * RANK), 0.35, 2.09375),
        "bin_gradient": bell_draw(streams_of[7], (EXPERIMENTS, COV), 1.0, 6.0, ((0, 64),)),
        "cover_bins": draw_cover_bins(jax.random.fold_in(streams_of[9], 71), 0),
    }


def gelu_value(value):
    return 0.5 * value * (1.0 + jax.scipy.special.erf(value * 0.7071067811865476))


def gelu_slope(value):
    return 0.5 * (1.0 + jax.scipy.special.erf(value * 0.7071067811865476)) + value * jnp.exp(-0.5 * value * value) * 0.3989422804014327


def reference(inputs_saved, conv_weight, expand_weight, head_weight, batch_of, erase_left, erase_right, bin_gradient, cover_bins):
    projected = jnp.dot(head_weight, erase_left, preferred_element_type=jnp.float32)
    columns = jnp.arange(NB * RANK) // RANK
    chosen = (columns[None, :] == batch_of[:, None]).astype(jnp.float32)
    removed_rows = jnp.dot(projected * chosen, erase_right.astype(jnp.float32).T, precision=lax.Precision.HIGHEST)
    head_vectors = (head_weight.astype(jnp.float32) - removed_rows).astype(jnp.bfloat16)

    blocks = EXPERIMENTS // E_DEV
    grad_blocks = bin_gradient.reshape(blocks, E_DEV, COV)
    vector_blocks = head_vectors.reshape(blocks, E_DEV, C)
    bin_blocks = cover_bins.reshape(blocks, E_DEV, COV)

    def add_block(total, piece):
        grads, vectors, places = piece
        contrib = grads.astype(jnp.float32)[:, :, None] * vectors.astype(jnp.float32)[:, None, :]
        return total.at[places.reshape(-1)].add(contrib.reshape(-1, C)), None

    grad, _ = lax.scan(add_block, jnp.zeros((POSITIONS, C), jnp.float32), (grad_blocks, vector_blocks, bin_blocks))

    for block_level in reversed(range(LAYERS)):
        dilation_factor = BASE_DILATION * 2 ** block_level
        saved = inputs_saved[block_level].astype(jnp.float32)
        act = gelu_value(saved).astype(jnp.bfloat16)
        act_pad = jnp.pad(act, ((dilation_factor, dilation_factor), (0, 0)))
        pre = jnp.zeros((POSITIONS, C2), jnp.float32)
        for kernel_tap in range(KW):
            start = kernel_tap * dilation_factor
            pre = pre + jnp.dot(act_pad[start:start + POSITIONS], conv_weight[block_level, kernel_tap], preferred_element_type=jnp.float32)
        grad_in = grad.astype(jnp.bfloat16)
        grad_mid = jnp.dot(grad_in, expand_weight[block_level].T, preferred_element_type=jnp.float32)
        grad_pre = (grad_mid * gelu_slope(pre)).astype(jnp.bfloat16)
        grad_pad = jnp.pad(grad_pre, ((dilation_factor, dilation_factor), (0, 0)))
        grad_act = jnp.zeros((POSITIONS, C), jnp.float32)
        for kernel_tap in range(KW):
            start = (KW - 1 - kernel_tap) * dilation_factor
            grad_act = grad_act + jnp.dot(grad_pad[start:start + POSITIONS], conv_weight[block_level, kernel_tap].T, preferred_element_type=jnp.float32)
        grad = grad + grad_act * gelu_slope(saved)
    return grad.astype(jnp.bfloat16)
```

```python
import functools

import jax
import jax.numpy as jnp
from jax import lax
from jax.experimental import pallas as pl
from jax.experimental.pallas import tpu as pltpu
from jax.sharding import PartitionSpec as P

BASE_DILATION = 4
RANK = 8
SLOTS = 64
COLS = 256
GROUP_AXES = ("pos", "head")
HALO_IN = {2: 32, 1: 16, 0: 8, -1: 0}
HALO_SAVED = {2: 48, 1: 32, 0: 16}
F32 = jnp.float32
BF16 = jnp.bfloat16
NT = (((1,), (1,)), ((), ()))


def cost(flops, bytes_accessed, transcendentals=0):
    return pl.CostEstimate(
        flops=int(flops), bytes_accessed=int(bytes_accessed), transcendentals=int(transcendentals)
    )


def params():
    return pltpu.CompilerParams(vmem_limit_bytes=40 * 2**20)


def gelu_parts(value):
    half = 0.5 * (1.0 + lax.erf(value * 0.7071067811865476))
    return value * half, half + value * jnp.exp(-0.5 * value * value) * 0.3989422804014327


def vectors_kernel(place, weight, share, batch, left, right, out):
    projected = jnp.dot(weight[...], left[...], preferred_element_type=F32)
    column = lax.broadcasted_iota(jnp.int32, projected.shape, 1) // RANK
    kept = jnp.where(column == batch[...], projected, 0.0)
    removed = lax.dot_general(
        kept, right[...].astype(F32), NT, precision=lax.Precision.HIGHEST,
        preferred_element_type=F32,
    )
    out[...] = (share[...].astype(F32) - removed).astype(BF16)


def head_vectors(place, head_weight, batch_of, erase_left, erase_right, share):
    count, channels = head_weight.shape
    whole = lambda i, place: (0, 0)
    return pl.pallas_call(
        vectors_kernel,
        grid_spec=pltpu.PrefetchScalarGridSpec(
            num_scalar_prefetch=1,
            grid=(1,),
            in_specs=[
                pl.BlockSpec((count, channels), whole),
                pl.BlockSpec((count, share), lambda i, place: (0, place[0])),
                pl.BlockSpec((count, 1), whole),
                pl.BlockSpec(erase_left.shape, whole),
                pl.BlockSpec((share, erase_right.shape[1]), lambda i, place: (place[0], 0)),
            ],
            out_specs=pl.BlockSpec((count, share), whole),
        ),
        out_shape=jax.ShapeDtypeStruct((count, share), BF16),
        cost_estimate=cost(1e9, 1e6),
        compiler_params=params(),
        name="head_vectors",
    )(place, head_weight, head_weight, batch_of[:, None], erase_left, erase_right)


def bucket_kernel(rows, cover, bins, grads, out):
    chunks, lanes = bins.shape
    members = out.shape[0]
    before = (
        lax.broadcasted_iota(jnp.int32, (lanes, lanes), 0)
        < lax.broadcasted_iota(jnp.int32, (lanes, lanes), 1)
    ).astype(F32).astype(BF16)
    index = lax.broadcasted_iota(jnp.int32, (members, lanes), 0)
    lane = lax.broadcasted_iota(jnp.int32, (1, lanes), 1)
    base = jnp.zeros((members, 1), F32)
    total = jnp.zeros((members, 4 * SLOTS), F32)
    for chunk in range(chunks):
        place = bins[chunk : chunk + 1, :]
        target = place // rows
        offset = place - target * rows
        mine = jnp.where(target == index, 1.0, 0.0)
        mine_low = mine.astype(BF16)
        earlier = jnp.dot(mine_low, before, preferred_element_type=F32) + base
        rank = jnp.sum(mine * earlier, axis=0, keepdims=True).astype(jnp.int32)
        base = base + jnp.sum(mine, axis=1, keepdims=True)
        expert = chunk * (lanes // cover) + lane // cover
        high = offset // 256
        low = (offset - high * 256).astype(F32)
        code = (expert + high * SLOTS).astype(F32)
        value = grads[chunk : chunk + 1, :].astype(F32)
        hit = rank == index
        spread = jnp.concatenate(
            [jnp.where(hit, v, 0.0) for v in (low, code, value)] + [jnp.zeros_like(mine)], axis=0
        ).astype(BF16)
        total = total + lax.dot_general(mine_low, spread, NT, preferred_element_type=F32)
    out[...] = total.astype(BF16)


def bucket(cover_bins, bin_gradient, members, rows):
    cover = cover_bins.shape[1]
    entries = cover_bins.size
    return pl.pallas_call(
        functools.partial(bucket_kernel, rows, cover),
        out_shape=jax.ShapeDtypeStruct((members, 4 * SLOTS), BF16),
        cost_estimate=cost(1e8, 1e5),
        compiler_params=params(),
        name="bucket_entries",
    )(cover_bins.reshape(entries // 128, 128), bin_gradient.reshape(entries // 128, 128))


def spread_kernel(groups, fields, out):
    group = pl.program_id(0)
    low = fields[pl.ds(group, 1), :]
    code = fields[pl.ds(groups + group, 1), :]
    value = fields[pl.ds(2 * groups + group, 1), :]
    high = code >= SLOTS
    offset = (low + jnp.where(high, 256.0, 0.0)).astype(jnp.int32)
    slot = lax.broadcasted_iota(jnp.int32, code.shape, 1)
    column = (code - jnp.where(high, 1.0 * SLOTS, 0.0)).astype(jnp.int32) + slot // SLOTS * SLOTS
    rows = out.shape[0]
    width = out.shape[1]
    at_row = jnp.where(
        lax.broadcasted_iota(jnp.int32, (rows, width), 0) == offset, 1.0, 0.0
    ).astype(BF16)
    at_column = jnp.where(
        lax.broadcasted_iota(jnp.int32, (width, width), 0) == column, value, 0.0
    ).astype(BF16)
    out[...] = lax.dot_general(at_row, at_column, NT, preferred_element_type=F32).astype(BF16)


def spread_entries(fields, rows):
    groups = fields.shape[0] // 4
    width = fields.shape[1]
    return pl.pallas_call(
        functools.partial(spread_kernel, groups),
        grid=(groups,),
        in_specs=[pl.BlockSpec(fields.shape, lambda i: (0, 0))],
        out_specs=pl.BlockSpec((rows, width), lambda i: (0, i)),
        out_shape=jax.ShapeDtypeStruct((rows, groups * width), BF16),
        cost_estimate=cost(6e9, 8e6),
        compiler_params=params(),
        name="spread_entries",
    )(fields)


def pre_kernel(level, rows, saved, low, high, weight, own, send, slope, act):
    dilation = BASE_DILATION * 2**level
    halo = HALO_SAVED[level]
    inner = HALO_IN[level - 1]

    @pl.when(pl.program_id(0) == 0)
    def _():
        act[:halo, :] = gelu_parts(low[...].astype(F32))[0]
        act[halo + rows :, :] = gelu_parts(high[...].astype(F32))[0]
        value, _ = gelu_parts(saved[...].astype(F32))
        act[halo : halo + rows, :] = value

    total = None
    first = halo - HALO_IN[level] - dilation
    count = own.shape[0]
    for tap in range(weight.shape[0]):
        start = first + tap * dilation
        part = jnp.dot(
            act[start : start + count, :].astype(BF16), weight[tap], preferred_element_type=F32
        )
        total = part if total is None else total + part
    own[...] = total
    send[...] = total.astype(BF16)


def slope_kernel(mask, flags, own, other, out, *, halo, rows):
    value = own[...] + other[...].astype(F32)
    _, slope = gelu_parts(value)
    if mask:
        at = lax.broadcasted_iota(jnp.int32, value.shape, 0)
        outside = ((at < halo) & (flags[0] != 0)) | ((at >= halo + rows) & (flags[1] != 0))
        slope = jnp.where(outside, 0.0, slope)
    out[...] = slope


def pre_partial(level, saved, low, high, weights):
    rows, share = saved.shape
    count = rows + 2 * HALO_IN[level]
    halo = HALO_SAVED[level]
    taps, _, width = weights.shape
    fixed = lambda i: (0, 0)
    blocks = pl.BlockSpec((count, COLS), lambda i: (0, i))

    def body(saved, low, high, weight, own, send, act):
        pre_kernel(level, rows, saved, low, high, weight, own, send, None, act)

    return pl.pallas_call(
        body,
        grid=(width // COLS,),
        in_specs=[
            pl.BlockSpec((rows, share), fixed),
            pl.BlockSpec((halo, share), fixed),
            pl.BlockSpec((halo, share), fixed),
            pl.BlockSpec((taps, share, COLS), lambda i: (0, 0, i)),
        ],
        out_specs=[blocks, blocks],
        out_shape=[
            jax.ShapeDtypeStruct((count, width), F32),
            jax.ShapeDtypeStruct((count, width), BF16),
        ],
        scratch_shapes=[pltpu.VMEM((rows + 2 * halo, share), F32)],
        cost_estimate=cost(4e9, 8e6, 1e6),
        compiler_params=params(),
        name=f"pre_partial_{level}",
    )(saved, low, high, weights)


def pre_slope(level, flags, own, other, rows):
    count, width = own.shape
    blocks = pl.BlockSpec((count, COLS), lambda i, flags: (0, i))

    def body(flags, own, other, out):
        slope_kernel(True, flags, own, other, out, halo=HALO_IN[level], rows=rows)

    return pl.pallas_call(
        body,
        grid_spec=pltpu.PrefetchScalarGridSpec(
            num_scalar_prefetch=1, grid=(width // COLS,), in_specs=[blocks, blocks], out_specs=blocks
        ),
        out_shape=jax.ShapeDtypeStruct((count, width), F32),
        cost_estimate=cost(4e9, 5e6, 1e6),
        compiler_params=params(),
        name=f"pre_slope_{level}",
    )(flags, own, other)


def saved_slope(level, saved, low, high):
    rows, share = saved.shape
    halo = HALO_SAVED[level]
    inner = HALO_IN[level - 1]

    def body(saved, low, high, out):
        slope = lambda value: gelu_parts(value.astype(F32))[1]
        if inner:
            out[:inner, :] = slope(low[...])[halo - inner :]
            out[inner + rows :, :] = slope(high[...])[:inner]
        out[inner : inner + rows, :] = slope(saved[...])

    fixed = lambda i: (0, i)
    return pl.pallas_call(
        body,
        grid=(share // COLS,),
        in_specs=[
            pl.BlockSpec((rows, COLS), fixed),
            pl.BlockSpec((halo, COLS), fixed),
            pl.BlockSpec((halo, COLS), fixed),
        ],
        out_specs=pl.BlockSpec((rows + 2 * inner, COLS), fixed),
        out_shape=jax.ShapeDtypeStruct((rows + 2 * inner, share), F32),
        cost_estimate=cost(4e9, 3e6, 1e6),
        compiler_params=params(),
        name=f"saved_slope_{level}",
    )(saved, low, high)


def to_middle(step, grad, expand, own, send, middle):
    part = lax.dot_general(grad.astype(BF16), expand[...], NT, preferred_element_type=F32)

    @pl.when(step == 0)
    def _():
        middle[...] = part

    @pl.when(step > 0)
    def _():
        middle[...] += part

    @pl.when(step == pl.num_programs(0) - 1)
    def _():
        own[...] = middle[...]
        send[...] = middle[...].astype(BF16)


def top_kernel(spread, vectors, expand, grad, own, send, middle):
    top = jnp.dot(spread[...], vectors[...], preferred_element_type=F32)
    grad[...] = top
    to_middle(pl.program_id(0), top, expand, own, send, middle)


def top_gradient(spread, vectors, expand):
    count, depth = spread.shape
    share = vectors.shape[1]
    width = expand.shape[0]
    fixed = lambda i: (0, 0)
    blocks = lambda i: (0, i)
    return pl.pallas_call(
        top_kernel,
        grid=(share // COLS,),
        in_specs=[
            pl.BlockSpec((count, depth), fixed),
            pl.BlockSpec((depth, COLS), blocks),
            pl.BlockSpec((width, COLS), blocks),
        ],
        out_specs=[
            pl.BlockSpec((count, COLS), blocks),
            pl.BlockSpec((count, width), fixed),
            pl.BlockSpec((count, width), fixed),
        ],
        out_shape=[
            jax.ShapeDtypeStruct((count, share), F32),
            jax.ShapeDtypeStruct((count, width), F32),
            jax.ShapeDtypeStruct((count, width), BF16),
        ],
        scratch_shapes=[pltpu.VMEM((count, width), F32)],
        cost_estimate=cost(5e9, 14e6),
        compiler_params=params(),
        name="top_gradient",
    )(spread, vectors, expand)


def block_kernel(level, refs):
    last = level == 0
    if last:
        own, other, slope, weight, grad, outer, out, pre, shifted = refs
    else:
        own, other, slope, weight, grad, outer, expand, out, own_next, send, pre, shifted, middle = refs
    dilation = BASE_DILATION * 2**level
    count = out.shape[0]
    trim = HALO_IN[level] - HALO_IN[level - 1]
    taps = weight.shape[0]

    @pl.when(pl.program_id(0) == 0)
    def _():
        pre[...] = (own[...] + other[...].astype(F32)) * slope[...]
        for tap in range(taps):
            start = trim - (tap - 1) * dilation
            shifted[tap] = pre[start : start + count, :].astype(BF16)

    total = None
    for tap in range(taps):
        part = lax.dot_general(shifted[tap], weight[tap], NT, preferred_element_type=F32)
        total = part if total is None else total + part
    new = grad[trim : trim + count, :] + total * outer[...]
    if last:
        out[...] = new.astype(BF16)
    else:
        out[...] = new
        to_middle(pl.program_id(0), new, expand, own_next, send, middle)


def block_step(level, own, other, slope, weight, grad, outer, expand):
    count_in, width = own.shape
    count = outer.shape[0]
    taps, share, _ = weight.shape
    fixed = lambda i: (0, 0)
    blocks = lambda i: (0, i)
    last = level == 0
    in_specs = [
        pl.BlockSpec((count_in, width), fixed),
        pl.BlockSpec((count_in, width), fixed),
        pl.BlockSpec((count_in, width), fixed),
        pl.BlockSpec((taps, COLS, width), lambda i: (0, i, 0)),
        pl.BlockSpec((count_in, COLS), blocks),
        pl.BlockSpec((count, COLS), blocks),
    ]
    args = [own, other, slope, weight, grad, outer]
    out_specs = [pl.BlockSpec((count, COLS), blocks)]
    out_shape = [jax.ShapeDtypeStruct((count, share), BF16 if last else F32)]
    scratch = [pltpu.VMEM((count_in, width), F32), pltpu.VMEM((taps, count, width), BF16)]
    if not last:
        in_specs.append(pl.BlockSpec((width, COLS), blocks))
        args.append(expand)
        out_specs += [pl.BlockSpec((count, width), fixed)] * 2
        out_shape += [
            jax.ShapeDtypeStruct((count, width), F32),
            jax.ShapeDtypeStruct((count, width), BF16),
        ]
        scratch.append(pltpu.VMEM((count, width), F32))
    return pl.pallas_call(
        lambda *refs: block_kernel(level, refs),
        grid=(share // COLS,),
        in_specs=in_specs,
        out_specs=out_specs,
        out_shape=out_shape,
        scratch_shapes=scratch,
        cost_estimate=cost(5e9, 14e6),
        compiler_params=params(),
        name=f"block_step_{level}",
    )(*args)


def gather_vectors(vectors):
    count = vectors.shape[0]
    place = lax.axis_index("head")
    along, turn = place // 4, place % 4
    same = lambda steps: [(a * 4 + z, a * 4 + (z - steps) % 4) for a in range(2) for z in range(4)]
    parts = [vectors] + [lax.ppermute(vectors, "head", same(k)) for k in (1, 2, 3)]
    twice = jnp.concatenate(parts + parts, axis=0)
    ring = lax.dynamic_slice_in_dim(twice, (4 - turn) % 4 * count, 4 * count, 0)
    other = lax.ppermute(ring, "head", [(k, (k + 4) % 8) for k in range(8)])
    both = jnp.where(
        along == 0,
        jnp.concatenate([ring, other], axis=0),
        jnp.concatenate([other, ring], axis=0),
    )
    return lax.all_gather(both, "pos", tiled=True)


def per_device(
    inputs_saved,
    conv_weight,
    expand_weight,
    head_weight,
    batch_of,
    erase_left,
    erase_right,
    bin_gradient,
    cover_bins,
):
    members = lax.axis_size(GROUP_AXES)
    layers, rows, share = inputs_saved.shape
    member = lax.axis_index(GROUP_AXES)
    chan_place = lax.axis_index("chan")
    up = [(k, k + 1) for k in range(members - 1)]
    down = [(k + 1, k) for k in range(members - 1)]
    swap = [(0, 1), (1, 0)]
    levels = list(reversed(range(layers)))

    vectors = head_vectors(
        chan_place[None].astype(jnp.int32), head_weight, batch_of, erase_left, erase_right, share
    )
    gathered = gather_vectors(vectors)

    payload = bucket(cover_bins, bin_gradient, members, rows)
    arrived = lax.all_to_all(payload, GROUP_AXES, split_axis=0, concat_axis=0, tiled=True)
    fields = (
        arrived.reshape(members, 4, SLOTS).transpose(1, 0, 2).reshape(-1, COLS).astype(F32)
    )
    spread = spread_entries(fields, rows)
    reach = HALO_IN[layers - 1]
    spread_low = lax.ppermute(spread[rows - reach :], GROUP_AXES, up)
    spread_high = lax.ppermute(spread[:reach], GROUP_AXES, down)
    spread = jnp.concatenate([spread_low, spread, spread_high], axis=0)

    edge_low = jnp.concatenate([inputs_saved[n, rows - HALO_SAVED[n] :] for n in levels], axis=0)
    edge_high = jnp.concatenate([inputs_saved[n, : HALO_SAVED[n]] for n in levels], axis=0)
    edge_low = lax.ppermute(edge_low, GROUP_AXES, up)
    edge_high = lax.ppermute(edge_high, GROUP_AXES, down)
    flags = jnp.stack([member == 0, member == members - 1]).astype(jnp.int32)
    start = 0
    slopes, outers = {}, {}
    for n in levels:
        size = HALO_SAVED[n]
        low, high = edge_low[start : start + size], edge_high[start : start + size]
        start += size
        own, send = pre_partial(n, inputs_saved[n], low, high, conv_weight[n])
        other = lax.ppermute(send, "chan", swap)
        slopes[n] = pre_slope(n, flags, own, other, rows)
        outers[n] = saved_slope(n, inputs_saved[n], low, high)

    grad, own, send = top_gradient(spread, gathered, expand_weight[layers - 1])
    for n in levels:
        other = lax.ppermute(send, "chan", swap)
        outs = block_step(
            n, own, other, slopes[n], conv_weight[n], grad, outers[n],
            expand_weight[n - 1] if n else None,
        )
        if n:
            grad, own, send = outs
    return outs[0]


def solution(mesh):
    return jax.shard_map(
        per_device,
        mesh=mesh,
        in_specs=(
            P(None, ("pos", "head"), "chan"),
            P(None, None, "chan", None),
            P(None, None, "chan"),
            P(("pos", "head"), None),
            P(("pos", "head")),
            P(),
            P(),
            P(("pos", "head"), None),
            P(("pos", "head"), None),
        ),
        out_specs=P(("pos", "head"), "chan"),
        check_vma=False,
    )
```

```python
import functools

import jax
import jax.numpy as jnp
from jax import lax
from jax.experimental import pallas as pl
from jax.experimental.pallas import tpu as pltpu
from jax.sharding import PartitionSpec as P

BASE_DILATION = 4
RANK = 8
SLOTS = 64
COLS = 256
GROUP_AXES = ("pos", "head")
HALO_IN = {2: 32, 1: 16, 0: 8, -1: 0}
HALO_SAVED = {2: 48, 1: 32, 0: 16}
EDGE_START = {1: 0, 0: 32, 2: 48}
EDGE_ORDER = (1, 0, 2)
F32 = jnp.float32
BF16 = jnp.bfloat16
NT = (((1,), (1,)), ((), ()))


def cost(flops, bytes_accessed, transcendentals=0):
    return pl.CostEstimate(
        flops=int(flops), bytes_accessed=int(bytes_accessed), transcendentals=int(transcendentals)
    )


def params():
    return pltpu.CompilerParams(vmem_limit_bytes=40 * 2**20)


def gelu_parts(value):
    half = 0.5 * (1.0 + lax.erf(value * 0.7071067811865476))
    return value * half, half + value * jnp.exp(-0.5 * value * value) * 0.3989422804014327


def vectors_kernel(place, weight, share, batch, left, right, out):
    projected = jnp.dot(weight[...], left[...], preferred_element_type=F32)
    column = lax.broadcasted_iota(jnp.int32, projected.shape, 1) // RANK
    kept = jnp.where(column == batch[...], projected, 0.0)
    removed = lax.dot_general(
        kept, right[...].astype(F32), NT, precision=lax.Precision.HIGHEST,
        preferred_element_type=F32,
    )
    out[...] = (share[...].astype(F32) - removed).astype(BF16)


def head_vectors(place, head_weight, batch_of, erase_left, erase_right, share):
    count, channels = head_weight.shape
    whole = lambda i, place: (0, 0)
    return pl.pallas_call(
        vectors_kernel,
        grid_spec=pltpu.PrefetchScalarGridSpec(
            num_scalar_prefetch=1,
            grid=(1,),
            in_specs=[
                pl.BlockSpec((count, channels), whole),
                pl.BlockSpec((count, share), lambda i, place: (0, place[0])),
                pl.BlockSpec((count, 1), whole),
                pl.BlockSpec(erase_left.shape, whole),
                pl.BlockSpec((share, erase_right.shape[1]), lambda i, place: (place[0], 0)),
            ],
            out_specs=pl.BlockSpec((count, share), whole),
        ),
        out_shape=jax.ShapeDtypeStruct((count, share), BF16),
        cost_estimate=cost(1e9, 1e6),
        compiler_params=params(),
        name="head_vectors",
    )(place, head_weight, head_weight, batch_of[:, None], erase_left, erase_right)


def bucket_kernel(rows, cover, place_of, bins, grads, out):
    chunks, lanes = bins.shape
    members = out.shape[0]
    before = (
        lax.broadcasted_iota(jnp.int32, (lanes, lanes), 0)
        < lax.broadcasted_iota(jnp.int32, (lanes, lanes), 1)
    ).astype(F32).astype(BF16)
    index = lax.broadcasted_iota(jnp.int32, (members, lanes), 0)
    slot = lax.broadcasted_iota(jnp.int32, (COLS, lanes), 0) - place_of[0] * SLOTS
    lane = lax.broadcasted_iota(jnp.int32, (1, lanes), 1)
    base = jnp.zeros((members, 1), F32)
    total = jnp.zeros(out.shape, F32)
    for chunk in range(chunks):
        place = bins[chunk : chunk + 1, :]
        target = place // rows
        offset = place - target * rows
        mine = jnp.where(target == index, 1.0, 0.0)
        mine_low = mine.astype(BF16)
        earlier = jnp.dot(mine_low, before, preferred_element_type=F32) + base
        rank = jnp.sum(mine * earlier, axis=0, keepdims=True).astype(jnp.int32)
        base = base + jnp.sum(mine, axis=1, keepdims=True)
        expert = chunk * (lanes // cover) + lane // cover
        high = offset // 256
        low = (offset - high * 256).astype(F32)
        code = (expert + high * SLOTS).astype(F32)
        value = grads[chunk : chunk + 1, :].astype(F32)
        hit = rank == slot
        spread = jnp.concatenate(
            [jnp.where(hit, v, 0.0) for v in (low, code, value)], axis=0
        ).astype(BF16)
        total = total + lax.dot_general(mine_low, spread, NT, preferred_element_type=F32)
    out[...] = total.astype(BF16)


def bucket(place, cover_bins, bin_gradient, members, rows):
    cover = cover_bins.shape[1]
    entries = cover_bins.size
    return pl.pallas_call(
        functools.partial(bucket_kernel, rows, cover),
        in_specs=[
            pl.BlockSpec(memory_space=pltpu.SMEM),
            pl.BlockSpec(memory_space=pltpu.VMEM),
            pl.BlockSpec(memory_space=pltpu.VMEM),
        ],
        out_shape=jax.ShapeDtypeStruct((members, 3 * COLS), BF16),
        cost_estimate=cost(1e8, 1e5),
        compiler_params=params(),
        name="bucket_entries",
    )(place, cover_bins.reshape(entries // 128, 128), bin_gradient.reshape(entries // 128, 128))


def spread_kernel(arrived, out, fields):
    group = pl.program_id(0)
    together = COLS // SLOTS

    @pl.when(group == 0)
    def _():
        members = arrived.shape[0]
        shape = (members // together, members)
        same = (
            lax.broadcasted_iota(jnp.int32, shape, 1) // together
            == lax.broadcasted_iota(jnp.int32, shape, 0)
        )
        fields[...] = jnp.dot(
            jnp.where(same, 1.0, 0.0).astype(BF16), arrived[...], preferred_element_type=F32
        )

    row = fields[pl.ds(group, 1), :]
    low = row[:, :COLS]
    code = row[:, COLS : 2 * COLS]
    value = row[:, 2 * COLS :]
    high = code >= SLOTS
    offset = (low + jnp.where(high, 256.0, 0.0)).astype(jnp.int32)
    slot = lax.broadcasted_iota(jnp.int32, code.shape, 1)
    column = (code - jnp.where(high, 1.0 * SLOTS, 0.0)).astype(jnp.int32) + slot // SLOTS * SLOTS
    rows = out.shape[0]
    width = out.shape[1]
    at_row = jnp.where(
        lax.broadcasted_iota(jnp.int32, (rows, width), 0) == offset, 1.0, 0.0
    ).astype(BF16)
    at_column = jnp.where(
        lax.broadcasted_iota(jnp.int32, (width, width), 0) == column, value, 0.0
    ).astype(BF16)
    out[...] = lax.dot_general(at_row, at_column, NT, preferred_element_type=F32).astype(BF16)


def spread_entries(arrived, rows):
    groups = arrived.shape[0] * SLOTS // COLS
    width = COLS
    return pl.pallas_call(
        spread_kernel,
        grid=(groups,),
        in_specs=[pl.BlockSpec(arrived.shape, lambda i: (0, 0))],
        scratch_shapes=[pltpu.VMEM((groups, arrived.shape[1]), F32)],
        out_specs=pl.BlockSpec((rows, width), lambda i: (0, i)),
        out_shape=jax.ShapeDtypeStruct((rows, groups * width), BF16),
        cost_estimate=cost(6e9, 8e6),
        compiler_params=params(),
        name="spread_entries",
    )(arrived)


def pre_kernel(level, rows, saved, low, high, weight, own, send, slope, act):
    dilation = BASE_DILATION * 2**level
    halo = HALO_SAVED[level]
    inner = HALO_IN[level - 1]

    @pl.when(pl.program_id(0) == 0)
    def _():
        act[:halo, :] = gelu_parts(low[...].astype(F32))[0]
        act[halo + rows :, :] = gelu_parts(high[...].astype(F32))[0]
        value, _ = gelu_parts(saved[...].astype(F32))
        act[halo : halo + rows, :] = value

    total = None
    first = halo - HALO_IN[level] - dilation
    count = own.shape[0]
    for tap in range(weight.shape[0]):
        start = first + tap * dilation
        part = jnp.dot(
            act[start : start + count, :].astype(BF16), weight[tap], preferred_element_type=F32
        )
        total = part if total is None else total + part
    own[...] = total
    send[...] = total.astype(BF16)


def slope_kernel(mask, flags, own, other, out, *, halo, rows):
    value = own[...] + other[...].astype(F32)
    _, slope = gelu_parts(value)
    if mask:
        at = lax.broadcasted_iota(jnp.int32, value.shape, 0)
        outside = ((at < halo) & (flags[0] != 0)) | ((at >= halo + rows) & (flags[1] != 0))
        slope = jnp.where(outside, 0.0, slope)
    out[...] = slope


def saved_specs(level, saved, columns=None):
    rows, share = saved.shape[1:]
    halo = HALO_SAVED[level]
    at = EDGE_START[level] // halo
    width = columns or share
    col = (lambda i: i) if columns else (lambda i: 0)
    return [
        pl.BlockSpec((None, rows, width), lambda i: (level, 0, col(i))),
        pl.BlockSpec((halo, width), lambda i: (at, col(i))),
        pl.BlockSpec((halo, width), lambda i: (at, col(i))),
    ]


def cut_edges(saved):
    levels, rows, share = saved.shape
    count = sum(HALO_SAVED.values())

    def body(*refs):
        first, last = refs[-2:]
        for k, level in enumerate(EDGE_ORDER):
            start, size = EDGE_START[level], HALO_SAVED[level]
            first[start : start + size, :] = refs[2 * k][...]
            last[start : start + size, :] = refs[2 * k + 1][...]

    specs = []
    for level in EDGE_ORDER:
        size = HALO_SAVED[level]
        for start in (0, rows - size):
            specs.append(
                pl.BlockSpec(
                    (None, pl.Element(size), pl.Element(share)),
                    lambda i, level=level, start=start: (level, start, 0),
                )
            )
    whole = pl.BlockSpec((count, share), lambda i: (0, 0))
    return pl.pallas_call(
        body,
        grid=(1,),
        in_specs=specs,
        out_specs=[whole, whole],
        out_shape=[jax.ShapeDtypeStruct((count, share), BF16)] * 2,
        cost_estimate=cost(1e6, 6e5),
        compiler_params=params(),
        name="cut_edges",
    )(*[saved] * len(specs))


def pre_partial(level, saved, low, high, weights):
    rows, share = saved.shape[1:]
    count = rows + 2 * HALO_IN[level]
    halo = HALO_SAVED[level]
    _, taps, _, width = weights.shape
    blocks = pl.BlockSpec((count, COLS), lambda i: (0, i))

    def body(saved, low, high, weight, own, send, act):
        pre_kernel(level, rows, saved, low, high, weight, own, send, None, act)

    return pl.pallas_call(
        body,
        grid=(width // COLS,),
        in_specs=saved_specs(level, saved)
        + [pl.BlockSpec((None, taps, share, COLS), lambda i: (level, 0, 0, i))],
        out_specs=[blocks, blocks],
        out_shape=[
            jax.ShapeDtypeStruct((count, width), F32),
            jax.ShapeDtypeStruct((count, width), BF16),
        ],
        scratch_shapes=[pltpu.VMEM((rows + 2 * halo, share), F32)],
        cost_estimate=cost(4e9, 8e6, 1e6),
        compiler_params=params(),
        name=f"pre_partial_{level}",
    )(saved, low, high, weights)


def pre_slope(level, flags, own, other, rows):
    count, width = own.shape
    blocks = pl.BlockSpec((count, COLS), lambda i, flags: (0, i))

    def body(flags, own, other, out):
        slope_kernel(True, flags, own, other, out, halo=HALO_IN[level], rows=rows)

    return pl.pallas_call(
        body,
        grid_spec=pltpu.PrefetchScalarGridSpec(
            num_scalar_prefetch=1, grid=(width // COLS,), in_specs=[blocks, blocks], out_specs=blocks
        ),
        out_shape=jax.ShapeDtypeStruct((count, width), F32),
        cost_estimate=cost(4e9, 5e6, 1e6),
        compiler_params=params(),
        name=f"pre_slope_{level}",
    )(flags, own, other)


def saved_slope(level, saved, low, high):
    rows, share = saved.shape[1:]
    halo = HALO_SAVED[level]
    inner = HALO_IN[level - 1]

    def body(saved, low, high, out):
        slope = lambda value: gelu_parts(value.astype(F32))[1]
        if inner:
            out[:inner, :] = slope(low[...])[halo - inner :]
            out[inner + rows :, :] = slope(high[...])[:inner]
        out[inner : inner + rows, :] = slope(saved[...])

    return pl.pallas_call(
        body,
        grid=(share // COLS,),
        in_specs=saved_specs(level, saved, COLS),
        out_specs=pl.BlockSpec((rows + 2 * inner, COLS), lambda i: (0, i)),
        out_shape=jax.ShapeDtypeStruct((rows + 2 * inner, share), F32),
        cost_estimate=cost(4e9, 3e6, 1e6),
        compiler_params=params(),
        name=f"saved_slope_{level}",
    )(saved, low, high)


def to_middle(step, grad, expand, own, send, middle):
    part = lax.dot_general(grad.astype(BF16), expand[...], NT, preferred_element_type=F32)

    @pl.when(step == 0)
    def _():
        middle[...] = part

    @pl.when(step > 0)
    def _():
        middle[...] += part

    @pl.when(step == pl.num_programs(0) - 1)
    def _():
        own[...] = middle[...]
        send[...] = middle[...].astype(BF16)


def top_kernel(spread, vectors, expand, grad, own, send, middle):
    top = jnp.dot(spread[...], vectors[...], preferred_element_type=F32)
    grad[...] = top
    to_middle(pl.program_id(0), top, expand, own, send, middle)


def top_gradient(spread, vectors, expand):
    count, depth = spread.shape
    share = vectors.shape[1]
    levels, width, _ = expand.shape
    fixed = lambda i: (0, 0)
    blocks = lambda i: (0, i)
    return pl.pallas_call(
        top_kernel,
        grid=(share // COLS,),
        in_specs=[
            pl.BlockSpec((count, depth), fixed),
            pl.BlockSpec((depth, COLS), blocks),
            pl.BlockSpec((None, width, COLS), lambda i: (levels - 1, 0, i)),
        ],
        out_specs=[
            pl.BlockSpec((count, COLS), blocks),
            pl.BlockSpec((count, width), fixed),
            pl.BlockSpec((count, width), fixed),
        ],
        out_shape=[
            jax.ShapeDtypeStruct((count, share), F32),
            jax.ShapeDtypeStruct((count, width), F32),
            jax.ShapeDtypeStruct((count, width), BF16),
        ],
        scratch_shapes=[pltpu.VMEM((count, width), F32)],
        cost_estimate=cost(5e9, 14e6),
        compiler_params=params(),
        name="top_gradient",
    )(spread, vectors, expand)


def block_kernel(level, refs):
    last = level == 0
    if last:
        own, other, slope, weight, grad, outer, out, pre, shifted = refs
    else:
        own, other, slope, weight, grad, outer, expand, out, own_next, send, pre, shifted, middle = refs
    dilation = BASE_DILATION * 2**level
    count = out.shape[0]
    trim = HALO_IN[level] - HALO_IN[level - 1]
    taps = weight.shape[0]

    @pl.when(pl.program_id(0) == 0)
    def _():
        pre[...] = (own[...] + other[...].astype(F32)) * slope[...]
        for tap in range(taps):
            start = trim - (tap - 1) * dilation
            shifted[tap] = pre[start : start + count, :].astype(BF16)

    total = None
    for tap in range(taps):
        part = lax.dot_general(shifted[tap], weight[tap], NT, preferred_element_type=F32)
        total = part if total is None else total + part
    new = grad[trim : trim + count, :] + total * outer[...]
    if last:
        out[...] = new.astype(BF16)
    else:
        out[...] = new
        to_middle(pl.program_id(0), new, expand, own_next, send, middle)


def block_step(level, own, other, slope, weight, grad, outer, expand):
    count_in, width = own.shape
    count = outer.shape[0]
    _, taps, share, _ = weight.shape
    fixed = lambda i: (0, 0)
    blocks = lambda i: (0, i)
    last = level == 0
    in_specs = [
        pl.BlockSpec((count_in, width), fixed),
        pl.BlockSpec((count_in, width), fixed),
        pl.BlockSpec((count_in, width), fixed),
        pl.BlockSpec((None, taps, COLS, width), lambda i: (level, 0, i, 0)),
        pl.BlockSpec((count_in, COLS), blocks),
        pl.BlockSpec((count, COLS), blocks),
    ]
    args = [own, other, slope, weight, grad, outer]
    out_specs = [pl.BlockSpec((count, COLS), blocks)]
    out_shape = [jax.ShapeDtypeStruct((count, share), BF16 if last else F32)]
    scratch = [pltpu.VMEM((count_in, width), F32), pltpu.VMEM((taps, count, width), BF16)]
    if not last:
        in_specs.append(pl.BlockSpec((None, width, COLS), lambda i: (level - 1, 0, i)))
        args.append(expand)
        out_specs += [pl.BlockSpec((count, width), fixed)] * 2
        out_shape += [
            jax.ShapeDtypeStruct((count, width), F32),
            jax.ShapeDtypeStruct((count, width), BF16),
        ]
        scratch.append(pltpu.VMEM((count, width), F32))
    return pl.pallas_call(
        lambda *refs: block_kernel(level, refs),
        grid=(share // COLS,),
        in_specs=in_specs,
        out_specs=out_specs,
        out_shape=out_shape,
        scratch_shapes=scratch,
        cost_estimate=cost(5e9, 14e6),
        compiler_params=params(),
        name=f"block_step_{level}",
    )(*args)


def after(value, *earlier):
    return lax.optimization_barrier((value, *earlier))[0]


def gather_vectors(vectors, meanwhile, later):
    count = vectors.shape[0]
    place = lax.axis_index("head")
    along, turn = place // 4, place % 4
    same = lambda steps: [(a * 4 + z, a * 4 + (z - steps) % 4) for a in range(2) for z in range(4)]
    parts = [lax.ppermute(vectors, "head", same(k)) for k in (1, 2, 3)]
    parts = [after(vectors, *meanwhile)] + parts
    twice = jnp.concatenate(parts + parts, axis=0)
    ring = lax.dynamic_slice_in_dim(twice, (4 - turn) % 4 * count, 4 * count, 0)
    other = lax.ppermute(ring, "head", [(k, (k + 4) % 8) for k in range(8)])
    ring = after(ring, *later)
    both = jnp.where(
        along == 0,
        jnp.concatenate([ring, other], axis=0),
        jnp.concatenate([other, ring], axis=0),
    )
    return lax.all_gather(both, "pos", tiled=True)


def per_device(
    inputs_saved,
    conv_weight,
    expand_weight,
    head_weight,
    batch_of,
    erase_left,
    erase_right,
    bin_gradient,
    cover_bins,
):
    members = lax.axis_size(GROUP_AXES)
    layers, rows, share = inputs_saved.shape
    member = lax.axis_index(GROUP_AXES)
    chan_place = lax.axis_index("chan")
    up = [(k, k + 1) for k in range(members - 1)]
    down = [(k + 1, k) for k in range(members - 1)]
    swap = [(0, 1), (1, 0)]
    levels = list(reversed(range(layers)))

    vectors = head_vectors(
        chan_place[None].astype(jnp.int32), head_weight, batch_of, erase_left, erase_right, share
    )
    first, final = cut_edges(inputs_saved)
    low = lax.ppermute(final, GROUP_AXES, up)
    high = lax.ppermute(first, GROUP_AXES, down)
    flags = jnp.stack([member == 0, member == members - 1]).astype(jnp.int32)
    sends, owns, others = {}, {}, {}
    for n in levels:
        owns[n], sends[n] = pre_partial(n, inputs_saved, low, high, conv_weight)
        others[n] = lax.ppermute(sends[n], "chan", swap)

    payload = bucket(
        (member % (COLS // SLOTS))[None].astype(jnp.int32), cover_bins, bin_gradient, members, rows
    )
    arrived = lax.all_to_all(payload, GROUP_AXES, split_axis=0, concat_axis=0, tiled=True)
    gathered = gather_vectors(vectors, (payload, low, high), (sends[levels[0]],))
    spread = spread_entries(after(arrived, *sends.values()), rows)
    reach = HALO_IN[layers - 1]
    spread_low = lax.ppermute(spread[rows - reach :], GROUP_AXES, up)
    spread_high = lax.ppermute(spread[:reach], GROUP_AXES, down)
    spread = jnp.concatenate([spread_low, spread, spread_high], axis=0)
    slopes = {n: pre_slope(n, flags, owns[n], others[n], rows) for n in levels}
    outers = {n: saved_slope(n, inputs_saved, low, high) for n in levels}
    spread = after(spread, others[levels[1]], slopes[levels[0]], *outers.values())

    grad, own, send = top_gradient(spread, gathered, expand_weight)
    for n in levels:
        other = lax.ppermute(send, "chan", swap)
        outs = block_step(
            n, own, other, slopes[n], conv_weight, grad, outers[n], expand_weight
        )
        if n:
            grad, own, send = outs
    return outs[0]


def solution(mesh):
    return jax.shard_map(
        per_device,
        mesh=mesh,
        in_specs=(
            P(None, ("pos", "head"), "chan"),
            P(None, None, "chan", None),
            P(None, None, "chan"),
            P(("pos", "head"), None),
            P(("pos", "head")),
            P(),
            P(),
            P(("pos", "head"), None),
            P(("pos", "head"), None),
        ),
        out_specs=P(("pos", "head"), "chan"),
        check_vma=False,
    )
```

```python
import functools

import jax
import jax.numpy as jnp
from jax import lax
from jax.experimental import pallas as pl
from jax.experimental.pallas import tpu as pltpu
from jax.sharding import PartitionSpec as P

BASE_DILATION = 4
RANK = 8
SLOTS = 64
COLS = 256
GROUP_AXES = ("pos", "head")
HALO_IN = {2: 32, 1: 16, 0: 8, -1: 0}
HALO_SAVED = {2: 48, 1: 32, 0: 16}
EDGE_START = {1: 0, 0: 32, 2: 48}
F32 = jnp.float32
BF16 = jnp.bfloat16
NT = (((1,), (1,)), ((), ()))


def cost(flops, bytes_accessed, transcendentals=0):
    return pl.CostEstimate(
        flops=int(flops / 5), bytes_accessed=int(bytes_accessed / 5), transcendentals=0
    )


def params():
    return pltpu.CompilerParams(vmem_limit_bytes=28 * 2**20)


VMEM = pl.BlockSpec(memory_space=pltpu.VMEM)
HBM = pl.BlockSpec(memory_space=pltpu.HBM)
SMEM = pl.BlockSpec(memory_space=pltpu.SMEM)
ROOT_HALF = 0.7071067811865476
DENSITY = 0.3989422804014327


def in_hbm(value):
    return pltpu.with_memory_space_constraint(value, pltpu.HBM)


def fetch(pairs, sems):
    copies = [pltpu.make_async_copy(a, b, sems.at[k]) for k, (a, b) in enumerate(pairs)]
    for copy in copies:
        copy.start()
    return copies


def column_blocks(share):
    return [slice(start, start + COLS) for start in range(0, share, COLS)]


def gelu_parts(value):
    half = 0.5 * (1.0 + lax.erf(value * ROOT_HALF))
    return value * half, half + value * jnp.exp(-0.5 * value * value) * DENSITY


def vectors_kernel(place, weight, share, batch, left, right, out):
    projected = lax.dot_general(left[...], weight[...], NT, preferred_element_type=F32)
    column = lax.broadcasted_iota(jnp.int32, projected.shape, 0) // RANK
    kept = jnp.where(column == batch[...], projected, 0.0)
    removed = lax.dot_general(
        kept, right[...].astype(F32), (((0,), (0,)), ((), ())),
        precision=lax.Precision.HIGHEST, preferred_element_type=F32,
    )
    out[...] = (share[...].astype(F32) - removed).astype(BF16)


def head_vectors(place, head_weight, batch_of, erase_left, erase_right, share):
    count, channels = head_weight.shape
    factors = erase_left.shape[1]
    whole = lambda i, place: (0, 0)
    mine = lambda i, place: (0, place[0])
    return pl.pallas_call(
        vectors_kernel,
        grid_spec=pltpu.PrefetchScalarGridSpec(
            num_scalar_prefetch=1,
            grid=(1,),
            in_specs=[
                pl.BlockSpec((count, channels), whole),
                pl.BlockSpec((count, share), mine),
                pl.BlockSpec((1, count), whole),
                pl.BlockSpec((factors, channels), whole),
                pl.BlockSpec((factors, share), mine),
            ],
            out_specs=pl.BlockSpec((count, share), whole),
        ),
        out_shape=jax.ShapeDtypeStruct((count, share), BF16),
        cost_estimate=cost(1e9, 1e6),
        compiler_params=params(),
        name="head_vectors",
    )(place, head_weight, head_weight, batch_of[None, :], erase_left.T, erase_right.T)


def bucket_kernel(rows, place_of, bins, grads, out):
    cover, experts = bins.shape
    together = 128 // experts
    lanes = together * experts
    chunks = cover // together
    members = out.shape[0]
    before = jnp.where(
        lax.broadcasted_iota(jnp.int32, (lanes, lanes), 0)
        < lax.broadcasted_iota(jnp.int32, (lanes, lanes), 1),
        1.0, 0.0,
    ).astype(BF16)
    index = lax.broadcasted_iota(jnp.int32, (members, lanes), 0)
    slot = lax.broadcasted_iota(jnp.int32, (COLS, lanes), 0) - place_of[0] * SLOTS
    expert = lax.broadcasted_iota(jnp.int32, (1, lanes), 1) % experts
    side = lambda ref, chunk: jnp.concatenate(
        [ref[chunk * together + k : chunk * together + k + 1, :] for k in range(together)], axis=1
    )
    base = jnp.zeros((members, 1), F32)
    total = jnp.zeros(out.shape, F32)
    grads = grads[...].astype(F32)
    for chunk in range(chunks):
        place = side(bins, chunk)
        target = place // rows
        offset = place - target * rows
        mine = jnp.where(target == index, 1.0, 0.0)
        mine_low = mine.astype(BF16)
        earlier = jnp.dot(mine_low, before, preferred_element_type=F32) + base
        rank = jnp.sum(mine * earlier, axis=0, keepdims=True).astype(jnp.int32)
        base = base + jnp.sum(mine, axis=1, keepdims=True)
        high = offset // 256
        low = (offset - high * 256).astype(F32)
        code = (expert + high * SLOTS).astype(F32)
        hit = rank == slot
        spread = jnp.concatenate(
            [jnp.where(hit, v, 0.0) for v in (low, code, side(grads, chunk))], axis=0
        ).astype(BF16)
        total = total + lax.dot_general(mine_low, spread, NT, preferred_element_type=F32)
    out[...] = total.astype(BF16)


def bucket(place, cover_bins, bin_gradient, members, rows):
    return pl.pallas_call(
        functools.partial(bucket_kernel, rows),
        in_specs=[SMEM, VMEM, VMEM],
        out_shape=jax.ShapeDtypeStruct((members, 3 * COLS), BF16),
        cost_estimate=cost(1e8, 1e5),
        compiler_params=params(),
        name="bucket_entries",
    )(place, cover_bins.T, bin_gradient.T)


def spread_kernel(rows, arrived, out, fields):
    group = pl.program_id(0)
    together = COLS // SLOTS

    @pl.when(group == 0)
    def _():
        members = arrived.shape[0]
        shape = (members // together, members)
        same = (
            lax.broadcasted_iota(jnp.int32, shape, 1) // together
            == lax.broadcasted_iota(jnp.int32, shape, 0)
        )
        fields[...] = jnp.dot(
            jnp.where(same, 1.0, 0.0).astype(BF16), arrived[...], preferred_element_type=F32
        )

    row = fields[pl.ds(group, 1), :]
    low = row[:, :COLS]
    code = row[:, COLS : 2 * COLS]
    value = row[:, 2 * COLS :]
    high = code >= SLOTS
    offset = (low + jnp.where(high, 256.0, 0.0)).astype(jnp.int32)
    slot = lax.broadcasted_iota(jnp.int32, code.shape, 1)
    column = (code - jnp.where(high, 1.0 * SLOTS, 0.0)).astype(jnp.int32) + slot // SLOTS * SLOTS
    width = out.shape[1]
    at_row = jnp.where(
        lax.broadcasted_iota(jnp.int32, (rows, width), 0) == offset, 1.0, 0.0
    ).astype(BF16)
    at_column = jnp.where(
        lax.broadcasted_iota(jnp.int32, (width, width), 0) == column, value, 0.0
    ).astype(BF16)
    reach = (out.shape[0] - rows) // 2
    out[reach : reach + rows, :] = lax.dot_general(
        at_row, at_column, NT, preferred_element_type=F32
    ).astype(BF16)
    out[:reach, :] = jnp.zeros((reach, width), BF16)
    out[reach + rows :, :] = jnp.zeros((reach, width), BF16)


def spread_entries(arrived, rows, reach):
    groups = arrived.shape[0] * SLOTS // COLS
    return pl.pallas_call(
        functools.partial(spread_kernel, rows),
        grid=(groups,),
        in_specs=[pl.BlockSpec(arrived.shape, lambda i: (0, 0))],
        scratch_shapes=[pltpu.VMEM((groups, arrived.shape[1]), F32)],
        out_specs=pl.BlockSpec((rows + 2 * reach, COLS), lambda i: (0, i)),
        out_shape=pltpu.HBM((rows + 2 * reach, groups * COLS), BF16),
        cost_estimate=cost(6e9, 8e6),
        compiler_params=params(),
        name="spread_entries",
    )(arrived)


def fill_edges(spread, low, high):
    reach = low.shape[0]
    rows = spread.shape[0]

    def body(old, low, high, out, sems):
        pairs = [
            (low, out.at[pl.ds(0, reach), :]),
            (high, out.at[pl.ds(rows - reach, reach), :]),
        ]
        for copy in fetch(pairs, sems):
            copy.wait()

    return pl.pallas_call(
        body,
        in_specs=[HBM, VMEM, VMEM],
        out_specs=HBM,
        out_shape=pltpu.HBM(spread.shape, spread.dtype),
        scratch_shapes=[pltpu.SemaphoreType.DMA((2,))],
        input_output_aliases={0: 0},
        cost_estimate=cost(1e6, 1e6),
        compiler_params=params(),
        name="fill_edges",
    )(in_hbm(spread), low, high)


def cut_edges(saved):
    _, rows, share = saved.shape
    count = sum(HALO_SAVED.values())

    def body(saved, first, last, sems):
        pairs = []
        for level, start in EDGE_START.items():
            size = HALO_SAVED[level]
            to = pl.ds(start, size)
            pairs.append((saved.at[level, pl.ds(0, size), :], first.at[to, :]))
            pairs.append((saved.at[level, pl.ds(rows - size, size), :], last.at[to, :]))
        for copy in fetch(pairs, sems):
            copy.wait()

    return pl.pallas_call(
        body,
        in_specs=[HBM],
        out_specs=[VMEM, VMEM],
        out_shape=[jax.ShapeDtypeStruct((count, share), BF16)] * 2,
        scratch_shapes=[pltpu.SemaphoreType.DMA((2 * len(EDGE_START),))],
        cost_estimate=cost(1e6, 6e5),
        compiler_params=params(),
        name="cut_edges",
    )(in_hbm(saved))


def pre_kernel(level, saved, low, high, weight, send, slope, value, act, shifted, kernel, sems):
    dilation = BASE_DILATION * 2**level
    halo, inner = HALO_SAVED[level], HALO_IN[level - 1]
    rows = value.shape[0]
    edge = slice(EDGE_START[level], EDGE_START[level] + halo)
    count = send.shape[0]
    taps = shifted.shape[0]
    columns = column_blocks(send.shape[1])
    pairs = [(saved.at[level], value)]
    for k, cols in enumerate(columns):
        pairs.append((weight.at[level, :, :, cols], kernel.at[k]))
    copies = fetch(pairs, sems)
    for side, start in ((low, 0), (high, halo + rows)):
        act[start : start + halo, :], outside = gelu_parts(side[edge, :].astype(F32))
        if inner and start:
            slope[inner + rows :, :] = outside[:inner].astype(BF16)
        elif inner:
            slope[:inner, :] = outside[halo - inner :].astype(BF16)
    copies[0].wait()
    step = 64

    def part_of(k, _):
        start = pl.multiple_of(k * step, step)
        one, two = gelu_parts(value[pl.ds(start, step), :].astype(F32))
        act[pl.ds(pl.multiple_of(start + halo, 16), step), :] = one
        value[pl.ds(start, step), :] = two.astype(BF16)
        return 0

    lax.fori_loop(0, rows // step, part_of, 0)
    slope[inner : inner + rows, :] = value[...]
    for tap in range(taps):
        start = halo - HALO_IN[level] + (tap - 1) * dilation
        shifted[tap] = act[start : start + count, :].astype(BF16)
    for k, cols in enumerate(columns):
        copies[1 + k].wait()
        total = None
        for tap in range(taps):
            part = jnp.dot(shifted[tap], kernel[k, tap], preferred_element_type=F32)
            total = part if total is None else total + part
        send[:, cols] = total.astype(BF16)


def pre_partial(level, saved, low, high, weights):
    rows, share = saved.shape[1:]
    count = rows + 2 * HALO_IN[level]
    halo = HALO_SAVED[level]
    _, taps, _, width = weights.shape
    blocks = width // COLS
    return pl.pallas_call(
        functools.partial(pre_kernel, level),
        in_specs=[HBM, VMEM, VMEM, HBM],
        out_specs=[VMEM, VMEM],
        out_shape=[
            jax.ShapeDtypeStruct((count, width), BF16),
            jax.ShapeDtypeStruct((rows + 2 * HALO_IN[level - 1], share), BF16),
        ],
        scratch_shapes=[
            pltpu.VMEM((rows, share), BF16),
            pltpu.VMEM((rows + 2 * halo, share), F32),
            pltpu.VMEM((taps, count, share), BF16),
            pltpu.VMEM((blocks, taps, share, COLS), BF16),
            pltpu.SemaphoreType.DMA((1 + blocks,)),
        ],
        cost_estimate=cost(5e9, 8e6),
        compiler_params=params(),
        name=f"pre_partial_{level}",
    )(in_hbm(saved), low, high, in_hbm(weights))


def pre_slope(level, flags, own, other, rows):
    count, width = own.shape
    blocks = pl.BlockSpec((count, COLS), lambda i, flags: (0, i))
    halo = HALO_IN[level]

    def body(flags, own, other, out):
        slope = gelu_parts(own[...].astype(F32) + other[...].astype(F32))[1]
        at = lax.broadcasted_iota(jnp.int32, slope.shape, 0)
        outside = ((at < halo) & (flags[0] != 0)) | ((at >= halo + rows) & (flags[1] != 0))
        out[...] = jnp.where(outside, 0.0, slope).astype(BF16)

    return pl.pallas_call(
        body,
        grid_spec=pltpu.PrefetchScalarGridSpec(
            num_scalar_prefetch=1, grid=(width // COLS,), in_specs=[blocks, blocks], out_specs=blocks
        ),
        out_shape=jax.ShapeDtypeStruct((count, width), BF16),
        cost_estimate=cost(4e9, 5e6),
        compiler_params=params(),
        name=f"pre_slope_{level}",
    )(flags, own, other)


def top_kernel(spread, vectors, expand, grad, send, matrix, held, kernel, sems):
    columns = column_blocks(grad.shape[1])
    level = expand.shape[0] - 1
    part = spread.shape[1] // 4
    quarters = [pl.ds(k * part, part) for k in range(4)]
    first, rest = [], []
    for rows in quarters:
        first.append((spread.at[:, rows], matrix.at[:, rows]))
        first.append((vectors.at[rows, columns[0]], held.at[0, rows, :]))
    for k, cols in enumerate(columns):
        rest.append((expand.at[level, :, cols], kernel.at[k]))
        if k:
            rest.append((vectors.at[:, cols], held.at[k]))
    copies = fetch(first + rest, sems)
    ready = iter(copies)
    middle = None
    for k, cols in enumerate(columns):
        if k == 0:
            top = None
            for rows in quarters:
                next(ready).wait()
                next(ready).wait()
                piece = jnp.dot(matrix[:, rows], held[0, rows, :], preferred_element_type=F32)
                top = piece if top is None else top + piece
            next(ready).wait()
        else:
            next(ready).wait()
            next(ready).wait()
            top = jnp.dot(matrix[...], held[k], preferred_element_type=F32)
        grad[:, cols] = top
        piece = lax.dot_general(top.astype(BF16), kernel[k], NT, preferred_element_type=F32)
        middle = piece if middle is None else middle + piece
    send[...] = middle.astype(BF16)


def top_gradient(spread, vectors, expand):
    count, depth = spread.shape
    share = vectors.shape[1]
    width = expand.shape[1]
    blocks = share // COLS
    return pl.pallas_call(
        top_kernel,
        in_specs=[HBM, HBM, HBM],
        out_specs=[VMEM, VMEM],
        out_shape=[
            jax.ShapeDtypeStruct((count, share), F32),
            jax.ShapeDtypeStruct((count, width), BF16),
        ],
        scratch_shapes=[
            pltpu.VMEM((count, depth), BF16),
            pltpu.VMEM((blocks, depth, COLS), BF16),
            pltpu.VMEM((blocks, width, COLS), BF16),
            pltpu.SemaphoreType.DMA((8 + 2 * blocks - 1,)),
        ],
        cost_estimate=cost(5e9, 14e6),
        compiler_params=params(),
        name="top_gradient",
    )(in_hbm(spread), in_hbm(vectors), in_hbm(expand))


def block_kernel(level, own, other, slope, weight, grad, outer, expand, out, *rest):
    last = level == 0
    pre, shifted, kernel, expander, sems = rest[-5:]
    dilation = BASE_DILATION * 2**level
    count, share = out.shape
    trim = HALO_IN[level] - HALO_IN[level - 1]
    taps = weight.shape[1]
    columns = column_blocks(share)
    pairs = [(weight.at[level, :, cols, :], kernel.at[k]) for k, cols in enumerate(columns)]
    if not last:
        pairs.append((expand.at[level - 1], expander))
    copies = fetch(pairs, sems)
    pre[...] = (own[...].astype(F32) + other[...].astype(F32)) * slope[...].astype(F32)
    for tap in range(taps):
        start = trim - (tap - 1) * dilation
        shifted[tap] = pre[start : start + count, :].astype(BF16)
    middle = None
    for k, cols in enumerate(columns):
        copies[k].wait()
        total = None
        for tap in range(taps):
            part = lax.dot_general(shifted[tap], kernel[k, tap], NT, preferred_element_type=F32)
            total = part if total is None else total + part
        new = grad[trim : trim + count, cols] + total * outer[:, cols].astype(F32)
        if last:
            out[:, cols] = new.astype(BF16)
            continue
        out[:, cols] = new
        if k == 0:
            copies[-1].wait()
        part = lax.dot_general(
            new.astype(BF16), expander[:, cols], NT, preferred_element_type=F32
        )
        middle = part if middle is None else middle + part
    if not last:
        rest[0][...] = middle.astype(BF16)


def block_step(level, own, other, slope, weight, grad, outer, expand):
    count_in, width = own.shape
    count, share = outer.shape
    taps = weight.shape[1]
    blocks = share // COLS
    last = level == 0
    out_shape = [jax.ShapeDtypeStruct((count, share), BF16 if last else F32)]
    if not last:
        out_shape.append(jax.ShapeDtypeStruct((count, width), BF16))
    return pl.pallas_call(
        functools.partial(block_kernel, level),
        in_specs=[VMEM, VMEM, VMEM, HBM, VMEM, VMEM, HBM],
        out_specs=[VMEM] * len(out_shape),
        out_shape=out_shape,
        scratch_shapes=[
            pltpu.VMEM((count_in, width), F32),
            pltpu.VMEM((taps, count, width), BF16),
            pltpu.VMEM((blocks, taps, COLS, width), BF16),
            pltpu.VMEM((width, share), BF16),
            pltpu.SemaphoreType.DMA((blocks + 1,)),
        ],
        cost_estimate=cost(5e9, 14e6),
        compiler_params=params(),
        name=f"block_step_{level}",
    )(own, other, slope, in_hbm(weight), grad, outer, in_hbm(expand))


def after(value, *earlier):
    return lax.optimization_barrier((value, *earlier))[0]


def gather_vectors(vectors, meanwhile, later):
    count = vectors.shape[0]
    place = lax.axis_index("head")
    along, turn = place // 4, place % 4
    same = lambda steps: [(a * 4 + z, a * 4 + (z - steps) % 4) for a in range(2) for z in range(4)]
    parts = [lax.ppermute(vectors, "head", same(k)) for k in (1, 2, 3)]
    parts = [after(vectors, *meanwhile)] + parts
    twice = jnp.concatenate(parts + parts, axis=0)
    ring = lax.dynamic_slice_in_dim(twice, (4 - turn) % 4 * count, 4 * count, 0)
    other = lax.ppermute(ring, "head", [(k, (k + 4) % 8) for k in range(8)])
    ring = after(ring, *later)
    both = jnp.where(
        along == 0,
        jnp.concatenate([ring, other], axis=0),
        jnp.concatenate([other, ring], axis=0),
    )
    return lax.all_gather(both, "pos", tiled=True)


def per_device(
    inputs_saved,
    conv_weight,
    expand_weight,
    head_weight,
    batch_of,
    erase_left,
    erase_right,
    bin_gradient,
    cover_bins,
):
    members = lax.axis_size(GROUP_AXES)
    layers, rows, share = inputs_saved.shape
    member = lax.axis_index(GROUP_AXES)
    chan_place = lax.axis_index("chan")
    up = [(k, k + 1) for k in range(members - 1)]
    down = [(k + 1, k) for k in range(members - 1)]
    swap = [(0, 1), (1, 0)]
    levels = list(reversed(range(layers)))

    vectors = head_vectors(
        chan_place[None].astype(jnp.int32), head_weight, batch_of, erase_left, erase_right, share
    )
    first, final = cut_edges(after(inputs_saved, vectors))
    low = lax.ppermute(final, GROUP_AXES, up)
    high = lax.ppermute(first, GROUP_AXES, down)
    flags = jnp.stack([member == 0, member == members - 1]).astype(jnp.int32)
    sends, outers, others = {}, {}, {}
    for n in levels:
        sends[n], outers[n] = pre_partial(n, inputs_saved, low, high, conv_weight)
        others[n] = lax.ppermute(sends[n], "chan", swap)

    payload = bucket(
        (member % (COLS // SLOTS))[None].astype(jnp.int32), cover_bins, bin_gradient, members, rows
    )
    arrived = lax.all_to_all(
        after(payload, sends[levels[0]]), GROUP_AXES, split_axis=0, concat_axis=0, tiled=True
    )
    gathered = gather_vectors(vectors, (payload, low, high), (sends[levels[0]],))
    reach = HALO_IN[layers - 1]
    spread = spread_entries(after(arrived, *sends.values()), rows, reach)
    spread_low = lax.ppermute(spread[rows : rows + reach], GROUP_AXES, up)
    spread_high = lax.ppermute(spread[reach : 2 * reach], GROUP_AXES, down)
    spread = fill_edges(spread, spread_low, spread_high)
    slopes = {n: pre_slope(n, flags, sends[n], others[n], rows) for n in levels}
    spread = after(spread, others[levels[1]], slopes[levels[0]])

    grad, send = top_gradient(spread, gathered, expand_weight)
    for n in levels:
        other = lax.ppermute(send, "chan", swap)
        outs = block_step(
            n, send, other, slopes[n], conv_weight, grad, outers[n], expand_weight
        )
        if n:
            grad, send = outs
    return outs[0]


def solution(mesh):
    return jax.shard_map(
        per_device,
        mesh=mesh,
        in_specs=(
            P(None, ("pos", "head"), "chan"),
            P(None, None, "chan", None),
            P(None, None, "chan"),
            P(("pos", "head"), None),
            P(("pos", "head")),
            P(),
            P(),
            P(("pos", "head"), None),
            P(("pos", "head"), None),
        ),
        out_specs=P(("pos", "head"), "chan"),
        check_vma=False,
    )
```

```python
import functools

import jax
import jax.numpy as jnp
from jax import lax
from jax.experimental import pallas as pl
from jax.experimental.pallas import tpu as pltpu
from jax.sharding import PartitionSpec as P

BASE_DILATION = 4
RANK = 8
SLOTS = 64
COLS = 256
GROUP_AXES = ("pos", "head")
HALO_IN = {2: 32, 1: 16, 0: 8, -1: 0}
HALO_SAVED = {2: 48, 1: 32, 0: 16}
EDGE_START = {1: 0, 0: 32, 2: 48}
F32 = jnp.float32
BF16 = jnp.bfloat16
NT = (((1,), (1,)), ((), ()))


def cost(flops, bytes_accessed, transcendentals=0):
    return pl.CostEstimate(
        flops=int(flops / 5), bytes_accessed=int(bytes_accessed / 5), transcendentals=0
    )


def params():
    return pltpu.CompilerParams(vmem_limit_bytes=28 * 2**20)


VMEM = pl.BlockSpec(memory_space=pltpu.VMEM)
HBM = pl.BlockSpec(memory_space=pltpu.HBM)
SMEM = pl.BlockSpec(memory_space=pltpu.SMEM)
ROOT_HALF = 0.7071067811865476
DENSITY = 0.3989422804014327


def in_hbm(value):
    return pltpu.with_memory_space_constraint(value, pltpu.HBM)


def fetch(pairs, sems):
    copies = [pltpu.make_async_copy(a, b, sems.at[k]) for k, (a, b) in enumerate(pairs)]
    for copy in copies:
        copy.start()
    return copies


def column_blocks(share):
    return [slice(start, start + COLS) for start in range(0, share, COLS)]


def gelu_parts(value):
    half = 0.5 * (1.0 + lax.erf(value * ROOT_HALF))
    return value * half, half + value * jnp.exp(-0.5 * value * value) * DENSITY


def vectors_kernel(place, weight, share, batch, left, right, out):
    projected = lax.dot_general(left[...], weight[...], NT, preferred_element_type=F32)
    column = lax.broadcasted_iota(jnp.int32, projected.shape, 0) // RANK
    kept = jnp.where(column == batch[...], projected, 0.0)
    removed = lax.dot_general(
        kept, right[...].astype(F32), (((0,), (0,)), ((), ())),
        precision=lax.Precision.HIGHEST, preferred_element_type=F32,
    )
    out[...] = (share[...].astype(F32) - removed).astype(BF16)


def head_vectors(place, head_weight, batch_of, erase_left, erase_right, share):
    count, channels = head_weight.shape
    factors = erase_left.shape[1]
    whole = lambda i, place: (0, 0)
    mine = lambda i, place: (0, place[0])
    return pl.pallas_call(
        vectors_kernel,
        grid_spec=pltpu.PrefetchScalarGridSpec(
            num_scalar_prefetch=1,
            grid=(1,),
            in_specs=[
                pl.BlockSpec((count, channels), whole),
                pl.BlockSpec((count, share), mine),
                pl.BlockSpec((1, count), whole),
                pl.BlockSpec((factors, channels), whole),
                pl.BlockSpec((factors, share), mine),
            ],
            out_specs=pl.BlockSpec((count, share), whole),
        ),
        out_shape=jax.ShapeDtypeStruct((count, share), BF16),
        cost_estimate=cost(1e9, 1e6),
        compiler_params=params(),
        name="head_vectors",
    )(place, *[in_hbm(a) for a in (head_weight, head_weight)], batch_of[None, :],
      in_hbm(erase_left.T), in_hbm(erase_right.T))


def bucket_kernel(rows, bins, grads, out):
    cover, experts = bins.shape
    together = 128 // experts
    lanes = together * experts
    chunks = cover // together
    members = out.shape[0]
    before = jnp.where(
        lax.broadcasted_iota(jnp.int32, (lanes, lanes), 0)
        < lax.broadcasted_iota(jnp.int32, (lanes, lanes), 1),
        1.0, 0.0,
    ).astype(BF16)
    index = lax.broadcasted_iota(jnp.int32, (members, lanes), 0)
    slot = lax.broadcasted_iota(jnp.int32, (SLOTS, lanes), 0)
    expert = lax.broadcasted_iota(jnp.int32, (1, lanes), 1) % experts
    side = lambda ref, chunk: jnp.concatenate(
        [ref[chunk * together + k : chunk * together + k + 1, :] for k in range(together)], axis=1
    )
    base = jnp.zeros((members, 1), F32)
    total = jnp.zeros(out.shape, F32)
    grads = grads[...].astype(F32)
    for chunk in range(chunks):
        place = side(bins, chunk)
        target = place // rows
        offset = place - target * rows
        mine = jnp.where(target == index, 1.0, 0.0)
        mine_low = mine.astype(BF16)
        earlier = jnp.dot(mine_low, before, preferred_element_type=F32) + base
        rank = jnp.sum(mine * earlier, axis=0, keepdims=True).astype(jnp.int32)
        base = base + jnp.sum(mine, axis=1, keepdims=True)
        high = offset // 256
        low = (offset - high * 256).astype(F32)
        code = (expert + high * SLOTS).astype(F32)
        hit = rank == slot
        spread = jnp.concatenate(
            [jnp.where(hit, v, 0.0) for v in (low, code, side(grads, chunk))]
            + [jnp.zeros(hit.shape, F32)],
            axis=0,
        ).astype(BF16)
        total = total + lax.dot_general(mine_low, spread, NT, preferred_element_type=F32)
    out[...] = total.astype(BF16)


def bucket(cover_bins, bin_gradient, members, rows):
    return pl.pallas_call(
        functools.partial(bucket_kernel, rows),
        in_specs=[VMEM, VMEM],
        out_shape=jax.ShapeDtypeStruct((members, 4 * SLOTS), BF16),
        cost_estimate=cost(1e8, 1e5),
        compiler_params=params(),
        name="bucket_entries",
    )(cover_bins.T, bin_gradient.T)


def spread_kernel(rows, along, arrived, out, fields):
    half, group = pl.program_id(0), pl.program_id(1)
    together = COLS // SLOTS

    @pl.when((half == 0) & (group == 0))
    def _():
        members = arrived.shape[0]
        repeat = jnp.where(
            lax.broadcasted_iota(jnp.int32, (SLOTS, COLS), 1) % SLOTS
            == lax.broadcasted_iota(jnp.int32, (SLOTS, COLS), 0),
            1.0, 0.0,
        ).astype(BF16)
        own = (
            lax.broadcasted_iota(jnp.int32, (members, COLS), 1) // SLOTS
            == lax.broadcasted_iota(jnp.int32, (members, COLS), 0) % together
        )
        shape = (members // together, members)
        same = jnp.where(
            lax.broadcasted_iota(jnp.int32, shape, 1) // together
            == lax.broadcasted_iota(jnp.int32, shape, 0),
            1.0, 0.0,
        ).astype(BF16)
        for k in range(3):
            wide = jnp.dot(
                arrived[:, k * SLOTS : (k + 1) * SLOTS], repeat, preferred_element_type=F32
            )
            wide = jnp.where(own, wide, 0.0).astype(BF16)
            fields[:, k * COLS : (k + 1) * COLS] = jnp.dot(
                same, wide, preferred_element_type=F32
            )

    row = fields[pl.ds(group * 2 + (half + along[0]) % 2, 1), :]
    low = row[:, :COLS]
    code = row[:, COLS : 2 * COLS]
    value = row[:, 2 * COLS :]
    high = code >= SLOTS
    offset = (low + jnp.where(high, 256.0, 0.0)).astype(jnp.int32)
    slot = lax.broadcasted_iota(jnp.int32, code.shape, 1)
    column = (code - jnp.where(high, 1.0 * SLOTS, 0.0)).astype(jnp.int32) + slot // SLOTS * SLOTS
    width = out.shape[1]
    at_row = jnp.where(
        lax.broadcasted_iota(jnp.int32, (rows, width), 0) == offset, 1.0, 0.0
    ).astype(BF16)
    at_column = jnp.where(
        lax.broadcasted_iota(jnp.int32, (width, width), 0) == column, value, 0.0
    ).astype(BF16)
    out[...] = lax.dot_general(
        at_row, at_column, NT, preferred_element_type=F32
    ).astype(BF16)


def spread_entries(along, arrived, rows):
    groups = arrived.shape[0] * SLOTS // COLS // 2
    return pl.pallas_call(
        functools.partial(spread_kernel, rows),
        grid_spec=pltpu.PrefetchScalarGridSpec(
            num_scalar_prefetch=1,
            grid=(2, groups),
            in_specs=[pl.BlockSpec(arrived.shape, lambda h, i, along: (0, 0))],
            scratch_shapes=[pltpu.VMEM((2 * groups, 3 * COLS), F32)],
            out_specs=pl.BlockSpec((None, rows, COLS), lambda h, i, along: (h, 0, i)),
        ),
        out_shape=jax.ShapeDtypeStruct((2, rows, groups * COLS), BF16),
        cost_estimate=cost(6e9, 8e6),
        compiler_params=params(),
        name="spread_entries",
    )(along, arrived)


def stage_weights(level, weight, expand):
    last = level == 0
    parts = [(weight, level)] + ([] if last else [(expand, level - 1)])

    def body(*refs):
        sems = refs[-1]
        pairs = [(refs[k].at[n], refs[len(parts) + k]) for k, (_, n) in enumerate(parts)]
        for copy in fetch(pairs, sems):
            copy.wait()

    return pl.pallas_call(
        body,
        in_specs=[HBM] * len(parts),
        out_specs=[VMEM] * len(parts),
        out_shape=[jax.ShapeDtypeStruct(a.shape[1:], a.dtype) for a, _ in parts],
        scratch_shapes=[pltpu.SemaphoreType.DMA((len(parts),))],
        cost_estimate=cost(1e9, 1e6),
        compiler_params=params(),
        name=f"stage_weights_{level}",
    )(*[in_hbm(a) for a, _ in parts])


def cut_edges(saved):
    _, rows, share = saved.shape
    count = sum(HALO_SAVED.values())

    def body(saved, first, last, sems):
        pairs = []
        for level, start in EDGE_START.items():
            size = HALO_SAVED[level]
            to = pl.ds(start, size)
            pairs.append((saved.at[level, pl.ds(0, size), :], first.at[to, :]))
            pairs.append((saved.at[level, pl.ds(rows - size, size), :], last.at[to, :]))
        for copy in fetch(pairs, sems):
            copy.wait()

    return pl.pallas_call(
        body,
        in_specs=[HBM],
        out_specs=[VMEM, VMEM],
        out_shape=[jax.ShapeDtypeStruct((count, share), BF16)] * 2,
        scratch_shapes=[pltpu.SemaphoreType.DMA((2 * len(EDGE_START),))],
        cost_estimate=cost(1e6, 6e5),
        compiler_params=params(),
        name="cut_edges",
    )(in_hbm(saved))


def pre_kernel(level, saved, low, high, weight, send, slope, value, act, shifted, kernel, sems):
    dilation = BASE_DILATION * 2**level
    halo, inner = HALO_SAVED[level], HALO_IN[level - 1]
    rows = value.shape[0]
    edge = slice(EDGE_START[level], EDGE_START[level] + halo)
    count = send.shape[0]
    taps = shifted.shape[0]
    columns = column_blocks(send.shape[1])
    pairs = [(saved.at[level], value)]
    for k, cols in enumerate(columns):
        pairs.append((weight.at[level, :, :, cols], kernel.at[k]))
    copies = fetch(pairs, sems)
    for side, start in ((low, 0), (high, halo + rows)):
        act[start : start + halo, :], outside = gelu_parts(side[edge, :].astype(F32))
        if inner and start:
            slope[inner + rows :, :] = outside[:inner].astype(BF16)
        elif inner:
            slope[:inner, :] = outside[halo - inner :].astype(BF16)
    copies[0].wait()
    step = 64

    def part_of(k, _):
        start = pl.multiple_of(k * step, step)
        one, two = gelu_parts(value[pl.ds(start, step), :].astype(F32))
        act[pl.ds(pl.multiple_of(start + halo, 16), step), :] = one
        value[pl.ds(start, step), :] = two.astype(BF16)
        return 0

    lax.fori_loop(0, rows // step, part_of, 0)
    slope[inner : inner + rows, :] = value[...]
    for tap in range(taps):
        start = halo - HALO_IN[level] + (tap - 1) * dilation
        shifted[tap] = act[start : start + count, :].astype(BF16)
    for k, cols in enumerate(columns):
        copies[1 + k].wait()
        total = None
        for tap in range(taps):
            part = jnp.dot(shifted[tap], kernel[k, tap], preferred_element_type=F32)
            total = part if total is None else total + part
        send[:, cols] = total.astype(BF16)


def pre_partial(level, saved, low, high, weights):
    rows, share = saved.shape[1:]
    count = rows + 2 * HALO_IN[level]
    halo = HALO_SAVED[level]
    _, taps, _, width = weights.shape
    blocks = width // COLS
    return pl.pallas_call(
        functools.partial(pre_kernel, level),
        in_specs=[HBM, VMEM, VMEM, HBM],
        out_specs=[VMEM, VMEM],
        out_shape=[
            jax.ShapeDtypeStruct((count, width), BF16),
            jax.ShapeDtypeStruct((rows + 2 * HALO_IN[level - 1], share), BF16),
        ],
        scratch_shapes=[
            pltpu.VMEM((rows, share), BF16),
            pltpu.VMEM((rows + 2 * halo, share), F32),
            pltpu.VMEM((taps, count, share), BF16),
            pltpu.VMEM((blocks, taps, share, COLS), BF16),
            pltpu.SemaphoreType.DMA((1 + blocks,)),
        ],
        cost_estimate=cost(5e9, 8e6),
        compiler_params=params(),
        name=f"pre_partial_{level}",
    )(in_hbm(saved), low, high, in_hbm(weights))


def pre_slope(level, flags, own, other, rows):
    count, width = own.shape
    blocks = pl.BlockSpec((count, COLS), lambda i, flags: (0, i))
    halo = HALO_IN[level]

    def body(flags, own, other, out):
        slope = gelu_parts(own[...].astype(F32) + other[...].astype(F32))[1]
        at = lax.broadcasted_iota(jnp.int32, slope.shape, 0)
        outside = ((at < halo) & (flags[0] != 0)) | ((at >= halo + rows) & (flags[1] != 0))
        out[...] = jnp.where(outside, 0.0, slope).astype(BF16)

    return pl.pallas_call(
        body,
        grid_spec=pltpu.PrefetchScalarGridSpec(
            num_scalar_prefetch=1, grid=(width // COLS,), in_specs=[blocks, blocks], out_specs=blocks
        ),
        out_shape=jax.ShapeDtypeStruct((count, width), BF16),
        cost_estimate=cost(4e9, 5e6),
        compiler_params=params(),
        name=f"pre_slope_{level}",
    )(flags, own, other)


def top_kernel(half, turned, spread, low, high, vectors, *rest):
    matrix, held, sems = rest[-3:]
    last = half == 1
    if last:
        before, expand, grad, send, kernel = rest[:-3]
    else:
        (grad,) = rest[:-3]
    rows, reach = spread.shape[1], low.shape[1]
    columns = column_blocks(grad.shape[1])
    pairs = [
        (spread.at[half], matrix.at[pl.ds(reach, rows), :]),
        (low.at[(half + turned[0]) % 2], matrix.at[pl.ds(0, reach), :]),
        (high.at[(half + turned[1]) % 2], matrix.at[pl.ds(reach + rows, reach), :]),
    ]
    pairs += [(vectors.at[:, cols], held.at[k]) for k, cols in enumerate(columns)]
    if last:
        pairs.append((expand.at[expand.shape[0] - 1], kernel))
    copies = fetch(pairs, sems)
    for copy in copies[:3]:
        copy.wait()
    middle = None
    for k, cols in enumerate(columns):
        copies[3 + k].wait()
        top = jnp.dot(matrix[...], held[k], preferred_element_type=F32)
        if not last:
            grad[:, cols] = top
            continue
        top = top + before[:, cols]
        grad[:, cols] = top
        if k == 0:
            copies[-1].wait()
        piece = lax.dot_general(
            top.astype(BF16), kernel[:, cols], NT, preferred_element_type=F32
        )
        middle = piece if middle is None else middle + piece
    if last:
        send[...] = middle.astype(BF16)


def top_gradient(half, turned, spread, low, high, vectors, *more):
    _, rows, depth = spread.shape
    count = rows + 2 * low.shape[1]
    share = vectors.shape[1]
    blocks = share // COLS
    out_shape = [jax.ShapeDtypeStruct((count, share), F32)]
    scratch = [pltpu.VMEM((count, depth), BF16), pltpu.VMEM((blocks, depth, COLS), BF16)]
    args = [in_hbm(a) for a in (spread, low, high, vectors)]
    if more:
        before, expand = more
        width = expand.shape[1]
        out_shape.append(jax.ShapeDtypeStruct((count, width), BF16))
        scratch.insert(0, pltpu.VMEM((width, share), BF16))
        args += [before, in_hbm(expand)]
    return pl.pallas_call(
        functools.partial(top_kernel, half),
        in_specs=[SMEM] + [HBM] * 4 + [VMEM, HBM][: len(more)],
        out_specs=[VMEM] * len(out_shape),
        out_shape=out_shape,
        scratch_shapes=scratch + [pltpu.SemaphoreType.DMA((3 + blocks + bool(more),))],
        cost_estimate=cost(5e9, 14e6),
        compiler_params=params(),
        name=f"top_gradient_{half}",
    )(turned, *args)


def block_kernel(level, own, other, slope, weight, grad, outer, *rest):
    last = level == 0
    if last:
        out, pre, shifted = rest
    else:
        expand, out, send, pre, shifted = rest
    dilation = BASE_DILATION * 2**level
    count, share = out.shape
    trim = HALO_IN[level] - HALO_IN[level - 1]
    taps = weight.shape[0]
    pre[...] = (own[...].astype(F32) + other[...].astype(F32)) * slope[...].astype(F32)
    for tap in range(taps):
        start = trim - (tap - 1) * dilation
        shifted[tap] = pre[start : start + count, :].astype(BF16)
    middle = None
    for cols in column_blocks(share):
        total = None
        for tap in range(taps):
            part = lax.dot_general(
                shifted[tap], weight[tap, cols, :], NT, preferred_element_type=F32
            )
            total = part if total is None else total + part
        new = grad[trim : trim + count, cols] + total * outer[:, cols].astype(F32)
        if last:
            out[:, cols] = new.astype(BF16)
            continue
        out[:, cols] = new
        part = lax.dot_general(new.astype(BF16), expand[:, cols], NT, preferred_element_type=F32)
        middle = part if middle is None else middle + part
    if not last:
        send[...] = middle.astype(BF16)


def block_step(level, own, other, slope, weight, grad, outer, *expand):
    count_in, width = own.shape
    count, share = outer.shape
    taps = weight.shape[0]
    last = level == 0
    out_shape = [jax.ShapeDtypeStruct((count, share), BF16 if last else F32)]
    if not last:
        out_shape.append(jax.ShapeDtypeStruct((count, width), BF16))
    return pl.pallas_call(
        functools.partial(block_kernel, level),
        in_specs=[VMEM] * (6 + len(expand)),
        out_specs=[VMEM] * len(out_shape),
        out_shape=out_shape,
        scratch_shapes=[
            pltpu.VMEM((count_in, width), F32),
            pltpu.VMEM((taps, count, width), BF16),
        ],
        cost_estimate=cost(5e9, 14e6),
        compiler_params=params(),
        name=f"block_step_{level}",
    )(own, other, slope, weight, grad, outer, *expand)


def after(value, *earlier):
    return lax.optimization_barrier((value, *earlier))[0]


def gather_vectors(vectors, place, meanwhile, later):
    count = vectors.shape[0]
    turn = place % 4
    same = lambda steps: [(a * 4 + z, a * 4 + (z - steps) % 4) for a in range(2) for z in range(4)]
    parts = [lax.ppermute(vectors, "head", same(k)) for k in (1, 2, 3)]
    parts = [after(vectors, *meanwhile)] + parts
    twice = jnp.concatenate(parts + parts, axis=0)
    ring = lax.dynamic_slice_in_dim(twice, (4 - turn) % 4 * count, 4 * count, 0)
    other = lax.ppermute(ring, "head", [(k, (k + 4) % 8) for k in range(8)])
    near = lax.all_gather(ring, "pos", tiled=True)
    return near, lax.all_gather(after(other, *later), "pos", tiled=True)


def per_device(
    inputs_saved,
    conv_weight,
    expand_weight,
    head_weight,
    batch_of,
    erase_left,
    erase_right,
    bin_gradient,
    cover_bins,
):
    members = lax.axis_size(GROUP_AXES)
    layers, rows, share = inputs_saved.shape
    member = lax.axis_index(GROUP_AXES)
    chan_place = lax.axis_index("chan")
    up = [(k, k + 1) for k in range(members - 1)]
    down = [(k + 1, k) for k in range(members - 1)]
    swap = [(0, 1), (1, 0)]
    levels = list(reversed(range(layers)))

    place = lax.axis_index("head")
    along, turn = place // 4, place % 4
    vectors = head_vectors(
        chan_place[None].astype(jnp.int32), head_weight, batch_of, erase_left, erase_right, share
    )
    first, final = cut_edges(after(inputs_saved, vectors))
    low = lax.ppermute(final, GROUP_AXES, up)
    high = lax.ppermute(first, GROUP_AXES, down)
    payload = bucket(cover_bins, bin_gradient, members, rows)
    flags = jnp.stack([member == 0, member == members - 1]).astype(jnp.int32)
    sends, outers, others = {}, {}, {}

    def begin(n, *earlier):
        sends[n], outers[n] = pre_partial(
            n, inputs_saved, after(low, *earlier), high, conv_weight
        )
        others[n] = lax.ppermute(sends[n], "chan", swap)

    begin(levels[0])
    near, far = gather_vectors(vectors, place, (payload, first), (sends[levels[0]],))
    arrived = lax.all_to_all(
        after(payload, sends[levels[0]]), GROUP_AXES, split_axis=0, concat_axis=0, tiled=True
    )
    reach = HALO_IN[layers - 1]
    spread = spread_entries(along[None].astype(jnp.int32), arrived, rows)
    spread_low = lax.ppermute(spread[:, rows - reach :], GROUP_AXES, up)
    spread_high = lax.ppermute(spread[:, :reach], GROUP_AXES, down)
    begin(levels[1], spread)
    begin(levels[2], spread, sends[levels[1]])
    turned = jnp.stack([turn == 0, turn == 3]).astype(jnp.int32)
    slopes = {n: pre_slope(n, flags, sends[n], others[n], rows) for n in levels}
    entries = (turned, spread, spread_low, spread_high)
    (half,) = top_gradient(0, *entries, after(near, sends[levels[2]]))
    far = after(far, half, others[levels[1]])
    grad, send = top_gradient(1, *entries, far, half, expand_weight)
    for n in levels:
        other = lax.ppermute(send, "chan", swap)
        weights = stage_weights(n, after(conv_weight, send), expand_weight)
        outs = block_step(n, send, other, slopes[n], weights[0], grad, outers[n], *weights[1:])
        if n:
            grad, send = outs
    return outs[0]


def solution(mesh):
    return jax.shard_map(
        per_device,
        mesh=mesh,
        in_specs=(
            P(None, ("pos", "head"), "chan"),
            P(None, None, "chan", None),
            P(None, None, "chan"),
            P(("pos", "head"), None),
            P(("pos", "head")),
            P(),
            P(),
            P(("pos", "head"), None),
            P(("pos", "head"), None),
        ),
        out_specs=P(("pos", "head"), "chan"),
        check_vma=False,
    )
```

```python
import functools

import jax
import jax.numpy as jnp
from jax import lax
from jax.experimental import pallas as pl
from jax.experimental.pallas import tpu as pltpu
from jax.sharding import PartitionSpec as P

BASE_DILATION = 4
RANK = 8
SLOTS = 64
COLS = 256
GROUP_AXES = ("pos", "head")
HALO_IN = {2: 32, 1: 16, 0: 8, -1: 0}
HALO_SAVED = {2: 48, 1: 32, 0: 16}
EDGE_START = {1: 0, 0: 32, 2: 48}
F32 = jnp.float32
BF16 = jnp.bfloat16
NT = (((1,), (1,)), ((), ()))


def cost(flops, bytes_accessed, transcendentals=0):
    return pl.CostEstimate(
        flops=int(flops / 100), bytes_accessed=int(bytes_accessed / 100), transcendentals=0
    )


def params():
    return pltpu.CompilerParams(vmem_limit_bytes=28 * 2**20)


VMEM = pl.BlockSpec(memory_space=pltpu.VMEM)
HBM = pl.BlockSpec(memory_space=pltpu.HBM)
SMEM = pl.BlockSpec(memory_space=pltpu.SMEM)
ROOT_HALF = 0.7071067811865476
DENSITY = 0.3989422804014327


def in_hbm(value):
    return pltpu.with_memory_space_constraint(value, pltpu.HBM)


def fetch(pairs, sems):
    copies = [pltpu.make_async_copy(a, b, sems.at[k]) for k, (a, b) in enumerate(pairs)]
    for copy in copies:
        copy.start()
    return copies


def column_blocks(share):
    return [slice(start, start + COLS) for start in range(0, share, COLS)]


def gelu_parts(value):
    half = 0.5 * (1.0 + lax.erf(value * ROOT_HALF))
    return value * half, half + value * jnp.exp(-0.5 * value * value) * DENSITY


def vectors_kernel(place, weight, share, batch, left, right, out):
    projected = lax.dot_general(left[...], weight[...], NT, preferred_element_type=F32)
    column = lax.broadcasted_iota(jnp.int32, projected.shape, 0) // RANK
    kept = jnp.where(column == batch[...], projected, 0.0)
    removed = lax.dot_general(
        kept, right[...].astype(F32), (((0,), (0,)), ((), ())),
        precision=lax.Precision.HIGHEST, preferred_element_type=F32,
    )
    out[...] = (share[...].astype(F32) - removed).astype(BF16)


def head_vectors(place, head_weight, batch_of, erase_left, erase_right, share):
    count, channels = head_weight.shape
    factors = erase_left.shape[1]
    whole = lambda i, place: (0, 0)
    mine = lambda i, place: (0, place[0])
    return pl.pallas_call(
        vectors_kernel,
        grid_spec=pltpu.PrefetchScalarGridSpec(
            num_scalar_prefetch=1,
            grid=(1,),
            in_specs=[
                pl.BlockSpec((count, channels), whole),
                pl.BlockSpec((count, share), mine),
                pl.BlockSpec((1, count), whole),
                pl.BlockSpec((factors, channels), whole),
                pl.BlockSpec((factors, share), mine),
            ],
            out_specs=pl.BlockSpec((count, share), whole),
        ),
        out_shape=jax.ShapeDtypeStruct((count, share), BF16),
        cost_estimate=cost(1e9, 1e6),
        compiler_params=params(),
        name="head_vectors",
    )(place, *[in_hbm(a) for a in (head_weight, head_weight)], batch_of[None, :],
      in_hbm(erase_left.T), in_hbm(erase_right.T))


def bucket_kernel(rows, bins, grads, out):
    cover, experts = bins.shape
    together = 128 // experts
    lanes = together * experts
    chunks = cover // together
    members = out.shape[0]
    before = jnp.where(
        lax.broadcasted_iota(jnp.int32, (lanes, lanes), 0)
        < lax.broadcasted_iota(jnp.int32, (lanes, lanes), 1),
        1.0, 0.0,
    ).astype(BF16)
    index = lax.broadcasted_iota(jnp.int32, (members, lanes), 0)
    slot = lax.broadcasted_iota(jnp.int32, (SLOTS, lanes), 0)
    expert = lax.broadcasted_iota(jnp.int32, (1, lanes), 1) % experts
    side = lambda ref, chunk: jnp.concatenate(
        [ref[chunk * together + k : chunk * together + k + 1, :] for k in range(together)], axis=1
    )
    base = jnp.zeros((members, 1), F32)
    total = jnp.zeros(out.shape, F32)
    grads = grads[...].astype(F32)
    for chunk in range(chunks):
        place = side(bins, chunk)
        target = place // rows
        offset = place - target * rows
        mine = jnp.where(target == index, 1.0, 0.0)
        mine_low = mine.astype(BF16)
        earlier = jnp.dot(mine_low, before, preferred_element_type=F32) + base
        rank = jnp.sum(mine * earlier, axis=0, keepdims=True).astype(jnp.int32)
        base = base + jnp.sum(mine, axis=1, keepdims=True)
        high = offset // 256
        low = (offset - high * 256).astype(F32)
        code = (expert + high * SLOTS).astype(F32)
        hit = rank == slot
        spread = jnp.concatenate(
            [jnp.where(hit, v, 0.0) for v in (low, code, side(grads, chunk))]
            + [jnp.zeros(hit.shape, F32)],
            axis=0,
        ).astype(BF16)
        total = total + lax.dot_general(mine_low, spread, NT, preferred_element_type=F32)
    out[...] = total.astype(BF16)


def bucket(cover_bins, bin_gradient, members, rows):
    return pl.pallas_call(
        functools.partial(bucket_kernel, rows),
        in_specs=[VMEM, VMEM],
        out_shape=jax.ShapeDtypeStruct((members, 4 * SLOTS), BF16),
        cost_estimate=cost(1e8, 1e5),
        compiler_params=params(),
        name="bucket_entries",
    )(cover_bins.T, bin_gradient.T)


def spread_kernel(rows, along, arrived, out, fields):
    half, group = pl.program_id(0), pl.program_id(1)
    together = COLS // SLOTS

    @pl.when((half == 0) & (group == 0))
    def _():
        members = arrived.shape[0]
        repeat = jnp.where(
            lax.broadcasted_iota(jnp.int32, (SLOTS, COLS), 1) % SLOTS
            == lax.broadcasted_iota(jnp.int32, (SLOTS, COLS), 0),
            1.0, 0.0,
        ).astype(BF16)
        own = (
            lax.broadcasted_iota(jnp.int32, (members, COLS), 1) // SLOTS
            == lax.broadcasted_iota(jnp.int32, (members, COLS), 0) % together
        )
        shape = (members // together, members)
        same = jnp.where(
            lax.broadcasted_iota(jnp.int32, shape, 1) // together
            == lax.broadcasted_iota(jnp.int32, shape, 0),
            1.0, 0.0,
        ).astype(BF16)
        for k in range(3):
            wide = jnp.dot(
                arrived[:, k * SLOTS : (k + 1) * SLOTS], repeat, preferred_element_type=F32
            )
            wide = jnp.where(own, wide, 0.0).astype(BF16)
            fields[:, k * COLS : (k + 1) * COLS] = jnp.dot(
                same, wide, preferred_element_type=F32
            )

    row = fields[pl.ds(group * 2 + (half + along[0]) % 2, 1), :]
    low = row[:, :COLS]
    code = row[:, COLS : 2 * COLS]
    value = row[:, 2 * COLS :]
    high = code >= SLOTS
    offset = (low + jnp.where(high, 256.0, 0.0)).astype(jnp.int32)
    slot = lax.broadcasted_iota(jnp.int32, code.shape, 1)
    column = (code - jnp.where(high, 1.0 * SLOTS, 0.0)).astype(jnp.int32) + slot // SLOTS * SLOTS
    width = out.shape[1]
    at_row = jnp.where(
        lax.broadcasted_iota(jnp.int32, (rows, width), 0) == offset, 1.0, 0.0
    ).astype(BF16)
    at_column = jnp.where(
        lax.broadcasted_iota(jnp.int32, (width, width), 0) == column, value, 0.0
    ).astype(BF16)
    out[...] = lax.dot_general(
        at_row, at_column, NT, preferred_element_type=F32
    ).astype(BF16)


def spread_entries(along, arrived, rows):
    groups = arrived.shape[0] * SLOTS // COLS // 2
    return pl.pallas_call(
        functools.partial(spread_kernel, rows),
        grid_spec=pltpu.PrefetchScalarGridSpec(
            num_scalar_prefetch=1,
            grid=(2, groups),
            in_specs=[pl.BlockSpec(arrived.shape, lambda h, i, along: (0, 0))],
            scratch_shapes=[pltpu.VMEM((2 * groups, 3 * COLS), F32)],
            out_specs=pl.BlockSpec((None, rows, COLS), lambda h, i, along: (h, 0, i)),
        ),
        out_shape=jax.ShapeDtypeStruct((2, rows, groups * COLS), BF16),
        cost_estimate=cost(6e9, 8e6),
        compiler_params=params(),
        name="spread_entries",
    )(along, arrived)


def stage_weights(level, weight, expand):
    last = level == 0
    parts = [(weight, level)] + ([] if last else [(expand, level - 1)])

    def body(*refs):
        sems = refs[-1]
        pairs = [(refs[k].at[n], refs[len(parts) + k]) for k, (_, n) in enumerate(parts)]
        for copy in fetch(pairs, sems):
            copy.wait()

    return pl.pallas_call(
        body,
        in_specs=[HBM] * len(parts),
        out_specs=[VMEM] * len(parts),
        out_shape=[jax.ShapeDtypeStruct(a.shape[1:], a.dtype) for a, _ in parts],
        scratch_shapes=[pltpu.SemaphoreType.DMA((len(parts),))],
        cost_estimate=cost(1e9, 1e6),
        compiler_params=params(),
        name=f"stage_weights_{level}",
    )(*[in_hbm(a) for a, _ in parts])


def cut_edges(saved):
    _, rows, share = saved.shape
    count = sum(HALO_SAVED.values())

    def body(saved, first, last, sems):
        pairs = []
        for level, start in EDGE_START.items():
            size = HALO_SAVED[level]
            to = pl.ds(start, size)
            pairs.append((saved.at[level, pl.ds(0, size), :], first.at[to, :]))
            pairs.append((saved.at[level, pl.ds(rows - size, size), :], last.at[to, :]))
        for copy in fetch(pairs, sems):
            copy.wait()

    return pl.pallas_call(
        body,
        in_specs=[HBM],
        out_specs=[VMEM, VMEM],
        out_shape=[jax.ShapeDtypeStruct((count, share), BF16)] * 2,
        scratch_shapes=[pltpu.SemaphoreType.DMA((2 * len(EDGE_START),))],
        cost_estimate=cost(1e6, 6e5),
        compiler_params=params(),
        name="cut_edges",
    )(in_hbm(saved))


def pre_kernel(level, saved, low, high, weight, send, slope, value, act, shifted, kernel, sems):
    dilation = BASE_DILATION * 2**level
    halo, inner = HALO_SAVED[level], HALO_IN[level - 1]
    rows = value.shape[0]
    edge = slice(EDGE_START[level], EDGE_START[level] + halo)
    count = send.shape[0]
    taps = shifted.shape[0]
    columns = column_blocks(send.shape[1])
    pairs = [(saved.at[level], value)]
    for k, cols in enumerate(columns):
        pairs.append((weight.at[level, :, :, cols], kernel.at[k]))
    copies = fetch(pairs, sems)
    for side, start in ((low, 0), (high, halo + rows)):
        act[start : start + halo, :], outside = gelu_parts(side[edge, :].astype(F32))
        if inner and start:
            slope[inner + rows :, :] = outside[:inner].astype(BF16)
        elif inner:
            slope[:inner, :] = outside[halo - inner :].astype(BF16)
    copies[0].wait()
    step = 64

    def part_of(k, _):
        start = pl.multiple_of(k * step, step)
        one, two = gelu_parts(value[pl.ds(start, step), :].astype(F32))
        act[pl.ds(pl.multiple_of(start + halo, 16), step), :] = one
        value[pl.ds(start, step), :] = two.astype(BF16)
        return 0

    lax.fori_loop(0, rows // step, part_of, 0)
    slope[inner : inner + rows, :] = value[...]
    for tap in range(taps):
        start = halo - HALO_IN[level] + (tap - 1) * dilation
        shifted[tap] = act[start : start + count, :].astype(BF16)
    for k, cols in enumerate(columns):
        copies[1 + k].wait()
        total = None
        for tap in range(taps):
            part = jnp.dot(shifted[tap], kernel[k, tap], preferred_element_type=F32)
            total = part if total is None else total + part
        send[:, cols] = total.astype(BF16)


def pre_partial(level, saved, low, high, weights):
    rows, share = saved.shape[1:]
    count = rows + 2 * HALO_IN[level]
    halo = HALO_SAVED[level]
    _, taps, _, width = weights.shape
    blocks = width // COLS
    return pl.pallas_call(
        functools.partial(pre_kernel, level),
        in_specs=[HBM, VMEM, VMEM, HBM],
        out_specs=[VMEM, VMEM],
        out_shape=[
            jax.ShapeDtypeStruct((count, width), BF16),
            jax.ShapeDtypeStruct((rows + 2 * HALO_IN[level - 1], share), BF16),
        ],
        scratch_shapes=[
            pltpu.VMEM((rows, share), BF16),
            pltpu.VMEM((rows + 2 * halo, share), F32),
            pltpu.VMEM((taps, count, share), BF16),
            pltpu.VMEM((blocks, taps, share, COLS), BF16),
            pltpu.SemaphoreType.DMA((1 + blocks,)),
        ],
        cost_estimate=cost(5e9, 8e6),
        compiler_params=params(),
        name=f"pre_partial_{level}",
    )(in_hbm(saved), low, high, in_hbm(weights))


def pre_slope(level, flags, own, other, rows):
    count, width = own.shape
    blocks = pl.BlockSpec((count, COLS), lambda i, flags: (0, i))
    halo = HALO_IN[level]

    def body(flags, own, other, out):
        slope = gelu_parts(own[...].astype(F32) + other[...].astype(F32))[1]
        at = lax.broadcasted_iota(jnp.int32, slope.shape, 0)
        outside = ((at < halo) & (flags[0] != 0)) | ((at >= halo + rows) & (flags[1] != 0))
        out[...] = jnp.where(outside, 0.0, slope).astype(BF16)

    return pl.pallas_call(
        body,
        grid_spec=pltpu.PrefetchScalarGridSpec(
            num_scalar_prefetch=1, grid=(width // COLS,), in_specs=[blocks, blocks], out_specs=blocks
        ),
        out_shape=jax.ShapeDtypeStruct((count, width), BF16),
        cost_estimate=cost(4e9, 5e6),
        compiler_params=params(),
        name=f"pre_slope_{level}",
    )(flags, own, other)


def top_kernel(turned, spread, low, high, vectors, expand, grad, send, matrix, held, kernel, sems):
    rows, reach = spread.shape[1], low.shape[1]
    columns = column_blocks(grad.shape[1])
    pairs = []
    for k, cols in enumerate(columns):
        for half in range(2):
            if k == 0:
                pairs += [
                    (spread.at[half], matrix.at[half, pl.ds(reach, rows), :]),
                    (low.at[(half + turned[0]) % 2], matrix.at[half, pl.ds(0, reach), :]),
                    (
                        high.at[(half + turned[1]) % 2],
                        matrix.at[half, pl.ds(reach + rows, reach), :],
                    ),
                ]
            pairs.append((vectors.at[:, half, :, cols], held.at[k, half]))
        pairs.append((expand.at[expand.shape[0] - 1, :, cols], kernel.at[k]))
    copies = iter(fetch(pairs, sems))
    middle = None
    for k, cols in enumerate(columns):
        top = None
        for half in range(2):
            for _ in range(1 if k else 4):
                next(copies).wait()
            these = held[k, half].reshape(matrix.shape[2], COLS)
            piece = jnp.dot(matrix[half], these, preferred_element_type=F32)
            top = piece if top is None else top + piece
        grad[:, cols] = top
        next(copies).wait()
        piece = lax.dot_general(top.astype(BF16), kernel[k], NT, preferred_element_type=F32)
        middle = piece if middle is None else middle + piece
    send[...] = middle.astype(BF16)


def top_gradient(turned, spread, low, high, vectors, expand):
    _, rows, depth = spread.shape
    count = rows + 2 * low.shape[1]
    share = vectors.shape[1]
    width = expand.shape[1]
    blocks = share // COLS
    vectors = vectors.reshape(depth // SLOTS, 2, SLOTS, share)
    return pl.pallas_call(
        top_kernel,
        in_specs=[SMEM] + [HBM] * 5,
        out_specs=[VMEM, VMEM],
        out_shape=[
            jax.ShapeDtypeStruct((count, share), F32),
            jax.ShapeDtypeStruct((count, width), BF16),
        ],
        scratch_shapes=[
            pltpu.VMEM((2, count, depth), BF16),
            pltpu.VMEM((blocks, 2, depth // SLOTS, SLOTS, COLS), BF16),
            pltpu.VMEM((blocks, width, COLS), BF16),
            pltpu.SemaphoreType.DMA((6 + 3 * blocks,)),
        ],
        cost_estimate=cost(5e9, 14e6),
        compiler_params=params(),
        name="top_gradient",
    )(turned, *[in_hbm(a) for a in (spread, low, high, vectors, expand)])


def block_kernel(level, own, other, slope, weight, grad, outer, *rest):
    last = level == 0
    if last:
        out, pre, shifted = rest
    else:
        expand, out, send, pre, shifted = rest
    dilation = BASE_DILATION * 2**level
    count, share = out.shape
    trim = HALO_IN[level] - HALO_IN[level - 1]
    taps = weight.shape[0]
    pre[...] = (own[...].astype(F32) + other[...].astype(F32)) * slope[...].astype(F32)
    for tap in range(taps):
        start = trim - (tap - 1) * dilation
        shifted[tap] = pre[start : start + count, :].astype(BF16)
    middle = None
    for cols in column_blocks(share):
        total = None
        for tap in range(taps):
            part = lax.dot_general(
                shifted[tap], weight[tap, cols, :], NT, preferred_element_type=F32
            )
            total = part if total is None else total + part
        new = grad[trim : trim + count, cols] + total * outer[:, cols].astype(F32)
        if last:
            out[:, cols] = new.astype(BF16)
            continue
        out[:, cols] = new
        part = lax.dot_general(new.astype(BF16), expand[:, cols], NT, preferred_element_type=F32)
        middle = part if middle is None else middle + part
    if not last:
        send[...] = middle.astype(BF16)


def block_step(level, own, other, slope, weight, grad, outer, *expand):
    count_in, width = own.shape
    count, share = outer.shape
    taps = weight.shape[0]
    last = level == 0
    out_shape = [jax.ShapeDtypeStruct((count, share), BF16 if last else F32)]
    if not last:
        out_shape.append(jax.ShapeDtypeStruct((count, width), BF16))
    return pl.pallas_call(
        functools.partial(block_kernel, level),
        in_specs=[VMEM] * (6 + len(expand)),
        out_specs=[VMEM] * len(out_shape),
        out_shape=out_shape,
        scratch_shapes=[
            pltpu.VMEM((count_in, width), F32),
            pltpu.VMEM((taps, count, width), BF16),
        ],
        cost_estimate=cost(5e9, 14e6),
        compiler_params=params(),
        name=f"block_step_{level}",
    )(own, other, slope, weight, grad, outer, *expand)


def after(value, *earlier):
    return lax.optimization_barrier((value, *earlier))[0]


def along_head(vectors, place, first, second):
    count = vectors.shape[0]
    turn = place % 4
    same = lambda steps: [(a * 4 + z, a * 4 + (z - steps) % 4) for a in range(2) for z in range(4)]
    other = lax.ppermute(vectors, "head", [(k, (k + 4) % 8) for k in range(8)])
    both = jnp.concatenate([after(vectors, *first), other], axis=0)
    parts = [lax.ppermute(both, "head", same(k)) for k in (1, 2, 3)]
    parts = [after(both, *second)] + parts
    twice = jnp.concatenate(parts + parts, axis=0)
    return lax.dynamic_slice_in_dim(twice, (4 - turn) % 4 * 2 * count, 8 * count, 0)


def per_device(
    inputs_saved,
    conv_weight,
    expand_weight,
    head_weight,
    batch_of,
    erase_left,
    erase_right,
    bin_gradient,
    cover_bins,
):
    members = lax.axis_size(GROUP_AXES)
    layers, rows, share = inputs_saved.shape
    member = lax.axis_index(GROUP_AXES)
    chan_place = lax.axis_index("chan")
    up = [(k, k + 1) for k in range(members - 1)]
    down = [(k + 1, k) for k in range(members - 1)]
    swap = [(0, 1), (1, 0)]
    levels = list(reversed(range(layers)))

    place = lax.axis_index("head")
    along, turn = place // 4, place % 4
    vectors = head_vectors(
        chan_place[None].astype(jnp.int32), head_weight, batch_of, erase_left, erase_right, share
    )
    first, final = cut_edges(after(inputs_saved, vectors))
    low = lax.ppermute(final, GROUP_AXES, up)
    high = lax.ppermute(first, GROUP_AXES, down)
    payload = bucket(cover_bins, bin_gradient, members, rows)
    flags = jnp.stack([member == 0, member == members - 1]).astype(jnp.int32)
    sends, outers, others = {}, {}, {}

    def begin(n, *earlier):
        sends[n], outers[n] = pre_partial(
            n, inputs_saved, after(low, *earlier), high, conv_weight
        )

    def exchange(n, *earlier):
        others[n] = lax.ppermute(after(sends[n], *earlier), "chan", swap)

    begin(levels[0])
    exchange(levels[0])
    ring = along_head(vectors, place, (payload, first), (sends[levels[0]],))
    gathered = lax.all_gather(ring, "pos", tiled=True)
    arrived = lax.all_to_all(
        after(payload, ring), GROUP_AXES, split_axis=0, concat_axis=0, tiled=True
    )
    begin(levels[1], ring)
    exchange(levels[1])
    reach = HALO_IN[layers - 1]
    spread = spread_entries(
        along[None].astype(jnp.int32), after(arrived, sends[levels[1]]), rows
    )
    spread_low = lax.ppermute(spread[:, rows - reach :], GROUP_AXES, up)
    spread_high = lax.ppermute(spread[:, :reach], GROUP_AXES, down)
    begin(levels[2], spread, others[levels[0]])
    turned = jnp.stack([turn == 0, turn == 3]).astype(jnp.int32)
    gathered = after(gathered, sends[levels[2]], others[levels[1]])
    grad, send = top_gradient(
        turned, spread, spread_low, spread_high, gathered, expand_weight
    )
    for n in levels:
        other = lax.ppermute(send, "chan", swap)
        if n == levels[0]:
            exchange(levels[2], other)
        slope = pre_slope(n, flags, sends[n], after(others[n], send), rows)
        weights = stage_weights(n, after(conv_weight, slope), expand_weight)
        outs = block_step(n, send, other, slope, weights[0], grad, outers[n], *weights[1:])
        if n:
            grad, send = outs
    return outs[0]


def solution(mesh):
    return jax.shard_map(
        per_device,
        mesh=mesh,
        in_specs=(
            P(None, ("pos", "head"), "chan"),
            P(None, None, "chan", None),
            P(None, None, "chan"),
            P(("pos", "head"), None),
            P(("pos", "head")),
            P(),
            P(),
            P(("pos", "head"), None),
            P(("pos", "head"), None),
        ),
        out_specs=P(("pos", "head"), "chan"),
        check_vma=False,
    )
```

```python
import functools

import jax
import jax.numpy as jnp
from jax import lax
from jax.experimental import pallas as pl
from jax.experimental.pallas import tpu as pltpu
from jax.sharding import PartitionSpec as P

BASE_DILATION = 4
RANK = 8
SLOTS = 64
COLS = 256
GROUP_AXES = ("pos", "head")
HALO_IN = {2: 32, 1: 16, 0: 8, -1: 0}
HALO_SAVED = {2: 48, 1: 32, 0: 16}
EDGE_START = {1: 0, 0: 32, 2: 48}
F32 = jnp.float32
BF16 = jnp.bfloat16
NT = (((1,), (1,)), ((), ()))


def cost(flops, bytes_accessed, transcendentals=0):
    return pl.CostEstimate(
        flops=int(flops / 100), bytes_accessed=int(bytes_accessed / 100), transcendentals=0
    )


def params():
    return pltpu.CompilerParams(vmem_limit_bytes=28 * 2**20)


VMEM = pl.BlockSpec(memory_space=pltpu.VMEM)
HBM = pl.BlockSpec(memory_space=pltpu.HBM)
SMEM = pl.BlockSpec(memory_space=pltpu.SMEM)
ROOT_HALF = 0.7071067811865476
DENSITY = 0.3989422804014327


def in_hbm(value):
    return pltpu.with_memory_space_constraint(value, pltpu.HBM)


def fetch(pairs, sems):
    copies = [pltpu.make_async_copy(a, b, sems.at[k]) for k, (a, b) in enumerate(pairs)]
    for copy in copies:
        copy.start()
    return copies


def staged(batches, sems):
    made, k = [], 0
    for batch in batches:
        made.append([pltpu.make_async_copy(a, b, sems.at[k + i]) for i, (a, b) in enumerate(batch)])
        k += len(batch)
    ahead = iter(made)

    def begin():
        for copy in next(ahead, ()):
            copy.start()

    behind = iter(made)

    def arrive():
        for copy in next(behind):
            copy.wait()
        begin()

    begin()
    begin()
    return arrive


def column_blocks(share):
    return [slice(start, start + COLS) for start in range(0, share, COLS)]


def gelu_parts(value):
    half = 0.5 * (1.0 + lax.erf(value * ROOT_HALF))
    return value * half, half + value * jnp.exp(-0.5 * value * value) * DENSITY


def vectors_kernel(place, weight, share, batch, left, right, out):
    projected = lax.dot_general(left[...], weight[...], NT, preferred_element_type=F32)
    column = lax.broadcasted_iota(jnp.int32, projected.shape, 0) // RANK
    kept = jnp.where(column == batch[...], projected, 0.0)
    removed = lax.dot_general(
        kept, right[...].astype(F32), (((0,), (0,)), ((), ())),
        precision=lax.Precision.HIGHEST, preferred_element_type=F32,
    )
    out[...] = (share[...].astype(F32) - removed).astype(BF16)


def head_vectors(place, head_weight, batch_of, erase_left, erase_right, share):
    count, channels = head_weight.shape
    factors = erase_left.shape[1]
    whole = lambda i, place: (0, 0)
    mine = lambda i, place: (0, place[0])
    return pl.pallas_call(
        vectors_kernel,
        grid_spec=pltpu.PrefetchScalarGridSpec(
            num_scalar_prefetch=1,
            grid=(1,),
            in_specs=[
                pl.BlockSpec((count, channels), whole),
                pl.BlockSpec((count, share), mine),
                pl.BlockSpec((1, count), whole),
                pl.BlockSpec((factors, channels), whole),
                pl.BlockSpec((factors, share), mine),
            ],
            out_specs=pl.BlockSpec((count, share), whole),
        ),
        out_shape=jax.ShapeDtypeStruct((count, share), BF16),
        cost_estimate=cost(1e9, 1e6),
        compiler_params=params(),
        name="head_vectors",
    )(place, *[in_hbm(a) for a in (head_weight, head_weight)], batch_of[None, :],
      in_hbm(erase_left.T), in_hbm(erase_right.T))


def bucket_kernel(rows, bins, grads, out):
    cover, experts = bins.shape
    together = 128 // experts
    lanes = together * experts
    chunks = cover // together
    members = out.shape[0]
    before = jnp.where(
        lax.broadcasted_iota(jnp.int32, (lanes, lanes), 0)
        < lax.broadcasted_iota(jnp.int32, (lanes, lanes), 1),
        1.0, 0.0,
    ).astype(BF16)
    index = lax.broadcasted_iota(jnp.int32, (members, lanes), 0)
    slot = lax.broadcasted_iota(jnp.int32, (SLOTS, lanes), 0)
    expert = lax.broadcasted_iota(jnp.int32, (1, lanes), 1) % experts
    side = lambda ref, chunk: jnp.concatenate(
        [ref[chunk * together + k : chunk * together + k + 1, :] for k in range(together)], axis=1
    )
    base = jnp.zeros((members, 1), F32)
    total = jnp.zeros(out.shape, F32)
    grads = grads[...].astype(F32)
    for chunk in range(chunks):
        place = side(bins, chunk)
        target = place // rows
        offset = place - target * rows
        mine = jnp.where(target == index, 1.0, 0.0)
        mine_low = mine.astype(BF16)
        earlier = jnp.dot(mine_low, before, preferred_element_type=F32) + base
        rank = jnp.sum(mine * earlier, axis=0, keepdims=True).astype(jnp.int32)
        base = base + jnp.sum(mine, axis=1, keepdims=True)
        high = offset // 256
        low = (offset - high * 256).astype(F32)
        code = (expert + high * SLOTS).astype(F32)
        hit = rank == slot
        spread = jnp.concatenate(
            [jnp.where(hit, v, 0.0) for v in (low, code, side(grads, chunk))]
            + [jnp.zeros(hit.shape, F32)],
            axis=0,
        ).astype(BF16)
        total = total + lax.dot_general(mine_low, spread, NT, preferred_element_type=F32)
    out[...] = total.astype(BF16)


def bucket(cover_bins, bin_gradient, members, rows):
    return pl.pallas_call(
        functools.partial(bucket_kernel, rows),
        in_specs=[VMEM, VMEM],
        out_shape=jax.ShapeDtypeStruct((members, 4 * SLOTS), BF16),
        cost_estimate=cost(1e8, 1e5),
        compiler_params=params(),
        name="bucket_entries",
    )(cover_bins.T, bin_gradient.T)


def spread_kernel(rows, along, arrived, out, fields):
    half, group = pl.program_id(0), pl.program_id(1)
    together = COLS // SLOTS

    @pl.when((half == 0) & (group == 0))
    def _():
        members = arrived.shape[0]
        repeat = jnp.where(
            lax.broadcasted_iota(jnp.int32, (SLOTS, COLS), 1) % SLOTS
            == lax.broadcasted_iota(jnp.int32, (SLOTS, COLS), 0),
            1.0, 0.0,
        ).astype(BF16)
        own = (
            lax.broadcasted_iota(jnp.int32, (members, COLS), 1) // SLOTS
            == lax.broadcasted_iota(jnp.int32, (members, COLS), 0) % together
        )
        shape = (members // together, members)
        same = jnp.where(
            lax.broadcasted_iota(jnp.int32, shape, 1) // together
            == lax.broadcasted_iota(jnp.int32, shape, 0),
            1.0, 0.0,
        ).astype(BF16)
        for k in range(3):
            wide = jnp.dot(
                arrived[:, k * SLOTS : (k + 1) * SLOTS], repeat, preferred_element_type=F32
            )
            wide = jnp.where(own, wide, 0.0).astype(BF16)
            fields[:, k * COLS : (k + 1) * COLS] = jnp.dot(
                same, wide, preferred_element_type=F32
            )

    row = fields[pl.ds(group * 2 + (half + along[0]) % 2, 1), :]
    low = row[:, :COLS]
    code = row[:, COLS : 2 * COLS]
    value = row[:, 2 * COLS :]
    high = code >= SLOTS
    offset = (low + jnp.where(high, 256.0, 0.0)).astype(jnp.int32)
    slot = lax.broadcasted_iota(jnp.int32, code.shape, 1)
    column = (code - jnp.where(high, 1.0 * SLOTS, 0.0)).astype(jnp.int32) + slot // SLOTS * SLOTS
    width = out.shape[1]
    at_row = jnp.where(
        lax.broadcasted_iota(jnp.int32, (rows, width), 0) == offset, 1.0, 0.0
    ).astype(BF16)
    at_column = jnp.where(
        lax.broadcasted_iota(jnp.int32, (width, width), 0) == column, value, 0.0
    ).astype(BF16)
    out[...] = lax.dot_general(
        at_row, at_column, NT, preferred_element_type=F32
    ).astype(BF16)


def spread_entries(along, arrived, rows):
    groups = arrived.shape[0] * SLOTS // COLS // 2
    return pl.pallas_call(
        functools.partial(spread_kernel, rows),
        grid_spec=pltpu.PrefetchScalarGridSpec(
            num_scalar_prefetch=1,
            grid=(2, groups),
            in_specs=[pl.BlockSpec(arrived.shape, lambda h, i, along: (0, 0))],
            scratch_shapes=[pltpu.VMEM((2 * groups, 3 * COLS), F32)],
            out_specs=pl.BlockSpec((None, rows, COLS), lambda h, i, along: (h, 0, i)),
        ),
        out_shape=jax.ShapeDtypeStruct((2, rows, groups * COLS), BF16),
        cost_estimate=cost(6e9, 8e6),
        compiler_params=params(),
        name="spread_entries",
    )(along, arrived)


def stage_weights(level, weight, expand):
    last = level == 0
    parts = [(weight, level)] + ([] if last else [(expand, level - 1)])

    def body(*refs):
        sems = refs[-1]
        pairs = [(refs[k].at[n], refs[len(parts) + k]) for k, (_, n) in enumerate(parts)]
        for copy in fetch(pairs, sems):
            copy.wait()

    return pl.pallas_call(
        body,
        in_specs=[HBM] * len(parts),
        out_specs=[VMEM] * len(parts),
        out_shape=[jax.ShapeDtypeStruct(a.shape[1:], a.dtype) for a, _ in parts],
        scratch_shapes=[pltpu.SemaphoreType.DMA((len(parts),))],
        cost_estimate=cost(1e9, 1e6),
        compiler_params=params(),
        name=f"stage_weights_{level}",
    )(*[in_hbm(a) for a, _ in parts])


def cut_edges(saved):
    _, rows, share = saved.shape
    count = sum(HALO_SAVED.values())

    def body(saved, first, last, sems):
        pairs = []
        for level, start in EDGE_START.items():
            size = HALO_SAVED[level]
            to = pl.ds(start, size)
            pairs.append((saved.at[level, pl.ds(0, size), :], first.at[to, :]))
            pairs.append((saved.at[level, pl.ds(rows - size, size), :], last.at[to, :]))
        for copy in fetch(pairs, sems):
            copy.wait()

    return pl.pallas_call(
        body,
        in_specs=[HBM],
        out_specs=[VMEM, VMEM],
        out_shape=[jax.ShapeDtypeStruct((count, share), BF16)] * 2,
        scratch_shapes=[pltpu.SemaphoreType.DMA((2 * len(EDGE_START),))],
        cost_estimate=cost(1e6, 6e5),
        compiler_params=params(),
        name="cut_edges",
    )(in_hbm(saved))


def pre_kernel(level, saved, low, high, weight, send, slope, value, act, shifted, kernel, sems):
    dilation = BASE_DILATION * 2**level
    halo, inner = HALO_SAVED[level], HALO_IN[level - 1]
    rows = value.shape[0]
    edge = slice(EDGE_START[level], EDGE_START[level] + halo)
    count = send.shape[0]
    taps = shifted.shape[0]
    columns = column_blocks(send.shape[1])
    batches = [[(saved.at[level], value)], []]
    for k, cols in enumerate(columns):
        batches.append([(weight.at[level, :, :, cols], kernel.at[k])])
    arrive = staged(batches, sems)
    for side, start in ((low, 0), (high, halo + rows)):
        act[start : start + halo, :], outside = gelu_parts(side[edge, :].astype(F32))
        if inner and start:
            slope[inner + rows :, :] = outside[:inner].astype(BF16)
        elif inner:
            slope[:inner, :] = outside[halo - inner :].astype(BF16)
    arrive()
    arrive()
    step = 64

    def part_of(k, _):
        start = pl.multiple_of(k * step, step)
        one, two = gelu_parts(value[pl.ds(start, step), :].astype(F32))
        act[pl.ds(pl.multiple_of(start + halo, 16), step), :] = one
        value[pl.ds(start, step), :] = two.astype(BF16)
        return 0

    lax.fori_loop(0, rows // step, part_of, 0)
    slope[inner : inner + rows, :] = value[...]
    for tap in range(taps):
        start = halo - HALO_IN[level] + (tap - 1) * dilation
        shifted[tap] = act[start : start + count, :].astype(BF16)
    for k, cols in enumerate(columns):
        arrive()
        total = None
        for tap in range(taps):
            part = jnp.dot(shifted[tap], kernel[k, tap], preferred_element_type=F32)
            total = part if total is None else total + part
        send[:, cols] = total.astype(BF16)


def pre_partial(level, saved, low, high, weights):
    rows, share = saved.shape[1:]
    count = rows + 2 * HALO_IN[level]
    halo = HALO_SAVED[level]
    _, taps, _, width = weights.shape
    blocks = width // COLS
    return pl.pallas_call(
        functools.partial(pre_kernel, level),
        in_specs=[HBM, VMEM, VMEM, HBM],
        out_specs=[VMEM, VMEM],
        out_shape=[
            jax.ShapeDtypeStruct((count, width), BF16),
            jax.ShapeDtypeStruct((rows + 2 * HALO_IN[level - 1], share), BF16),
        ],
        scratch_shapes=[
            pltpu.VMEM((rows, share), BF16),
            pltpu.VMEM((rows + 2 * halo, share), F32),
            pltpu.VMEM((taps, count, share), BF16),
            pltpu.VMEM((blocks, taps, share, COLS), BF16),
            pltpu.SemaphoreType.DMA((1 + blocks,)),
        ],
        cost_estimate=cost(5e9, 8e6),
        compiler_params=params(),
        name=f"pre_partial_{level}",
    )(in_hbm(saved), low, high, in_hbm(weights))


def pre_slope(level, flags, own, other, rows):
    count, width = own.shape
    blocks = pl.BlockSpec((count, COLS), lambda i, flags: (0, i))
    halo = HALO_IN[level]

    def body(flags, own, other, out):
        slope = gelu_parts(own[...].astype(F32) + other[...].astype(F32))[1]
        at = lax.broadcasted_iota(jnp.int32, slope.shape, 0)
        outside = ((at < halo) & (flags[0] != 0)) | ((at >= halo + rows) & (flags[1] != 0))
        out[...] = jnp.where(outside, 0.0, slope).astype(BF16)

    return pl.pallas_call(
        body,
        grid_spec=pltpu.PrefetchScalarGridSpec(
            num_scalar_prefetch=1, grid=(width // COLS,), in_specs=[blocks, blocks], out_specs=blocks
        ),
        out_shape=jax.ShapeDtypeStruct((count, width), BF16),
        cost_estimate=cost(4e9, 5e6),
        compiler_params=params(),
        name=f"pre_slope_{level}",
    )(flags, own, other)


def top_kernel(
    turned, spread, low, high, vectors, expand, grad, send, matrix, held, kernel, rounded, sems
):
    rows, reach = spread.shape[1], low.shape[1]
    columns = column_blocks(grad.shape[1])
    to_held = lambda k, half: (
        vectors.at[:, half, :, columns[k]],
        held.at[k, half].reshape(vectors.shape[0], vectors.shape[2], COLS),
    )
    batches = []
    for half in range(2):
        batches.append([
            (spread.at[half], matrix.at[half, pl.ds(reach, rows), :]),
            (low.at[(half + turned[0]) % 2], matrix.at[half, pl.ds(0, reach), :]),
            (high.at[(half + turned[1]) % 2], matrix.at[half, pl.ds(reach + rows, reach), :]),
            to_held(0, half),
        ])
    for k in range(1, len(columns)):
        batches.append([to_held(k, half) for half in range(2)])
    batches.append([(expand.at[expand.shape[0] - 1], kernel)])
    arrive = staged(batches, sems)
    for k, cols in enumerate(columns):
        top = None
        for half in range(2):
            if k == 0 or half == 0:
                arrive()
            piece = jnp.dot(matrix[half], held[k, half], preferred_element_type=F32)
            top = piece if top is None else top + piece
        grad[:, cols] = top
        rounded[:, cols] = top.astype(BF16)
    arrive()
    for cols in column_blocks(send.shape[1]):
        send[:, cols] = lax.dot_general(
            rounded[...], kernel[cols, :], NT, preferred_element_type=F32
        ).astype(BF16)


def top_gradient(turned, spread, low, high, vectors, expand):
    _, rows, depth = spread.shape
    count = rows + 2 * low.shape[1]
    share = vectors.shape[1]
    width = expand.shape[1]
    blocks = share // COLS
    vectors = vectors.reshape(depth // SLOTS, 2, SLOTS, share)
    return pl.pallas_call(
        top_kernel,
        in_specs=[SMEM] + [HBM] * 5,
        out_specs=[VMEM, VMEM],
        out_shape=[
            jax.ShapeDtypeStruct((count, share), F32),
            jax.ShapeDtypeStruct((count, width), BF16),
        ],
        scratch_shapes=[
            pltpu.VMEM((2, count, depth), BF16),
            pltpu.VMEM((blocks, 2, depth, COLS), BF16),
            pltpu.VMEM((width, share), BF16),
            pltpu.VMEM((count, share), BF16),
            pltpu.SemaphoreType.DMA((7 + 2 * blocks,)),
        ],
        cost_estimate=cost(5e9, 14e6),
        compiler_params=params(),
        name="top_gradient",
    )(turned, *[in_hbm(a) for a in (spread, low, high, vectors, expand)])


def block_kernel(level, own, other, slope, weight, grad, outer, *rest):
    last = level == 0
    if last:
        out, pre, shifted = rest
    else:
        expand, out, send, pre, shifted = rest
    dilation = BASE_DILATION * 2**level
    count, share = out.shape
    trim = HALO_IN[level] - HALO_IN[level - 1]
    taps = weight.shape[0]
    pre[...] = (own[...].astype(F32) + other[...].astype(F32)) * slope[...].astype(F32)
    for tap in range(taps):
        start = trim - (tap - 1) * dilation
        shifted[tap] = pre[start : start + count, :].astype(BF16)
    middle = None
    for cols in column_blocks(share):
        total = None
        for tap in range(taps):
            part = lax.dot_general(
                shifted[tap], weight[tap, cols, :], NT, preferred_element_type=F32
            )
            total = part if total is None else total + part
        new = grad[trim : trim + count, cols] + total * outer[:, cols].astype(F32)
        if last:
            out[:, cols] = new.astype(BF16)
            continue
        out[:, cols] = new
        part = lax.dot_general(new.astype(BF16), expand[:, cols], NT, preferred_element_type=F32)
        middle = part if middle is None else middle + part
    if not last:
        send[...] = middle.astype(BF16)


def block_step(level, own, other, slope, weight, grad, outer, *expand):
    count_in, width = own.shape
    count, share = outer.shape
    taps = weight.shape[0]
    last = level == 0
    out_shape = [jax.ShapeDtypeStruct((count, share), BF16 if last else F32)]
    if not last:
        out_shape.append(jax.ShapeDtypeStruct((count, width), BF16))
    return pl.pallas_call(
        functools.partial(block_kernel, level),
        in_specs=[VMEM] * (6 + len(expand)),
        out_specs=[VMEM] * len(out_shape),
        out_shape=out_shape,
        scratch_shapes=[
            pltpu.VMEM((count_in, width), F32),
            pltpu.VMEM((taps, count, width), BF16),
        ],
        cost_estimate=cost(5e9, 14e6),
        compiler_params=params(),
        name=f"block_step_{level}",
    )(own, other, slope, weight, grad, outer, *expand)


def after(value, *earlier):
    return lax.optimization_barrier((value, *earlier))[0]


def along_head(vectors, place, first, second):
    count = vectors.shape[0]
    turn = place % 4
    same = lambda steps: [(a * 4 + z, a * 4 + (z - steps) % 4) for a in range(2) for z in range(4)]
    other = lax.ppermute(vectors, "head", [(k, (k + 4) % 8) for k in range(8)])
    both = jnp.concatenate([after(vectors, *first), other], axis=0)
    parts = [lax.ppermute(both, "head", same(k)) for k in (1, 2, 3)]
    parts = [after(both, *second)] + parts
    twice = jnp.concatenate(parts + parts, axis=0)
    return lax.dynamic_slice_in_dim(twice, (4 - turn) % 4 * 2 * count, 8 * count, 0)


def per_device(
    inputs_saved,
    conv_weight,
    expand_weight,
    head_weight,
    batch_of,
    erase_left,
    erase_right,
    bin_gradient,
    cover_bins,
):
    members = lax.axis_size(GROUP_AXES)
    layers, rows, share = inputs_saved.shape
    member = lax.axis_index(GROUP_AXES)
    chan_place = lax.axis_index("chan")
    up = [(k, k + 1) for k in range(members - 1)]
    down = [(k + 1, k) for k in range(members - 1)]
    swap = [(0, 1), (1, 0)]
    levels = list(reversed(range(layers)))

    place = lax.axis_index("head")
    along, turn = place // 4, place % 4
    vectors = head_vectors(
        chan_place[None].astype(jnp.int32), head_weight, batch_of, erase_left, erase_right, share
    )
    first, final = cut_edges(after(inputs_saved, vectors))
    low = lax.ppermute(final, GROUP_AXES, up)
    high = lax.ppermute(first, GROUP_AXES, down)
    payload = bucket(cover_bins, bin_gradient, members, rows)
    flags = jnp.stack([member == 0, member == members - 1]).astype(jnp.int32)
    sends, outers, others = {}, {}, {}

    def begin(n, *earlier):
        sends[n], outers[n] = pre_partial(
            n, inputs_saved, after(low, *earlier), high, conv_weight
        )

    def exchange(n, *earlier):
        others[n] = lax.ppermute(after(sends[n], *earlier), "chan", swap)

    begin(levels[0])
    exchange(levels[0])
    arrived = lax.all_to_all(payload, GROUP_AXES, split_axis=0, concat_axis=0, tiled=True)
    ring = along_head(vectors, place, (payload, first), (sends[levels[0]], arrived))
    gathered = lax.all_gather(ring, "pos", tiled=True)
    begin(levels[1], ring)
    exchange(levels[1])
    reach = HALO_IN[layers - 1]
    spread = spread_entries(
        along[None].astype(jnp.int32), after(arrived, sends[levels[1]]), rows
    )
    spread_low = lax.ppermute(spread[:, rows - reach :], GROUP_AXES, up)
    spread_high = lax.ppermute(spread[:, :reach], GROUP_AXES, down)
    begin(levels[2], spread, others[levels[0]])
    turned = jnp.stack([turn == 0, turn == 3]).astype(jnp.int32)
    gathered = after(gathered, sends[levels[2]], others[levels[1]])
    grad, send = top_gradient(
        turned, spread, spread_low, spread_high, gathered, expand_weight
    )
    for n in levels:
        other = lax.ppermute(send, "chan", swap)
        if n == levels[0]:
            exchange(levels[2], other)
        slope = pre_slope(n, flags, sends[n], after(others[n], send), rows)
        weights = stage_weights(n, after(conv_weight, slope), expand_weight)
        outs = block_step(n, send, other, slope, weights[0], grad, outers[n], *weights[1:])
        if n:
            grad, send = outs
    return outs[0]


def solution(mesh):
    return jax.shard_map(
        per_device,
        mesh=mesh,
        in_specs=(
            P(None, ("pos", "head"), "chan"),
            P(None, None, "chan", None),
            P(None, None, "chan"),
            P(("pos", "head"), None),
            P(("pos", "head")),
            P(),
            P(),
            P(("pos", "head"), None),
            P(("pos", "head"), None),
        ),
        out_specs=P(("pos", "head"), "chan"),
        check_vma=False,
    )
```

```python
import functools

import jax
import jax.numpy as jnp
from jax import lax
from jax.experimental import pallas as pl
from jax.experimental.pallas import tpu as pltpu
from jax.sharding import PartitionSpec as P

BASE_DILATION = 4
RANK = 8
SLOTS = 64
COLS = 256
GROUP_AXES = ("pos", "head")
HALO_IN = {2: 32, 1: 16, 0: 8, -1: 0}
HALO_SAVED = {2: 48, 1: 32, 0: 16}
EDGE_START = {1: 0, 0: 32, 2: 48}
F32 = jnp.float32
BF16 = jnp.bfloat16
NT = (((1,), (1,)), ((), ()))


def cost(flops, bytes_accessed, transcendentals=0):
    return pl.CostEstimate(
        flops=int(flops / 100), bytes_accessed=int(bytes_accessed / 100), transcendentals=0
    )


def params():
    return pltpu.CompilerParams(vmem_limit_bytes=28 * 2**20)


VMEM = pl.BlockSpec(memory_space=pltpu.VMEM)
HBM = pl.BlockSpec(memory_space=pltpu.HBM)
SMEM = pl.BlockSpec(memory_space=pltpu.SMEM)
ROOT_HALF = 0.7071067811865476
DENSITY = 0.3989422804014327


def in_hbm(value):
    return pltpu.with_memory_space_constraint(value, pltpu.HBM)


def fetch(pairs, sems):
    copies = [pltpu.make_async_copy(a, b, sems.at[k]) for k, (a, b) in enumerate(pairs)]
    for copy in copies:
        copy.start()
    return copies


def staged(batches, sems):
    made, k = [], 0
    for batch in batches:
        made.append([pltpu.make_async_copy(a, b, sems.at[k + i]) for i, (a, b) in enumerate(batch)])
        k += len(batch)
    ahead = iter(made)

    def begin():
        for copy in next(ahead, ()):
            copy.start()

    behind = iter(made)

    def arrive():
        for copy in next(behind):
            copy.wait()
        begin()

    begin()
    begin()
    return arrive


def column_blocks(share):
    return [slice(start, start + COLS) for start in range(0, share, COLS)]


def gelu_parts(value):
    half = 0.5 * (1.0 + lax.erf(value * ROOT_HALF))
    return value * half, half + value * jnp.exp(-0.5 * value * value) * DENSITY


def vectors_kernel(place, weight, share, batch, left, right, out):
    projected = lax.dot_general(left[...], weight[...], NT, preferred_element_type=F32)
    column = lax.broadcasted_iota(jnp.int32, projected.shape, 0) // RANK
    kept = jnp.where(column == batch[...], projected, 0.0)
    removed = lax.dot_general(
        kept, right[...].astype(F32), (((0,), (0,)), ((), ())),
        precision=lax.Precision.HIGHEST, preferred_element_type=F32,
    )
    out[...] = (share[...].astype(F32) - removed).astype(BF16)


def head_vectors(place, head_weight, batch_of, erase_left, erase_right, share):
    count, channels = head_weight.shape
    factors = erase_left.shape[1]
    whole = lambda i, place: (0, 0)
    mine = lambda i, place: (0, place[0])
    return pl.pallas_call(
        vectors_kernel,
        grid_spec=pltpu.PrefetchScalarGridSpec(
            num_scalar_prefetch=1,
            grid=(1,),
            in_specs=[
                pl.BlockSpec((count, channels), whole),
                pl.BlockSpec((count, share), mine),
                pl.BlockSpec((1, count), whole),
                pl.BlockSpec((factors, channels), whole),
                pl.BlockSpec((factors, share), mine),
            ],
            out_specs=pl.BlockSpec((count, share), whole),
        ),
        out_shape=jax.ShapeDtypeStruct((count, share), BF16),
        cost_estimate=cost(1e9, 1e6),
        compiler_params=params(),
        name="head_vectors",
    )(place, *[in_hbm(a) for a in (head_weight, head_weight)], batch_of[None, :],
      in_hbm(erase_left.T), in_hbm(erase_right.T))


def bucket_kernel(rows, bins, grads, out):
    cover, experts = bins.shape
    together = 128 // experts
    lanes = together * experts
    chunks = cover // together
    members = out.shape[0]
    before = jnp.where(
        lax.broadcasted_iota(jnp.int32, (lanes, lanes), 0)
        < lax.broadcasted_iota(jnp.int32, (lanes, lanes), 1),
        1.0, 0.0,
    ).astype(BF16)
    index = lax.broadcasted_iota(jnp.int32, (members, lanes), 0)
    slot = lax.broadcasted_iota(jnp.int32, (SLOTS, lanes), 0)
    expert = lax.broadcasted_iota(jnp.int32, (1, lanes), 1) % experts
    side = lambda ref, chunk: jnp.concatenate(
        [ref[chunk * together + k : chunk * together + k + 1, :] for k in range(together)], axis=1
    )
    base = jnp.zeros((members, 1), F32)
    total = jnp.zeros(out.shape, F32)
    grads = grads[...].astype(F32)
    for chunk in range(chunks):
        place = side(bins, chunk)
        target = place // rows
        offset = place - target * rows
        mine = jnp.where(target == index, 1.0, 0.0)
        mine_low = mine.astype(BF16)
        earlier = jnp.dot(mine_low, before, preferred_element_type=F32) + base
        rank = jnp.sum(mine * earlier, axis=0, keepdims=True).astype(jnp.int32)
        base = base + jnp.sum(mine, axis=1, keepdims=True)
        high = offset // 256
        low = (offset - high * 256).astype(F32)
        code = (expert + high * SLOTS).astype(F32)
        hit = rank == slot
        spread = jnp.concatenate(
            [jnp.where(hit, v, 0.0) for v in (low, code, side(grads, chunk))]
            + [jnp.zeros(hit.shape, F32)],
            axis=0,
        ).astype(BF16)
        total = total + lax.dot_general(mine_low, spread, NT, preferred_element_type=F32)
    out[...] = total.astype(BF16)


def bucket(cover_bins, bin_gradient, members, rows):
    return pl.pallas_call(
        functools.partial(bucket_kernel, rows),
        in_specs=[VMEM, VMEM],
        out_shape=jax.ShapeDtypeStruct((members, 4 * SLOTS), BF16),
        cost_estimate=cost(1e8, 1e5),
        compiler_params=params(),
        name="bucket_entries",
    )(cover_bins.T, bin_gradient.T)


def spread_kernel(rows, along, arrived, out, fields):
    half, group = pl.program_id(0), pl.program_id(1)
    together = COLS // SLOTS

    @pl.when((half == 0) & (group == 0))
    def _():
        members = arrived.shape[0]
        repeat = jnp.where(
            lax.broadcasted_iota(jnp.int32, (SLOTS, COLS), 1) % SLOTS
            == lax.broadcasted_iota(jnp.int32, (SLOTS, COLS), 0),
            1.0, 0.0,
        ).astype(BF16)
        own = (
            lax.broadcasted_iota(jnp.int32, (members, COLS), 1) // SLOTS
            == lax.broadcasted_iota(jnp.int32, (members, COLS), 0) % together
        )
        shape = (members // together, members)
        same = jnp.where(
            lax.broadcasted_iota(jnp.int32, shape, 1) // together
            == lax.broadcasted_iota(jnp.int32, shape, 0),
            1.0, 0.0,
        ).astype(BF16)
        for k in range(3):
            wide = jnp.dot(
                arrived[:, k * SLOTS : (k + 1) * SLOTS], repeat, preferred_element_type=F32
            )
            wide = jnp.where(own, wide, 0.0).astype(BF16)
            fields[:, k * COLS : (k + 1) * COLS] = jnp.dot(
                same, wide, preferred_element_type=F32
            )

    row = fields[pl.ds(group * 2 + (half + along[0]) % 2, 1), :]
    low = row[:, :COLS]
    code = row[:, COLS : 2 * COLS]
    value = row[:, 2 * COLS :]
    high = code >= SLOTS
    offset = (low + jnp.where(high, 256.0, 0.0)).astype(jnp.int32)
    slot = lax.broadcasted_iota(jnp.int32, code.shape, 1)
    column = (code - jnp.where(high, 1.0 * SLOTS, 0.0)).astype(jnp.int32) + slot // SLOTS * SLOTS
    width = out.shape[1]
    at_row = jnp.where(
        lax.broadcasted_iota(jnp.int32, (rows, width), 0) == offset, 1.0, 0.0
    ).astype(BF16)
    at_column = jnp.where(
        lax.broadcasted_iota(jnp.int32, (width, width), 0) == column, value, 0.0
    ).astype(BF16)
    out[...] = lax.dot_general(
        at_row, at_column, NT, preferred_element_type=F32
    ).astype(BF16)


def spread_entries(along, arrived, rows):
    groups = arrived.shape[0] * SLOTS // COLS // 2
    return pl.pallas_call(
        functools.partial(spread_kernel, rows),
        grid_spec=pltpu.PrefetchScalarGridSpec(
            num_scalar_prefetch=1,
            grid=(2, groups),
            in_specs=[pl.BlockSpec(arrived.shape, lambda h, i, along: (0, 0))],
            scratch_shapes=[pltpu.VMEM((2 * groups, 3 * COLS), F32)],
            out_specs=pl.BlockSpec((None, rows, COLS), lambda h, i, along: (h, 0, i)),
        ),
        out_shape=jax.ShapeDtypeStruct((2, rows, groups * COLS), BF16),
        cost_estimate=cost(6e9, 8e6),
        compiler_params=params(),
        name="spread_entries",
    )(along, arrived)


def stage_weights(level, weight, expand):
    last = level == 0
    parts = [(weight, level)] + ([] if last else [(expand, level - 1)])

    def body(*refs):
        sems = refs[-1]
        pairs = [(refs[k].at[n], refs[len(parts) + k]) for k, (_, n) in enumerate(parts)]
        for copy in fetch(pairs, sems):
            copy.wait()

    return pl.pallas_call(
        body,
        in_specs=[HBM] * len(parts),
        out_specs=[VMEM] * len(parts),
        out_shape=[jax.ShapeDtypeStruct(a.shape[1:], a.dtype) for a, _ in parts],
        scratch_shapes=[pltpu.SemaphoreType.DMA((len(parts),))],
        cost_estimate=cost(1e9, 1e6),
        compiler_params=params(),
        name=f"stage_weights_{level}",
    )(*[in_hbm(a) for a, _ in parts])


def cut_edges(saved):
    _, rows, share = saved.shape
    count = sum(HALO_SAVED.values())

    def body(saved, first, last, sems):
        pairs = []
        for level, start in EDGE_START.items():
            size = HALO_SAVED[level]
            to = pl.ds(start, size)
            pairs.append((saved.at[level, pl.ds(0, size), :], first.at[to, :]))
            pairs.append((saved.at[level, pl.ds(rows - size, size), :], last.at[to, :]))
        for copy in fetch(pairs, sems):
            copy.wait()

    return pl.pallas_call(
        body,
        in_specs=[HBM],
        out_specs=[VMEM, VMEM],
        out_shape=[jax.ShapeDtypeStruct((count, share), BF16)] * 2,
        scratch_shapes=[pltpu.SemaphoreType.DMA((2 * len(EDGE_START),))],
        cost_estimate=cost(1e6, 6e5),
        compiler_params=params(),
        name="cut_edges",
    )(in_hbm(saved))


def pre_kernel(level, saved, low, high, weight, send, slope, value, act, shifted, kernel, sems):
    dilation = BASE_DILATION * 2**level
    halo, inner = HALO_SAVED[level], HALO_IN[level - 1]
    rows = value.shape[0]
    edge = slice(EDGE_START[level], EDGE_START[level] + halo)
    count = send.shape[0]
    taps = shifted.shape[0]
    columns = column_blocks(send.shape[1])
    batches = [[(saved.at[level], value)], []]
    for k, cols in enumerate(columns):
        batches.append([(weight.at[level, :, :, cols], kernel.at[k])])
    arrive = staged(batches, sems)
    for side, start in ((low, 0), (high, halo + rows)):
        act[start : start + halo, :], outside = gelu_parts(side[edge, :].astype(F32))
        if inner and start:
            slope[inner + rows :, :] = outside[:inner].astype(BF16)
        elif inner:
            slope[:inner, :] = outside[halo - inner :].astype(BF16)
    arrive()
    arrive()
    step = 64

    def part_of(k, _):
        start = pl.multiple_of(k * step, step)
        one, two = gelu_parts(value[pl.ds(start, step), :].astype(F32))
        act[pl.ds(pl.multiple_of(start + halo, 16), step), :] = one
        value[pl.ds(start, step), :] = two.astype(BF16)
        return 0

    lax.fori_loop(0, rows // step, part_of, 0)
    slope[inner : inner + rows, :] = value[...]
    for tap in range(taps):
        start = halo - HALO_IN[level] + (tap - 1) * dilation
        shifted[tap] = act[start : start + count, :].astype(BF16)
    for k, cols in enumerate(columns):
        arrive()
        total = None
        for tap in range(taps):
            part = jnp.dot(shifted[tap], kernel[k, tap], preferred_element_type=F32)
            total = part if total is None else total + part
        send[:, cols] = total.astype(BF16)


def pre_partial(level, saved, low, high, weights):
    rows, share = saved.shape[1:]
    count = rows + 2 * HALO_IN[level]
    halo = HALO_SAVED[level]
    _, taps, _, width = weights.shape
    blocks = width // COLS
    return pl.pallas_call(
        functools.partial(pre_kernel, level),
        in_specs=[HBM, VMEM, VMEM, HBM],
        out_specs=[VMEM, VMEM],
        out_shape=[
            jax.ShapeDtypeStruct((count, width), BF16),
            jax.ShapeDtypeStruct((rows + 2 * HALO_IN[level - 1], share), BF16),
        ],
        scratch_shapes=[
            pltpu.VMEM((rows, share), BF16),
            pltpu.VMEM((rows + 2 * halo, share), F32),
            pltpu.VMEM((taps, count, share), BF16),
            pltpu.VMEM((blocks, taps, share, COLS), BF16),
            pltpu.SemaphoreType.DMA((1 + blocks,)),
        ],
        cost_estimate=cost(5e9, 8e6),
        compiler_params=params(),
        name=f"pre_partial_{level}",
    )(in_hbm(saved), low, high, in_hbm(weights))


def pre_slope(level, flags, own, other, rows):
    count, width = own.shape
    blocks = pl.BlockSpec((count, COLS), lambda i, flags: (0, i))
    halo = HALO_IN[level]

    def body(flags, own, other, out):
        slope = gelu_parts(own[...].astype(F32) + other[...].astype(F32))[1]
        at = lax.broadcasted_iota(jnp.int32, slope.shape, 0)
        outside = ((at < halo) & (flags[0] != 0)) | ((at >= halo + rows) & (flags[1] != 0))
        out[...] = jnp.where(outside, 0.0, slope).astype(BF16)

    return pl.pallas_call(
        body,
        grid_spec=pltpu.PrefetchScalarGridSpec(
            num_scalar_prefetch=1, grid=(width // COLS,), in_specs=[blocks, blocks], out_specs=blocks
        ),
        out_shape=jax.ShapeDtypeStruct((count, width), BF16),
        cost_estimate=cost(4e9, 5e6),
        compiler_params=params(),
        name=f"pre_slope_{level}",
    )(flags, own, other)


def top_kernel(
    turned, spread, low, high, vectors, expand, grad, send, matrix, held, kernel, rounded, sems
):
    rows, reach = spread.shape[1], low.shape[1]
    columns = column_blocks(grad.shape[1])
    to_held = lambda k, half: (
        vectors.at[:, half, :, columns[k]],
        held.at[k, half].reshape(vectors.shape[0], vectors.shape[2], COLS),
    )
    batches = []
    for half in range(2):
        batches.append([
            (spread.at[half], matrix.at[half, pl.ds(reach, rows), :]),
            (low.at[(half + turned[0]) % 2], matrix.at[half, pl.ds(0, reach), :]),
            (high.at[(half + turned[1]) % 2], matrix.at[half, pl.ds(reach + rows, reach), :]),
            to_held(0, half),
        ])
    for k in range(1, len(columns)):
        batches.append([to_held(k, half) for half in range(2)])
    batches.append([(expand.at[expand.shape[0] - 1], kernel)])
    arrive = staged(batches, sems)
    for k, cols in enumerate(columns):
        top = None
        for half in range(2):
            if k == 0 or half == 0:
                arrive()
            piece = jnp.dot(matrix[half], held[k, half], preferred_element_type=F32)
            top = piece if top is None else top + piece
        grad[:, cols] = top
        rounded[:, cols] = top.astype(BF16)
    arrive()
    for cols in column_blocks(send.shape[1]):
        send[:, cols] = lax.dot_general(
            rounded[...], kernel[cols, :], NT, preferred_element_type=F32
        ).astype(BF16)


def top_gradient(turned, spread, low, high, vectors, expand):
    _, rows, depth = spread.shape
    count = rows + 2 * low.shape[1]
    share = vectors.shape[1]
    width = expand.shape[1]
    blocks = share // COLS
    vectors = vectors.reshape(depth // SLOTS, 2, SLOTS, share)
    return pl.pallas_call(
        top_kernel,
        in_specs=[SMEM] + [HBM] * 5,
        out_specs=[VMEM, VMEM],
        out_shape=[
            jax.ShapeDtypeStruct((count, share), F32),
            jax.ShapeDtypeStruct((count, width), BF16),
        ],
        scratch_shapes=[
            pltpu.VMEM((2, count, depth), BF16),
            pltpu.VMEM((blocks, 2, depth, COLS), BF16),
            pltpu.VMEM((width, share), BF16),
            pltpu.VMEM((count, share), BF16),
            pltpu.SemaphoreType.DMA((7 + 2 * blocks,)),
        ],
        cost_estimate=cost(5e9, 14e6),
        compiler_params=params(),
        name="top_gradient",
    )(turned, *[in_hbm(a) for a in (spread, low, high, vectors, expand)])


def block_kernel(level, own, other, slope, weight, grad, outer, *rest):
    last = level == 0
    if last:
        out, pre, shifted = rest
    else:
        expand, out, send, pre, shifted = rest
    dilation = BASE_DILATION * 2**level
    count, share = out.shape
    trim = HALO_IN[level] - HALO_IN[level - 1]
    taps = weight.shape[0]
    pre[...] = (own[...].astype(F32) + other[...].astype(F32)) * slope[...].astype(F32)
    for tap in range(taps):
        start = trim - (tap - 1) * dilation
        shifted[tap] = pre[start : start + count, :].astype(BF16)
    middle = None
    for cols in column_blocks(share):
        total = None
        for tap in range(taps):
            part = lax.dot_general(
                shifted[tap], weight[tap, cols, :], NT, preferred_element_type=F32
            )
            total = part if total is None else total + part
        new = grad[trim : trim + count, cols] + total * outer[:, cols].astype(F32)
        if last:
            out[:, cols] = new.astype(BF16)
            continue
        out[:, cols] = new
        part = lax.dot_general(new.astype(BF16), expand[:, cols], NT, preferred_element_type=F32)
        middle = part if middle is None else middle + part
    if not last:
        send[...] = middle.astype(BF16)


def block_step(level, own, other, slope, weight, grad, outer, *expand):
    count_in, width = own.shape
    count, share = outer.shape
    taps = weight.shape[0]
    last = level == 0
    out_shape = [jax.ShapeDtypeStruct((count, share), BF16 if last else F32)]
    if not last:
        out_shape.append(jax.ShapeDtypeStruct((count, width), BF16))
    return pl.pallas_call(
        functools.partial(block_kernel, level),
        in_specs=[VMEM] * (6 + len(expand)),
        out_specs=[VMEM] * len(out_shape),
        out_shape=out_shape,
        scratch_shapes=[
            pltpu.VMEM((count_in, width), F32),
            pltpu.VMEM((taps, count, width), BF16),
        ],
        cost_estimate=cost(5e9, 14e6),
        compiler_params=params(),
        name=f"block_step_{level}",
    )(own, other, slope, weight, grad, outer, *expand)


def after(value, *earlier):
    return lax.optimization_barrier((value, *earlier))[0]


def along_head(vectors, place, first, second):
    count = vectors.shape[0]
    turn = place % 4
    same = lambda steps: [(a * 4 + z, a * 4 + (z - steps) % 4) for a in range(2) for z in range(4)]
    other = lax.ppermute(vectors, "head", [(k, (k + 4) % 8) for k in range(8)])
    both = jnp.concatenate([after(vectors, *first), other], axis=0)
    parts = [lax.ppermute(both, "head", same(k)) for k in (1, 2, 3)]
    parts = [after(both, *second)] + parts
    twice = jnp.concatenate(parts + parts, axis=0)
    return lax.dynamic_slice_in_dim(twice, (4 - turn) % 4 * 2 * count, 8 * count, 0)


def per_device(
    inputs_saved,
    conv_weight,
    expand_weight,
    head_weight,
    batch_of,
    erase_left,
    erase_right,
    bin_gradient,
    cover_bins,
):
    members = lax.axis_size(GROUP_AXES)
    layers, rows, share = inputs_saved.shape
    member = lax.axis_index(GROUP_AXES)
    chan_place = lax.axis_index("chan")
    up = [(k, k + 1) for k in range(members - 1)]
    down = [(k + 1, k) for k in range(members - 1)]
    swap = [(0, 1), (1, 0)]
    levels = list(reversed(range(layers)))

    place = lax.axis_index("head")
    along, turn = place // 4, place % 4
    vectors = head_vectors(
        chan_place[None].astype(jnp.int32), head_weight, batch_of, erase_left, erase_right, share
    )
    payload = bucket(cover_bins, bin_gradient, members, rows)
    arrived = lax.all_to_all(
        after(payload, vectors), GROUP_AXES, split_axis=0, concat_axis=0, tiled=True
    )
    first, final = cut_edges(after(inputs_saved, payload))
    low = lax.ppermute(final, GROUP_AXES, up)
    high = lax.ppermute(first, GROUP_AXES, down)
    flags = jnp.stack([member == 0, member == members - 1]).astype(jnp.int32)
    sends, outers, others = {}, {}, {}

    def begin(n, *earlier):
        sends[n], outers[n] = pre_partial(
            n, inputs_saved, after(low, *earlier), high, conv_weight
        )

    def exchange(n, *earlier):
        others[n] = lax.ppermute(after(sends[n], *earlier), "chan", swap)

    begin(levels[0])
    exchange(levels[0])
    ring = along_head(vectors, place, (arrived, first), (sends[levels[0]],))
    gathered = lax.all_gather(ring, "pos", tiled=True)
    begin(levels[1], ring)
    exchange(levels[1])
    reach = HALO_IN[layers - 1]
    spread = spread_entries(
        along[None].astype(jnp.int32), after(arrived, sends[levels[1]]), rows
    )
    spread_low = lax.ppermute(spread[:, rows - reach :], GROUP_AXES, up)
    spread_high = lax.ppermute(spread[:, :reach], GROUP_AXES, down)
    begin(levels[2], spread, others[levels[0]])
    turned = jnp.stack([turn == 0, turn == 3]).astype(jnp.int32)
    gathered = after(gathered, sends[levels[2]], others[levels[1]])
    grad, send = top_gradient(
        turned, spread, spread_low, spread_high, gathered, expand_weight
    )
    for n in levels:
        other = lax.ppermute(send, "chan", swap)
        if n == levels[0]:
            exchange(levels[2], other)
        slope = pre_slope(n, flags, sends[n], after(others[n], send), rows)
        weights = stage_weights(n, after(conv_weight, slope), expand_weight)
        outs = block_step(n, send, other, slope, weights[0], grad, outers[n], *weights[1:])
        if n:
            grad, send = outs
    return outs[0]


def solution(mesh):
    return jax.shard_map(
        per_device,
        mesh=mesh,
        in_specs=(
            P(None, ("pos", "head"), "chan"),
            P(None, None, "chan", None),
            P(None, None, "chan"),
            P(("pos", "head"), None),
            P(("pos", "head")),
            P(),
            P(),
            P(("pos", "head"), None),
            P(("pos", "head"), None),
        ),
        out_specs=P(("pos", "head"), "chan"),
        check_vma=False,
    )
```

```python
import functools

import jax
import jax.numpy as jnp
from jax import lax
from jax.experimental import pallas as pl
from jax.experimental.pallas import tpu as pltpu
from jax.sharding import PartitionSpec as P

BASE_DILATION = 4
RANK = 8
SLOTS = 64
COLS = 256
GROUP_AXES = ("pos", "head")
HALO_IN = {2: 32, 1: 16, 0: 8, -1: 0}
HALO_SAVED = {2: 48, 1: 32, 0: 16}
EDGE_START = {1: 0, 0: 32, 2: 48}
F32 = jnp.float32
BF16 = jnp.bfloat16
NT = (((1,), (1,)), ((), ()))


def cost(flops, bytes_accessed, transcendentals=0):
    return pl.CostEstimate(
        flops=int(flops / 100), bytes_accessed=int(bytes_accessed / 100), transcendentals=0
    )


def params():
    return pltpu.CompilerParams(vmem_limit_bytes=28 * 2**20)


VMEM = pl.BlockSpec(memory_space=pltpu.VMEM)
HBM = pl.BlockSpec(memory_space=pltpu.HBM)
SMEM = pl.BlockSpec(memory_space=pltpu.SMEM)
ROOT_HALF = 0.7071067811865476
DENSITY = 0.3989422804014327


def in_hbm(value):
    return pltpu.with_memory_space_constraint(value, pltpu.HBM)


def fetch(pairs, sems):
    copies = [pltpu.make_async_copy(a, b, sems.at[k]) for k, (a, b) in enumerate(pairs)]
    for copy in copies:
        copy.start()
    return copies


def staged(batches, sems):
    made, k = [], 0
    for batch in batches:
        made.append([pltpu.make_async_copy(a, b, sems.at[k + i]) for i, (a, b) in enumerate(batch)])
        k += len(batch)
    ahead = iter(made)

    def begin():
        for copy in next(ahead, ()):
            copy.start()

    behind = iter(made)

    def arrive():
        for copy in next(behind):
            copy.wait()
        begin()

    begin()
    begin()
    return arrive


def column_blocks(share):
    return [slice(start, start + COLS) for start in range(0, share, COLS)]


def gelu_parts(value):
    half = 0.5 * (1.0 + lax.erf(value * ROOT_HALF))
    return value * half, half + value * jnp.exp(-0.5 * value * value) * DENSITY


def vectors_kernel(place, weight, share, batch, left, right, out):
    projected = lax.dot_general(left[...], weight[...], NT, preferred_element_type=F32)
    column = lax.broadcasted_iota(jnp.int32, projected.shape, 0) // RANK
    kept = jnp.where(column == batch[...], projected, 0.0)
    removed = lax.dot_general(
        kept, right[...].astype(F32), (((0,), (0,)), ((), ())),
        precision=lax.Precision.HIGHEST, preferred_element_type=F32,
    )
    out[...] = (share[...].astype(F32) - removed).astype(BF16)


def head_vectors(place, head_weight, batch_of, erase_left, erase_right, share):
    count, channels = head_weight.shape
    factors = erase_left.shape[1]
    whole = lambda i, place: (0, 0)
    mine = lambda i, place: (0, place[0])
    return pl.pallas_call(
        vectors_kernel,
        grid_spec=pltpu.PrefetchScalarGridSpec(
            num_scalar_prefetch=1,
            grid=(1,),
            in_specs=[
                pl.BlockSpec((count, channels), whole),
                pl.BlockSpec((count, share), mine),
                pl.BlockSpec((1, count), whole),
                pl.BlockSpec((factors, channels), whole),
                pl.BlockSpec((factors, share), mine),
            ],
            out_specs=pl.BlockSpec((count, share), whole),
        ),
        out_shape=jax.ShapeDtypeStruct((count, share), BF16),
        cost_estimate=cost(1e9, 1e6),
        compiler_params=params(),
        name="head_vectors",
    )(place, *[in_hbm(a) for a in (head_weight, head_weight)], batch_of[None, :],
      in_hbm(erase_left.T), in_hbm(erase_right.T))


def bucket_kernel(rows, bins, grads, out):
    cover, experts = bins.shape
    together = 128 // experts
    lanes = together * experts
    chunks = cover // together
    members = out.shape[0]
    before = jnp.where(
        lax.broadcasted_iota(jnp.int32, (lanes, lanes), 0)
        < lax.broadcasted_iota(jnp.int32, (lanes, lanes), 1),
        1.0, 0.0,
    ).astype(BF16)
    index = lax.broadcasted_iota(jnp.int32, (members, lanes), 0)
    slot = lax.broadcasted_iota(jnp.int32, (SLOTS, lanes), 0)
    expert = lax.broadcasted_iota(jnp.int32, (1, lanes), 1) % experts
    side = lambda ref, chunk: jnp.concatenate(
        [ref[chunk * together + k : chunk * together + k + 1, :] for k in range(together)], axis=1
    )
    base = jnp.zeros((members, 1), F32)
    total = jnp.zeros(out.shape, F32)
    grads = grads[...].astype(F32)
    for chunk in range(chunks):
        place = side(bins, chunk)
        target = place // rows
        offset = place - target * rows
        mine = jnp.where(target == index, 1.0, 0.0)
        mine_low = mine.astype(BF16)
        earlier = jnp.dot(mine_low, before, preferred_element_type=F32) + base
        rank = jnp.sum(mine * earlier, axis=0, keepdims=True).astype(jnp.int32)
        base = base + jnp.sum(mine, axis=1, keepdims=True)
        high = offset // 256
        low = (offset - high * 256).astype(F32)
        code = (expert + high * SLOTS).astype(F32)
        hit = rank == slot
        spread = jnp.concatenate(
            [jnp.where(hit, v, 0.0) for v in (low, code, side(grads, chunk))]
            + [jnp.zeros(hit.shape, F32)],
            axis=0,
        ).astype(BF16)
        total = total + lax.dot_general(mine_low, spread, NT, preferred_element_type=F32)
    out[...] = total.astype(BF16)


def bucket(cover_bins, bin_gradient, members, rows):
    return pl.pallas_call(
        functools.partial(bucket_kernel, rows),
        in_specs=[VMEM, VMEM],
        out_shape=jax.ShapeDtypeStruct((members, 4 * SLOTS), BF16),
        cost_estimate=cost(1e8, 1e5),
        compiler_params=params(),
        name="bucket_entries",
    )(cover_bins.T, bin_gradient.T)


def spread_kernel(rows, along, arrived, out, fields):
    half, group = pl.program_id(0), pl.program_id(1)
    together = COLS // SLOTS

    @pl.when((half == 0) & (group == 0))
    def _():
        members = arrived.shape[0]
        repeat = jnp.where(
            lax.broadcasted_iota(jnp.int32, (SLOTS, COLS), 1) % SLOTS
            == lax.broadcasted_iota(jnp.int32, (SLOTS, COLS), 0),
            1.0, 0.0,
        ).astype(BF16)
        own = (
            lax.broadcasted_iota(jnp.int32, (members, COLS), 1) // SLOTS
            == lax.broadcasted_iota(jnp.int32, (members, COLS), 0) % together
        )
        shape = (members // together, members)
        same = jnp.where(
            lax.broadcasted_iota(jnp.int32, shape, 1) // together
            == lax.broadcasted_iota(jnp.int32, shape, 0),
            1.0, 0.0,
        ).astype(BF16)
        for k in range(3):
            wide = jnp.dot(
                arrived[:, k * SLOTS : (k + 1) * SLOTS], repeat, preferred_element_type=F32
            )
            wide = jnp.where(own, wide, 0.0).astype(BF16)
            fields[:, k * COLS : (k + 1) * COLS] = jnp.dot(
                same, wide, preferred_element_type=F32
            )

    row = fields[pl.ds(group * 2 + (half + along[0]) % 2, 1), :]
    low = row[:, :COLS]
    code = row[:, COLS : 2 * COLS]
    value = row[:, 2 * COLS :]
    high = code >= SLOTS
    offset = (low + jnp.where(high, 256.0, 0.0)).astype(jnp.int32)
    slot = lax.broadcasted_iota(jnp.int32, code.shape, 1)
    column = (code - jnp.where(high, 1.0 * SLOTS, 0.0)).astype(jnp.int32) + slot // SLOTS * SLOTS
    width = out.shape[1]
    at_row = jnp.where(
        lax.broadcasted_iota(jnp.int32, (rows, width), 0) == offset, 1.0, 0.0
    ).astype(BF16)
    at_column = jnp.where(
        lax.broadcasted_iota(jnp.int32, (width, width), 0) == column, value, 0.0
    ).astype(BF16)
    out[...] = lax.dot_general(
        at_row, at_column, NT, preferred_element_type=F32
    ).astype(BF16)


def spread_entries(along, arrived, rows):
    groups = arrived.shape[0] * SLOTS // COLS // 2
    return pl.pallas_call(
        functools.partial(spread_kernel, rows),
        grid_spec=pltpu.PrefetchScalarGridSpec(
            num_scalar_prefetch=1,
            grid=(2, groups),
            in_specs=[pl.BlockSpec(arrived.shape, lambda h, i, along: (0, 0))],
            scratch_shapes=[pltpu.VMEM((2 * groups, 3 * COLS), F32)],
            out_specs=pl.BlockSpec((None, rows, COLS), lambda h, i, along: (h, 0, i)),
        ),
        out_shape=jax.ShapeDtypeStruct((2, rows, groups * COLS), BF16),
        cost_estimate=cost(6e9, 8e6),
        compiler_params=params(),
        name="spread_entries",
    )(along, arrived)


def stage_weights(level, weight, expand):
    last = level == 0
    parts = [(weight, level)] + ([] if last else [(expand, level - 1)])

    def body(*refs):
        sems = refs[-1]
        pairs = [(refs[k].at[n], refs[len(parts) + k]) for k, (_, n) in enumerate(parts)]
        for copy in fetch(pairs, sems):
            copy.wait()

    return pl.pallas_call(
        body,
        in_specs=[HBM] * len(parts),
        out_specs=[VMEM] * len(parts),
        out_shape=[jax.ShapeDtypeStruct(a.shape[1:], a.dtype) for a, _ in parts],
        scratch_shapes=[pltpu.SemaphoreType.DMA((len(parts),))],
        cost_estimate=cost(1e9, 1e6),
        compiler_params=params(),
        name=f"stage_weights_{level}",
    )(*[in_hbm(a) for a, _ in parts])


def cut_edges(saved):
    _, rows, share = saved.shape
    count = sum(HALO_SAVED.values())

    def body(saved, first, last, sems):
        pairs = []
        for level, start in EDGE_START.items():
            size = HALO_SAVED[level]
            to = pl.ds(start, size)
            pairs.append((saved.at[level, pl.ds(0, size), :], first.at[to, :]))
            pairs.append((saved.at[level, pl.ds(rows - size, size), :], last.at[to, :]))
        for copy in fetch(pairs, sems):
            copy.wait()

    return pl.pallas_call(
        body,
        in_specs=[HBM],
        out_specs=[VMEM, VMEM],
        out_shape=[jax.ShapeDtypeStruct((count, share), BF16)] * 2,
        scratch_shapes=[pltpu.SemaphoreType.DMA((2 * len(EDGE_START),))],
        cost_estimate=cost(1e6, 6e5),
        compiler_params=params(),
        name="cut_edges",
    )(in_hbm(saved))


def pre_kernel(level, saved, low, high, weight, send, slope, value, act, shifted, kernel, sems):
    dilation = BASE_DILATION * 2**level
    halo, inner = HALO_SAVED[level], HALO_IN[level - 1]
    rows = value.shape[0]
    edge = slice(EDGE_START[level], EDGE_START[level] + halo)
    count = send.shape[0]
    taps = shifted.shape[0]
    columns = column_blocks(send.shape[1])
    batches = [[(saved.at[level], value)], []]
    for k, cols in enumerate(columns):
        batches.append([(weight.at[level, :, :, cols], kernel.at[k])])
    arrive = staged(batches, sems)
    for side, start in ((low, 0), (high, halo + rows)):
        act[start : start + halo, :], outside = gelu_parts(side[edge, :].astype(F32))
        if inner and start:
            slope[inner + rows :, :] = outside[:inner].astype(BF16)
        elif inner:
            slope[:inner, :] = outside[halo - inner :].astype(BF16)
    arrive()
    arrive()
    step = 64

    def part_of(k, _):
        start = pl.multiple_of(k * step, step)
        one, two = gelu_parts(value[pl.ds(start, step), :].astype(F32))
        act[pl.ds(pl.multiple_of(start + halo, 16), step), :] = one
        value[pl.ds(start, step), :] = two.astype(BF16)
        return 0

    lax.fori_loop(0, rows // step, part_of, 0)
    slope[inner : inner + rows, :] = value[...]
    for tap in range(taps):
        start = halo - HALO_IN[level] + (tap - 1) * dilation
        shifted[tap] = act[start : start + count, :].astype(BF16)
    for k, cols in enumerate(columns):
        arrive()
        total = None
        for tap in range(taps):
            part = jnp.dot(shifted[tap], kernel[k, tap], preferred_element_type=F32)
            total = part if total is None else total + part
        send[:, cols] = total.astype(BF16)


def pre_partial(level, saved, low, high, weights):
    rows, share = saved.shape[1:]
    count = rows + 2 * HALO_IN[level]
    halo = HALO_SAVED[level]
    _, taps, _, width = weights.shape
    blocks = width // COLS
    return pl.pallas_call(
        functools.partial(pre_kernel, level),
        in_specs=[HBM, VMEM, VMEM, HBM],
        out_specs=[VMEM, VMEM],
        out_shape=[
            jax.ShapeDtypeStruct((count, width), BF16),
            jax.ShapeDtypeStruct((rows + 2 * HALO_IN[level - 1], share), BF16),
        ],
        scratch_shapes=[
            pltpu.VMEM((rows, share), BF16),
            pltpu.VMEM((rows + 2 * halo, share), F32),
            pltpu.VMEM((taps, count, share), BF16),
            pltpu.VMEM((blocks, taps, share, COLS), BF16),
            pltpu.SemaphoreType.DMA((1 + blocks,)),
        ],
        cost_estimate=cost(5e9, 8e6),
        compiler_params=params(),
        name=f"pre_partial_{level}",
    )(in_hbm(saved), low, high, in_hbm(weights))


def pre_slope(level, flags, own, others, rows):
    count, width = own.shape
    blocks = lambda size: pl.BlockSpec((size, COLS), lambda i, flags: (0, i))
    halo = HALO_IN[level]

    def body(flags, own, *refs):
        out = refs[-1]
        start = 0
        for other in refs[:-1]:
            end = start + other.shape[0]
            slope = gelu_parts(own[start:end, :].astype(F32) + other[...].astype(F32))[1]
            at = lax.broadcasted_iota(jnp.int32, slope.shape, 0) + start
            outside = ((at < halo) & (flags[0] != 0)) | ((at >= halo + rows) & (flags[1] != 0))
            out[start:end, :] = jnp.where(outside, 0.0, slope).astype(BF16)
            start = end

    return pl.pallas_call(
        body,
        grid_spec=pltpu.PrefetchScalarGridSpec(
            num_scalar_prefetch=1,
            grid=(width // COLS,),
            in_specs=[blocks(count)] + [blocks(other.shape[0]) for other in others],
            out_specs=blocks(count),
        ),
        out_shape=jax.ShapeDtypeStruct((count, width), BF16),
        cost_estimate=cost(4e9, 5e6),
        compiler_params=params(),
        name=f"pre_slope_{level}",
    )(flags, own, *others)


def top_kernel(
    turned, spread, low, high, vectors, expand, grad, send, matrix, held, kernel, rounded, sems
):
    rows, reach = spread.shape[1], low.shape[1]
    columns = column_blocks(grad.shape[1])
    batches = []
    for half in range(2):
        batches.append([
            (spread.at[half], matrix.at[half, pl.ds(reach, rows), :]),
            (low.at[(half + turned[0]) % 2], matrix.at[half, pl.ds(0, reach), :]),
            (high.at[(half + turned[1]) % 2], matrix.at[half, pl.ds(reach + rows, reach), :]),
            (vectors.at[:, half], held.at[half].reshape(vectors.shape[0], *vectors.shape[2:])),
        ])
    batches.append([(expand.at[expand.shape[0] - 1], kernel)])
    arrive = staged(batches, sems)
    arrive()
    for cols in columns:
        grad[:, cols] = jnp.dot(matrix[0], held[0, :, cols], preferred_element_type=F32)
    arrive()
    for cols in columns:
        top = grad[:, cols] + jnp.dot(
            matrix[1], held[1, :, cols], preferred_element_type=F32
        )
        grad[:, cols] = top
        rounded[:, cols] = top.astype(BF16)
    arrive()
    for cols in column_blocks(send.shape[1]):
        send[:, cols] = lax.dot_general(
            rounded[...], kernel[cols, :], NT, preferred_element_type=F32
        ).astype(BF16)


def top_gradient(turned, spread, low, high, vectors, expand):
    _, rows, depth = spread.shape
    count = rows + 2 * low.shape[1]
    share = vectors.shape[1]
    width = expand.shape[1]
    vectors = vectors.reshape(depth // SLOTS, 2, SLOTS, share)
    return pl.pallas_call(
        top_kernel,
        in_specs=[SMEM] + [HBM] * 5,
        out_specs=[VMEM, VMEM],
        out_shape=[
            jax.ShapeDtypeStruct((count, share), F32),
            jax.ShapeDtypeStruct((count, width), BF16),
        ],
        scratch_shapes=[
            pltpu.VMEM((2, count, depth), BF16),
            pltpu.VMEM((2, depth, share), BF16),
            pltpu.VMEM((width, share), BF16),
            pltpu.VMEM((count, share), BF16),
            pltpu.SemaphoreType.DMA((9,)),
        ],
        cost_estimate=cost(5e9, 14e6),
        compiler_params=params(),
        name="top_gradient",
    )(turned, *[in_hbm(a) for a in (spread, low, high, vectors, expand)])


def block_kernel(level, own, other, slope, weight, grad, outer, *rest):
    last = level == 0
    if last:
        out, pre, shifted = rest
    else:
        expand, out, send, pre, shifted = rest
    dilation = BASE_DILATION * 2**level
    count, share = out.shape
    trim = HALO_IN[level] - HALO_IN[level - 1]
    taps = weight.shape[0]
    pre[...] = (own[...].astype(F32) + other[...].astype(F32)) * slope[...].astype(F32)
    for tap in range(taps):
        start = trim - (tap - 1) * dilation
        shifted[tap] = pre[start : start + count, :].astype(BF16)
    middle = None
    for cols in column_blocks(share):
        total = None
        for tap in range(taps):
            part = lax.dot_general(
                shifted[tap], weight[tap, cols, :], NT, preferred_element_type=F32
            )
            total = part if total is None else total + part
        new = grad[trim : trim + count, cols] + total * outer[:, cols].astype(F32)
        if last:
            out[:, cols] = new.astype(BF16)
            continue
        out[:, cols] = new
        part = lax.dot_general(new.astype(BF16), expand[:, cols], NT, preferred_element_type=F32)
        middle = part if middle is None else middle + part
    if not last:
        send[...] = middle.astype(BF16)


def block_step(level, own, other, slope, weight, grad, outer, *expand):
    count_in, width = own.shape
    count, share = outer.shape
    taps = weight.shape[0]
    last = level == 0
    out_shape = [jax.ShapeDtypeStruct((count, share), BF16 if last else F32)]
    if not last:
        out_shape.append(jax.ShapeDtypeStruct((count, width), BF16))
    return pl.pallas_call(
        functools.partial(block_kernel, level),
        in_specs=[VMEM] * (6 + len(expand)),
        out_specs=[VMEM] * len(out_shape),
        out_shape=out_shape,
        scratch_shapes=[
            pltpu.VMEM((count_in, width), F32),
            pltpu.VMEM((taps, count, width), BF16),
        ],
        cost_estimate=cost(5e9, 14e6),
        compiler_params=params(),
        name=f"block_step_{level}",
    )(own, other, slope, weight, grad, outer, *expand)


def after(value, *earlier):
    return lax.optimization_barrier((value, *earlier))[0]


def along_head(vectors, other, place, first, second):
    count = vectors.shape[0]
    turn = place % 4
    same = lambda steps: [(a * 4 + z, a * 4 + (z - steps) % 4) for a in range(2) for z in range(4)]
    both = jnp.concatenate([after(vectors, *first), other], axis=0)
    parts = [lax.ppermute(both, "head", same(k)) for k in (1, 2, 3)]
    parts = [after(both, *second)] + parts
    twice = jnp.concatenate(parts + parts, axis=0)
    return lax.dynamic_slice_in_dim(twice, (4 - turn) % 4 * 2 * count, 8 * count, 0)


def per_device(
    inputs_saved,
    conv_weight,
    expand_weight,
    head_weight,
    batch_of,
    erase_left,
    erase_right,
    bin_gradient,
    cover_bins,
):
    members = lax.axis_size(GROUP_AXES)
    layers, rows, share = inputs_saved.shape
    member = lax.axis_index(GROUP_AXES)
    chan_place = lax.axis_index("chan")
    up = [(k, k + 1) for k in range(members - 1)]
    down = [(k + 1, k) for k in range(members - 1)]
    swap = [(0, 1), (1, 0)]
    levels = list(reversed(range(layers)))

    place = lax.axis_index("head")
    along, turn = place // 4, place % 4
    first, final = cut_edges(inputs_saved)
    low = lax.ppermute(final, GROUP_AXES, up)
    high = lax.ppermute(first, GROUP_AXES, down)
    vectors = head_vectors(
        chan_place[None].astype(jnp.int32), after(head_weight, first), batch_of, erase_left, erase_right, share
    )
    beside = lax.ppermute(vectors, "head", [(k, (k + 4) % 8) for k in range(8)])
    payload = bucket(after(cover_bins, vectors), bin_gradient, members, rows)
    arrived = lax.all_to_all(
        after(payload, low, high, beside), GROUP_AXES, split_axis=0, concat_axis=0, tiled=True
    )
    flags = jnp.stack([member == 0, member == members - 1]).astype(jnp.int32)
    sends, outers, others = {}, {}, {}

    def begin(n, *earlier):
        sends[n], outers[n] = pre_partial(
            n, inputs_saved, after(low, *earlier), high, conv_weight
        )

    def exchange(n, *earlier):
        others[n] = (lax.ppermute(after(sends[n], *earlier), "chan", swap),)

    begin(levels[0])
    exchange(levels[0])
    begin(levels[1], arrived)
    exchange(levels[1])
    ring = along_head(
        vectors, beside, place, (arrived, sends[levels[0]]), (sends[levels[1]],)
    )
    gathered = lax.all_gather(ring, "pos", tiled=True)
    reach = HALO_IN[layers - 1]
    spread = spread_entries(
        along[None].astype(jnp.int32), after(arrived, ring), rows
    )
    spread_low = lax.ppermute(spread[:, rows - reach :], GROUP_AXES, up)
    spread_high = lax.ppermute(spread[:, :reach], GROUP_AXES, down)
    begin(levels[2], spread, *others[levels[0]])
    parts = sends[levels[2]].shape[0] // 32 * 16
    early = lax.ppermute(sends[levels[2]][:parts], "chan", swap)
    turned = jnp.stack([turn == 0, turn == 3]).astype(jnp.int32)
    gathered = after(gathered, early, *others[levels[1]])
    grad, send = top_gradient(
        turned, spread, spread_low, spread_high, gathered, expand_weight
    )
    for n in levels:
        other = lax.ppermute(send, "chan", swap)
        if n == levels[0]:
            late = after(sends[levels[2]][parts:], other)
            others[levels[2]] = (early, lax.ppermute(late, "chan", swap))
        there = (after(others[n][0], send), *others[n][1:])
        slope = pre_slope(n, flags, sends[n], there, rows)
        ready = (slope, *others[levels[2]]) if n == levels[1] else (slope,)
        weights = stage_weights(n, after(conv_weight, *ready), expand_weight)
        outs = block_step(n, send, other, slope, weights[0], grad, outers[n], *weights[1:])
        if n:
            grad, send = outs
    return outs[0]


def solution(mesh):
    return jax.shard_map(
        per_device,
        mesh=mesh,
        in_specs=(
            P(None, ("pos", "head"), "chan"),
            P(None, None, "chan", None),
            P(None, None, "chan"),
            P(("pos", "head"), None),
            P(("pos", "head")),
            P(),
            P(),
            P(("pos", "head"), None),
            P(("pos", "head"), None),
        ),
        out_specs=P(("pos", "head"), "chan"),
        check_vma=False,
    )
```

```python
import functools

import jax
import jax.numpy as jnp
from jax import lax
from jax.experimental import pallas as pl
from jax.experimental.pallas import tpu as pltpu
from jax.sharding import PartitionSpec as P

BASE_DILATION = 4
RANK = 8
SLOTS = 64
COLS = 256
GROUP_AXES = ("pos", "head")
HALO_IN = {2: 32, 1: 16, 0: 8, -1: 0}
HALO_SAVED = {2: 48, 1: 32, 0: 16}
EDGE_START = {1: 0, 0: 32, 2: 48}
F32 = jnp.float32
BF16 = jnp.bfloat16
NT = (((1,), (1,)), ((), ()))


def cost(flops, bytes_accessed, transcendentals=0):
    return pl.CostEstimate(
        flops=int(flops / 100), bytes_accessed=int(bytes_accessed / 100), transcendentals=0
    )


def params():
    return pltpu.CompilerParams(vmem_limit_bytes=28 * 2**20)


VMEM = pl.BlockSpec(memory_space=pltpu.VMEM)
HBM = pl.BlockSpec(memory_space=pltpu.HBM)
SMEM = pl.BlockSpec(memory_space=pltpu.SMEM)
ROOT_HALF = 0.7071067811865476
DENSITY = 0.3989422804014327


def in_hbm(value):
    return pltpu.with_memory_space_constraint(value, pltpu.HBM)


def fetch(pairs, sems):
    copies = [pltpu.make_async_copy(a, b, sems.at[k]) for k, (a, b) in enumerate(pairs)]
    for copy in copies:
        copy.start()
    return copies


def staged(batches, sems):
    made, k = [], 0
    for batch in batches:
        made.append([pltpu.make_async_copy(a, b, sems.at[k + i]) for i, (a, b) in enumerate(batch)])
        k += len(batch)
    ahead = iter(made)

    def begin():
        for copy in next(ahead, ()):
            copy.start()

    behind = iter(made)

    def arrive():
        for copy in next(behind):
            copy.wait()
        begin()

    begin()
    begin()
    return arrive


def column_blocks(share):
    return [slice(start, start + COLS) for start in range(0, share, COLS)]


def gelu_parts(value):
    half = 0.5 * (1.0 + lax.erf(value * ROOT_HALF))
    return value * half, half + value * jnp.exp(-0.5 * value * value) * DENSITY


def vectors_kernel(place, weight, share, batch, left, right, out):
    projected = lax.dot_general(left[...], weight[...], NT, preferred_element_type=F32)
    column = lax.broadcasted_iota(jnp.int32, projected.shape, 0) // RANK
    kept = jnp.where(column == batch[...], projected, 0.0)
    removed = lax.dot_general(
        kept, right[...].astype(F32), (((0,), (0,)), ((), ())),
        precision=lax.Precision.HIGHEST, preferred_element_type=F32,
    )
    out[...] = (share[...].astype(F32) - removed).astype(BF16)


def head_vectors(place, head_weight, batch_of, erase_left, erase_right, share):
    count, channels = head_weight.shape
    factors = erase_left.shape[1]
    whole = lambda i, place: (0, 0)
    mine = lambda i, place: (0, place[0])
    return pl.pallas_call(
        vectors_kernel,
        grid_spec=pltpu.PrefetchScalarGridSpec(
            num_scalar_prefetch=1,
            grid=(1,),
            in_specs=[
                pl.BlockSpec((count, channels), whole),
                pl.BlockSpec((count, share), mine),
                pl.BlockSpec((1, count), whole),
                pl.BlockSpec((factors, channels), whole),
                pl.BlockSpec((factors, share), mine),
            ],
            out_specs=pl.BlockSpec((count, share), whole),
        ),
        out_shape=jax.ShapeDtypeStruct((count, share), BF16),
        cost_estimate=cost(1e9, 1e6),
        compiler_params=params(),
        name="head_vectors",
    )(place, *[in_hbm(a) for a in (head_weight, head_weight)], batch_of[None, :],
      in_hbm(erase_left.T), in_hbm(erase_right.T))


def bucket_kernel(rows, bins, grads, out):
    cover, experts = bins.shape
    together = 128 // experts
    lanes = together * experts
    chunks = cover // together
    members = out.shape[0]
    before = jnp.where(
        lax.broadcasted_iota(jnp.int32, (lanes, lanes), 0)
        < lax.broadcasted_iota(jnp.int32, (lanes, lanes), 1),
        1.0, 0.0,
    ).astype(BF16)
    index = lax.broadcasted_iota(jnp.int32, (members, lanes), 0)
    slot = lax.broadcasted_iota(jnp.int32, (SLOTS, lanes), 0)
    expert = lax.broadcasted_iota(jnp.int32, (1, lanes), 1) % experts
    side = lambda ref, chunk: jnp.concatenate(
        [ref[chunk * together + k : chunk * together + k + 1, :] for k in range(together)], axis=1
    )
    base = jnp.zeros((members, 1), F32)
    total = jnp.zeros(out.shape, F32)
    grads = grads[...].astype(F32)
    for chunk in range(chunks):
        place = side(bins, chunk)
        target = place // rows
        offset = place - target * rows
        mine = jnp.where(target == index, 1.0, 0.0)
        mine_low = mine.astype(BF16)
        earlier = jnp.dot(mine_low, before, preferred_element_type=F32) + base
        rank = jnp.sum(mine * earlier, axis=0, keepdims=True).astype(jnp.int32)
        base = base + jnp.sum(mine, axis=1, keepdims=True)
        high = offset // 256
        low = (offset - high * 256).astype(F32)
        code = (expert + high * SLOTS).astype(F32)
        hit = rank == slot
        spread = jnp.concatenate(
            [jnp.where(hit, v, 0.0) for v in (low, code, side(grads, chunk))]
            + [jnp.zeros(hit.shape, F32)],
            axis=0,
        ).astype(BF16)
        total = total + lax.dot_general(mine_low, spread, NT, preferred_element_type=F32)
    out[...] = total.astype(BF16)


def bucket(cover_bins, bin_gradient, members, rows):
    return pl.pallas_call(
        functools.partial(bucket_kernel, rows),
        in_specs=[VMEM, VMEM],
        out_shape=jax.ShapeDtypeStruct((members, 4 * SLOTS), BF16),
        cost_estimate=cost(1e8, 1e5),
        compiler_params=params(),
        name="bucket_entries",
    )(cover_bins.T, bin_gradient.T)


def spread_kernel(rows, along, arrived, out, fields):
    half, group = pl.program_id(0), pl.program_id(1)
    together = COLS // SLOTS

    @pl.when((half == 0) & (group == 0))
    def _():
        members = arrived.shape[0]
        repeat = jnp.where(
            lax.broadcasted_iota(jnp.int32, (SLOTS, COLS), 1) % SLOTS
            == lax.broadcasted_iota(jnp.int32, (SLOTS, COLS), 0),
            1.0, 0.0,
        ).astype(BF16)
        own = (
            lax.broadcasted_iota(jnp.int32, (members, COLS), 1) // SLOTS
            == lax.broadcasted_iota(jnp.int32, (members, COLS), 0) % together
        )
        shape = (members // together, members)
        same = jnp.where(
            lax.broadcasted_iota(jnp.int32, shape, 1) // together
            == lax.broadcasted_iota(jnp.int32, shape, 0),
            1.0, 0.0,
        ).astype(BF16)
        for k in range(3):
            wide = jnp.dot(
                arrived[:, k * SLOTS : (k + 1) * SLOTS], repeat, preferred_element_type=F32
            )
            wide = jnp.where(own, wide, 0.0).astype(BF16)
            fields[:, k * COLS : (k + 1) * COLS] = jnp.dot(
                same, wide, preferred_element_type=F32
            )

    row = fields[pl.ds(group * 2 + (half + along[0]) % 2, 1), :]
    low = row[:, :COLS]
    code = row[:, COLS : 2 * COLS]
    value = row[:, 2 * COLS :]
    high = code >= SLOTS
    offset = (low + jnp.where(high, 256.0, 0.0)).astype(jnp.int32)
    slot = lax.broadcasted_iota(jnp.int32, code.shape, 1)
    column = (code - jnp.where(high, 1.0 * SLOTS, 0.0)).astype(jnp.int32) + slot // SLOTS * SLOTS
    width = out.shape[1]
    at_row = jnp.where(
        lax.broadcasted_iota(jnp.int32, (rows, width), 0) == offset, 1.0, 0.0
    ).astype(BF16)
    at_column = jnp.where(
        lax.broadcasted_iota(jnp.int32, (width, width), 0) == column, value, 0.0
    ).astype(BF16)
    out[...] = lax.dot_general(
        at_row, at_column, NT, preferred_element_type=F32
    ).astype(BF16)


def spread_entries(along, arrived, rows):
    groups = arrived.shape[0] * SLOTS // COLS // 2
    return pl.pallas_call(
        functools.partial(spread_kernel, rows),
        grid_spec=pltpu.PrefetchScalarGridSpec(
            num_scalar_prefetch=1,
            grid=(2, groups),
            in_specs=[pl.BlockSpec(arrived.shape, lambda h, i, along: (0, 0))],
            scratch_shapes=[pltpu.VMEM((2 * groups, 3 * COLS), F32)],
            out_specs=pl.BlockSpec((None, rows, COLS), lambda h, i, along: (h, 0, i)),
        ),
        out_shape=jax.ShapeDtypeStruct((2, rows, groups * COLS), BF16),
        cost_estimate=cost(6e9, 8e6),
        compiler_params=params(),
        name="spread_entries",
    )(along, arrived)


def stage_weights(level, weight, expand):
    last = level == 0
    parts = [(weight, level)] + ([] if last else [(expand, level - 1)])

    def body(*refs):
        sems = refs[-1]
        pairs = [(refs[k].at[n], refs[len(parts) + k]) for k, (_, n) in enumerate(parts)]
        for copy in fetch(pairs, sems):
            copy.wait()

    return pl.pallas_call(
        body,
        in_specs=[HBM] * len(parts),
        out_specs=[VMEM] * len(parts),
        out_shape=[jax.ShapeDtypeStruct(a.shape[1:], a.dtype) for a, _ in parts],
        scratch_shapes=[pltpu.SemaphoreType.DMA((len(parts),))],
        cost_estimate=cost(1e9, 1e6),
        compiler_params=params(),
        name=f"stage_weights_{level}",
    )(*[in_hbm(a) for a, _ in parts])


def cut_edges(saved):
    _, rows, share = saved.shape
    count = sum(HALO_SAVED.values())

    def body(saved, first, last, sems):
        pairs = []
        for level, start in EDGE_START.items():
            size = HALO_SAVED[level]
            to = pl.ds(start, size)
            pairs.append((saved.at[level, pl.ds(0, size), :], first.at[to, :]))
            pairs.append((saved.at[level, pl.ds(rows - size, size), :], last.at[to, :]))
        for copy in fetch(pairs, sems):
            copy.wait()

    return pl.pallas_call(
        body,
        in_specs=[HBM],
        out_specs=[VMEM, VMEM],
        out_shape=[jax.ShapeDtypeStruct((count, share), BF16)] * 2,
        scratch_shapes=[pltpu.SemaphoreType.DMA((2 * len(EDGE_START),))],
        cost_estimate=cost(1e6, 6e5),
        compiler_params=params(),
        name="cut_edges",
    )(in_hbm(saved))


def pre_kernel(level, saved, low, high, weight, send, slope, value, act, shifted, kernel, sems):
    dilation = BASE_DILATION * 2**level
    halo, inner = HALO_SAVED[level], HALO_IN[level - 1]
    rows = value.shape[0]
    edge = slice(EDGE_START[level], EDGE_START[level] + halo)
    count = send.shape[0]
    taps = shifted.shape[0]
    columns = column_blocks(send.shape[1])
    batches = [[(saved.at[level], value)], []]
    for k, cols in enumerate(columns):
        batches.append([(weight.at[level, :, :, cols], kernel.at[k])])
    arrive = staged(batches, sems)
    for side, start in ((low, 0), (high, halo + rows)):
        act[start : start + halo, :], outside = gelu_parts(side[edge, :].astype(F32))
        if inner and start:
            slope[inner + rows :, :] = outside[:inner].astype(BF16)
        elif inner:
            slope[:inner, :] = outside[halo - inner :].astype(BF16)
    arrive()
    arrive()
    step = 64

    def part_of(k, _):
        start = pl.multiple_of(k * step, step)
        one, two = gelu_parts(value[pl.ds(start, step), :].astype(F32))
        act[pl.ds(pl.multiple_of(start + halo, 16), step), :] = one
        value[pl.ds(start, step), :] = two.astype(BF16)
        return 0

    lax.fori_loop(0, rows // step, part_of, 0)
    slope[inner : inner + rows, :] = value[...]
    for tap in range(taps):
        start = halo - HALO_IN[level] + (tap - 1) * dilation
        shifted[tap] = act[start : start + count, :].astype(BF16)
    for k, cols in enumerate(columns):
        arrive()
        total = None
        for tap in range(taps):
            part = jnp.dot(shifted[tap], kernel[k, tap], preferred_element_type=F32)
            total = part if total is None else total + part
        send[:, cols] = total.astype(BF16)


def pre_partial(level, saved, low, high, weights):
    rows, share = saved.shape[1:]
    count = rows + 2 * HALO_IN[level]
    halo = HALO_SAVED[level]
    _, taps, _, width = weights.shape
    blocks = width // COLS
    return pl.pallas_call(
        functools.partial(pre_kernel, level),
        in_specs=[HBM, VMEM, VMEM, HBM],
        out_specs=[VMEM, VMEM],
        out_shape=[
            jax.ShapeDtypeStruct((count, width), BF16),
            jax.ShapeDtypeStruct((rows + 2 * HALO_IN[level - 1], share), BF16),
        ],
        scratch_shapes=[
            pltpu.VMEM((rows, share), BF16),
            pltpu.VMEM((rows + 2 * halo, share), F32),
            pltpu.VMEM((taps, count, share), BF16),
            pltpu.VMEM((blocks, taps, share, COLS), BF16),
            pltpu.SemaphoreType.DMA((1 + blocks,)),
        ],
        cost_estimate=cost(5e9, 8e6),
        compiler_params=params(),
        name=f"pre_partial_{level}",
    )(in_hbm(saved), low, high, in_hbm(weights))


def pre_slope(level, flags, own, other, rows):
    count, width = own.shape
    blocks = pl.BlockSpec((count, COLS), lambda i, flags: (0, i))
    halo = HALO_IN[level]

    def body(flags, own, other, out):
        slope = gelu_parts(own[...].astype(F32) + other[...].astype(F32))[1]
        at = lax.broadcasted_iota(jnp.int32, slope.shape, 0)
        outside = ((at < halo) & (flags[0] != 0)) | ((at >= halo + rows) & (flags[1] != 0))
        out[...] = jnp.where(outside, 0.0, slope).astype(BF16)

    return pl.pallas_call(
        body,
        grid_spec=pltpu.PrefetchScalarGridSpec(
            num_scalar_prefetch=1, grid=(width // COLS,), in_specs=[blocks, blocks], out_specs=blocks
        ),
        out_shape=jax.ShapeDtypeStruct((count, width), BF16),
        cost_estimate=cost(4e9, 5e6),
        compiler_params=params(),
        name=f"pre_slope_{level}",
    )(flags, own, other)


def top_kernel(
    turned, spread, low, high, vectors, expand, grad, send, matrix, held, kernel, rounded, sems
):
    rows, reach = spread.shape[1], low.shape[1]
    columns = column_blocks(grad.shape[1])
    batches = []
    for half in range(2):
        batches.append([
            (spread.at[half], matrix.at[half, pl.ds(reach, rows), :]),
            (low.at[(half + turned[0]) % 2], matrix.at[half, pl.ds(0, reach), :]),
            (high.at[(half + turned[1]) % 2], matrix.at[half, pl.ds(reach + rows, reach), :]),
            (vectors.at[:, half], held.at[half].reshape(vectors.shape[0], *vectors.shape[2:])),
        ])
    batches.append([(expand.at[expand.shape[0] - 1], kernel)])
    arrive = staged(batches, sems)
    arrive()
    for cols in columns:
        grad[:, cols] = jnp.dot(matrix[0], held[0, :, cols], preferred_element_type=F32)
    arrive()
    for cols in columns:
        top = grad[:, cols] + jnp.dot(
            matrix[1], held[1, :, cols], preferred_element_type=F32
        )
        grad[:, cols] = top
        rounded[:, cols] = top.astype(BF16)
    arrive()
    for cols in column_blocks(send.shape[1]):
        send[:, cols] = lax.dot_general(
            rounded[...], kernel[cols, :], NT, preferred_element_type=F32
        ).astype(BF16)


def top_gradient(turned, spread, low, high, vectors, expand):
    _, rows, depth = spread.shape
    count = rows + 2 * low.shape[1]
    share = vectors.shape[1]
    width = expand.shape[1]
    vectors = vectors.reshape(depth // SLOTS, 2, SLOTS, share)
    return pl.pallas_call(
        top_kernel,
        in_specs=[SMEM] + [HBM] * 5,
        out_specs=[VMEM, VMEM],
        out_shape=[
            jax.ShapeDtypeStruct((count, share), F32),
            jax.ShapeDtypeStruct((count, width), BF16),
        ],
        scratch_shapes=[
            pltpu.VMEM((2, count, depth), BF16),
            pltpu.VMEM((2, depth, share), BF16),
            pltpu.VMEM((width, share), BF16),
            pltpu.VMEM((count, share), BF16),
            pltpu.SemaphoreType.DMA((9,)),
        ],
        cost_estimate=cost(5e9, 14e6),
        compiler_params=params(),
        name="top_gradient",
    )(turned, *[in_hbm(a) for a in (spread, low, high, vectors, expand)])


def block_kernel(level, own, other, slope, weight, grad, outer, *rest):
    last = level == 0
    if last:
        out, pre, shifted = rest
    else:
        expand, out, send, pre, shifted = rest
    dilation = BASE_DILATION * 2**level
    count, share = out.shape
    trim = HALO_IN[level] - HALO_IN[level - 1]
    taps = weight.shape[0]
    pre[...] = (own[...].astype(F32) + other[...].astype(F32)) * slope[...].astype(F32)
    for tap in range(taps):
        start = trim - (tap - 1) * dilation
        shifted[tap] = pre[start : start + count, :].astype(BF16)
    middle = None
    for cols in column_blocks(share):
        total = None
        for tap in range(taps):
            part = lax.dot_general(
                shifted[tap], weight[tap, cols, :], NT, preferred_element_type=F32
            )
            total = part if total is None else total + part
        new = grad[trim : trim + count, cols] + total * outer[:, cols].astype(F32)
        if last:
            out[:, cols] = new.astype(BF16)
            continue
        out[:, cols] = new
        part = lax.dot_general(new.astype(BF16), expand[:, cols], NT, preferred_element_type=F32)
        middle = part if middle is None else middle + part
    if not last:
        send[...] = middle.astype(BF16)


def block_step(level, own, other, slope, weight, grad, outer, *expand):
    count_in, width = own.shape
    count, share = outer.shape
    taps = weight.shape[0]
    last = level == 0
    out_shape = [jax.ShapeDtypeStruct((count, share), BF16 if last else F32)]
    if not last:
        out_shape.append(jax.ShapeDtypeStruct((count, width), BF16))
    return pl.pallas_call(
        functools.partial(block_kernel, level),
        in_specs=[VMEM] * (6 + len(expand)),
        out_specs=[VMEM] * len(out_shape),
        out_shape=out_shape,
        scratch_shapes=[
            pltpu.VMEM((count_in, width), F32),
            pltpu.VMEM((taps, count, width), BF16),
        ],
        cost_estimate=cost(5e9, 14e6),
        compiler_params=params(),
        name=f"block_step_{level}",
    )(own, other, slope, weight, grad, outer, *expand)


def after(value, *earlier):
    return lax.optimization_barrier((value, *earlier))[0]


def along_head(vectors, place, first, second):
    count = vectors.shape[0]
    turn = place % 4
    same = lambda steps: [(a * 4 + z, a * 4 + (z - steps) % 4) for a in range(2) for z in range(4)]
    other = lax.ppermute(vectors, "head", [(k, (k + 4) % 8) for k in range(8)])
    both = jnp.concatenate([after(vectors, *first), other], axis=0)
    parts = [lax.ppermute(both, "head", same(k)) for k in (1, 2, 3)]
    parts = [after(both, *second)] + parts
    twice = jnp.concatenate(parts + parts, axis=0)
    return lax.dynamic_slice_in_dim(twice, (4 - turn) % 4 * 2 * count, 8 * count, 0)


def per_device(
    inputs_saved,
    conv_weight,
    expand_weight,
    head_weight,
    batch_of,
    erase_left,
    erase_right,
    bin_gradient,
    cover_bins,
):
    members = lax.axis_size(GROUP_AXES)
    layers, rows, share = inputs_saved.shape
    member = lax.axis_index(GROUP_AXES)
    chan_place = lax.axis_index("chan")
    up = [(k, k + 1) for k in range(members - 1)]
    down = [(k + 1, k) for k in range(members - 1)]
    swap = [(0, 1), (1, 0)]
    levels = list(reversed(range(layers)))

    place = lax.axis_index("head")
    along, turn = place // 4, place % 4
    vectors = head_vectors(
        chan_place[None].astype(jnp.int32), head_weight, batch_of, erase_left, erase_right, share
    )
    payload = bucket(cover_bins, bin_gradient, members, rows)
    arrived = lax.all_to_all(
        after(payload, vectors), GROUP_AXES, split_axis=0, concat_axis=0, tiled=True
    )
    first, final = cut_edges(after(inputs_saved, payload))
    low = lax.ppermute(final, GROUP_AXES, up)
    high = lax.ppermute(first, GROUP_AXES, down)
    flags = jnp.stack([member == 0, member == members - 1]).astype(jnp.int32)
    sends, outers, others = {}, {}, {}

    def begin(n, *earlier):
        sends[n], outers[n] = pre_partial(
            n, inputs_saved, after(low, *earlier), high, conv_weight
        )

    def exchange(n, *earlier):
        others[n] = lax.ppermute(after(sends[n], *earlier), "chan", swap)

    begin(levels[0])
    exchange(levels[0])
    ring = along_head(vectors, place, (arrived, first), (sends[levels[0]],))
    gathered = lax.all_gather(ring, "pos", tiled=True)
    begin(levels[1], ring)
    exchange(levels[1])
    reach = HALO_IN[layers - 1]
    spread = spread_entries(
        along[None].astype(jnp.int32), after(arrived, sends[levels[1]]), rows
    )
    spread_low = lax.ppermute(spread[:, rows - reach :], GROUP_AXES, up)
    spread_high = lax.ppermute(spread[:, :reach], GROUP_AXES, down)
    begin(levels[2], spread, others[levels[0]])
    turned = jnp.stack([turn == 0, turn == 3]).astype(jnp.int32)
    gathered = after(gathered, sends[levels[2]], others[levels[1]])
    grad, send = top_gradient(
        turned, spread, spread_low, spread_high, gathered, expand_weight
    )
    exchange(levels[2])
    send = after(send, others[levels[2]])
    for n in levels:
        other = lax.ppermute(send, "chan", swap)
        slope = pre_slope(n, flags, sends[n], after(others[n], send), rows)
        weights = stage_weights(n, after(conv_weight, slope), expand_weight)
        outs = block_step(n, send, other, slope, weights[0], grad, outers[n], *weights[1:])
        if n:
            grad, send = outs
    return outs[0]


def solution(mesh):
    return jax.shard_map(
        per_device,
        mesh=mesh,
        in_specs=(
            P(None, ("pos", "head"), "chan"),
            P(None, None, "chan", None),
            P(None, None, "chan"),
            P(("pos", "head"), None),
            P(("pos", "head")),
            P(),
            P(),
            P(("pos", "head"), None),
            P(("pos", "head"), None),
        ),
        out_specs=P(("pos", "head"), "chan"),
        check_vma=False,
    )
```

```python
import functools

import jax
import jax.numpy as jnp
from jax import lax
from jax.experimental import pallas as pl
from jax.experimental.pallas import tpu as pltpu
from jax.sharding import PartitionSpec as P

BASE_DILATION = 4
RANK = 8
SLOTS = 64
COLS = 256
GROUP_AXES = ("pos", "head")
HALO_IN = {2: 32, 1: 16, 0: 8, -1: 0}
HALO_SAVED = {2: 48, 1: 32, 0: 16}
EDGE_START = {1: 0, 0: 32, 2: 48}
F32 = jnp.float32
BF16 = jnp.bfloat16
NT = (((1,), (1,)), ((), ()))


def cost(flops, bytes_accessed, transcendentals=0):
    return pl.CostEstimate(
        flops=int(flops / 100), bytes_accessed=int(bytes_accessed / 100), transcendentals=0
    )


def params():
    return pltpu.CompilerParams(vmem_limit_bytes=28 * 2**20)


VMEM = pl.BlockSpec(memory_space=pltpu.VMEM)
HBM = pl.BlockSpec(memory_space=pltpu.HBM)
SMEM = pl.BlockSpec(memory_space=pltpu.SMEM)
ROOT_HALF = 0.7071067811865476
DENSITY = 0.3989422804014327


def in_hbm(value):
    return pltpu.with_memory_space_constraint(value, pltpu.HBM)


def fetch(pairs, sems):
    copies = [pltpu.make_async_copy(a, b, sems.at[k]) for k, (a, b) in enumerate(pairs)]
    for copy in copies:
        copy.start()
    return copies


def staged(batches, sems):
    made, k = [], 0
    for batch in batches:
        made.append([pltpu.make_async_copy(a, b, sems.at[k + i]) for i, (a, b) in enumerate(batch)])
        k += len(batch)
    ahead = iter(made)

    def begin():
        for copy in next(ahead, ()):
            copy.start()

    behind = iter(made)

    def arrive():
        for copy in next(behind):
            copy.wait()
        begin()

    begin()
    begin()
    return arrive


def column_blocks(share):
    return [slice(start, start + COLS) for start in range(0, share, COLS)]


def gelu_parts(value):
    half = 0.5 * (1.0 + lax.erf(value * ROOT_HALF))
    return value * half, half + value * jnp.exp(-0.5 * value * value) * DENSITY


def vectors_kernel(place, weight, share, batch, left, right, out):
    projected = lax.dot_general(left[...], weight[...], NT, preferred_element_type=F32)
    column = lax.broadcasted_iota(jnp.int32, projected.shape, 0) // RANK
    kept = jnp.where(column == batch[...], projected, 0.0)
    removed = lax.dot_general(
        kept, right[...].astype(F32), (((0,), (0,)), ((), ())),
        precision=lax.Precision.HIGHEST, preferred_element_type=F32,
    )
    out[...] = (share[...].astype(F32) - removed).astype(BF16)


def head_vectors(place, head_weight, batch_of, erase_left, erase_right, share):
    count, channels = head_weight.shape
    factors = erase_left.shape[1]
    whole = lambda i, place: (0, 0)
    mine = lambda i, place: (0, place[0])
    return pl.pallas_call(
        vectors_kernel,
        grid_spec=pltpu.PrefetchScalarGridSpec(
            num_scalar_prefetch=1,
            grid=(1,),
            in_specs=[
                pl.BlockSpec((count, channels), whole),
                pl.BlockSpec((count, share), mine),
                pl.BlockSpec((1, count), whole),
                pl.BlockSpec((factors, channels), whole),
                pl.BlockSpec((factors, share), mine),
            ],
            out_specs=pl.BlockSpec((count, share), whole),
        ),
        out_shape=jax.ShapeDtypeStruct((count, share), BF16),
        cost_estimate=cost(1e9, 1e6),
        compiler_params=params(),
        name="head_vectors",
    )(place, *[in_hbm(a) for a in (head_weight, head_weight)], batch_of[None, :],
      in_hbm(erase_left.T), in_hbm(erase_right.T))


def bucket_kernel(rows, bins, grads, out):
    cover, experts = bins.shape
    together = 128 // experts
    lanes = together * experts
    chunks = cover // together
    members = out.shape[0]
    before = jnp.where(
        lax.broadcasted_iota(jnp.int32, (lanes, lanes), 0)
        < lax.broadcasted_iota(jnp.int32, (lanes, lanes), 1),
        1.0, 0.0,
    ).astype(BF16)
    index = lax.broadcasted_iota(jnp.int32, (members, lanes), 0)
    slot = lax.broadcasted_iota(jnp.int32, (SLOTS, lanes), 0)
    expert = lax.broadcasted_iota(jnp.int32, (1, lanes), 1) % experts
    side = lambda ref, chunk: jnp.concatenate(
        [ref[chunk * together + k : chunk * together + k + 1, :] for k in range(together)], axis=1
    )
    base = jnp.zeros((members, 1), F32)
    total = jnp.zeros(out.shape, F32)
    grads = grads[...].astype(F32)
    for chunk in range(chunks):
        place = side(bins, chunk)
        target = place // rows
        offset = place - target * rows
        mine = jnp.where(target == index, 1.0, 0.0)
        mine_low = mine.astype(BF16)
        earlier = jnp.dot(mine_low, before, preferred_element_type=F32) + base
        rank = jnp.sum(mine * earlier, axis=0, keepdims=True).astype(jnp.int32)
        base = base + jnp.sum(mine, axis=1, keepdims=True)
        high = offset // 256
        low = (offset - high * 256).astype(F32)
        code = (expert + high * SLOTS).astype(F32)
        hit = rank == slot
        spread = jnp.concatenate(
            [jnp.where(hit, v, 0.0) for v in (low, code, side(grads, chunk))]
            + [jnp.zeros(hit.shape, F32)],
            axis=0,
        ).astype(BF16)
        total = total + lax.dot_general(mine_low, spread, NT, preferred_element_type=F32)
    out[...] = total.astype(BF16)


def bucket(cover_bins, bin_gradient, members, rows):
    return pl.pallas_call(
        functools.partial(bucket_kernel, rows),
        in_specs=[VMEM, VMEM],
        out_shape=jax.ShapeDtypeStruct((members, 4 * SLOTS), BF16),
        cost_estimate=cost(1e8, 1e5),
        compiler_params=params(),
        name="bucket_entries",
    )(cover_bins.T, bin_gradient.T)


def spread_kernel(rows, reach, along, *refs):
    arrived, (out, fields) = refs[:3], refs[3:]
    half, group = pl.program_id(0), pl.program_id(1)
    together = COLS // SLOTS
    groups = fields.shape[1]

    @pl.when((half == 0) & (group == 0))
    def _():
        members = arrived[0].shape[0]
        repeat = jnp.where(
            lax.broadcasted_iota(jnp.int32, (SLOTS, COLS), 1) % SLOTS
            == lax.broadcasted_iota(jnp.int32, (SLOTS, COLS), 0),
            1.0, 0.0,
        ).astype(BF16)
        own = (
            lax.broadcasted_iota(jnp.int32, (members, COLS), 1) // SLOTS
            == lax.broadcasted_iota(jnp.int32, (members, COLS), 0) % together
        )
        shape = (groups, members)
        same = jnp.where(
            lax.broadcasted_iota(jnp.int32, shape, 1) // together
            == lax.broadcasted_iota(jnp.int32, shape, 0),
            1.0, 0.0,
        ).astype(BF16)
        for which, payload in enumerate(arrived):
            for k in range(3):
                wide = jnp.dot(
                    payload[:, k * SLOTS : (k + 1) * SLOTS], repeat, preferred_element_type=F32
                )
                wide = jnp.where(own, wide, 0.0).astype(BF16)
                fields[which, :, k * COLS : (k + 1) * COLS] = jnp.dot(
                    same, wide, preferred_element_type=F32
                )

    width = out.shape[1]
    square = lax.broadcasted_iota(jnp.int32, (width, width), 0)
    parts = ((reach, rows, 0), (0, reach, rows - reach), (reach + rows, reach, 0))
    for which, (start, count, first) in enumerate(parts):
        row = fields[which, pl.ds(group * 2 + (half + along[0]) % 2, 1), :]
        low = row[:, :COLS]
        code = row[:, COLS : 2 * COLS]
        value = row[:, 2 * COLS :]
        high = code >= SLOTS
        offset = (low + jnp.where(high, 256.0, 0.0)).astype(jnp.int32) - first
        slot = lax.broadcasted_iota(jnp.int32, code.shape, 1)
        column = (code - jnp.where(high, 1.0 * SLOTS, 0.0)).astype(jnp.int32)
        column = column + slot // SLOTS * SLOTS
        at_row = jnp.where(
            lax.broadcasted_iota(jnp.int32, (count, width), 0) == offset, 1.0, 0.0
        ).astype(BF16)
        at_column = jnp.where(square == column, value, 0.0).astype(BF16)
        out[start : start + count, :] = lax.dot_general(
            at_row, at_column, NT, preferred_element_type=F32
        ).astype(BF16)


def spread_entries(along, arrived, below, above, rows, reach):
    groups = arrived.shape[0] * SLOTS // COLS
    whole = pl.BlockSpec(arrived.shape, lambda h, i, along: (0, 0))
    return pl.pallas_call(
        functools.partial(spread_kernel, rows, reach),
        grid_spec=pltpu.PrefetchScalarGridSpec(
            num_scalar_prefetch=1,
            grid=(2, groups // 2),
            in_specs=[whole] * 3,
            scratch_shapes=[pltpu.VMEM((3, groups, 3 * COLS), F32)],
            out_specs=pl.BlockSpec((None, rows + 2 * reach, COLS), lambda h, i, along: (h, 0, i)),
        ),
        out_shape=jax.ShapeDtypeStruct((2, rows + 2 * reach, groups // 2 * COLS), BF16),
        cost_estimate=cost(6e9, 8e6),
        compiler_params=params(),
        name="spread_entries",
    )(along, arrived, below, above)


def stage_weights(level, weight, expand):
    last = level == 0
    parts = [(weight, level)] + ([] if last else [(expand, level - 1)])

    def body(*refs):
        sems = refs[-1]
        pairs = [(refs[k].at[n], refs[len(parts) + k]) for k, (_, n) in enumerate(parts)]
        for copy in fetch(pairs, sems):
            copy.wait()

    return pl.pallas_call(
        body,
        in_specs=[HBM] * len(parts),
        out_specs=[VMEM] * len(parts),
        out_shape=[jax.ShapeDtypeStruct(a.shape[1:], a.dtype) for a, _ in parts],
        scratch_shapes=[pltpu.SemaphoreType.DMA((len(parts),))],
        cost_estimate=cost(1e9, 1e6),
        compiler_params=params(),
        name=f"stage_weights_{level}",
    )(*[in_hbm(a) for a, _ in parts])


def cut_edges(saved):
    _, rows, share = saved.shape
    count = sum(HALO_SAVED.values())

    def body(saved, first, last, sems):
        pairs = []
        for level, start in EDGE_START.items():
            size = HALO_SAVED[level]
            to = pl.ds(start, size)
            pairs.append((saved.at[level, pl.ds(0, size), :], first.at[to, :]))
            pairs.append((saved.at[level, pl.ds(rows - size, size), :], last.at[to, :]))
        for copy in fetch(pairs, sems):
            copy.wait()

    return pl.pallas_call(
        body,
        in_specs=[HBM],
        out_specs=[VMEM, VMEM],
        out_shape=[jax.ShapeDtypeStruct((count, share), BF16)] * 2,
        scratch_shapes=[pltpu.SemaphoreType.DMA((2 * len(EDGE_START),))],
        cost_estimate=cost(1e6, 6e5),
        compiler_params=params(),
        name="cut_edges",
    )(in_hbm(saved))


def pre_kernel(level, saved, low, high, weight, send, slope, value, act, shifted, kernel, sems):
    dilation = BASE_DILATION * 2**level
    halo, inner = HALO_SAVED[level], HALO_IN[level - 1]
    rows = value.shape[0]
    edge = slice(EDGE_START[level], EDGE_START[level] + halo)
    count = send.shape[0]
    taps = shifted.shape[0]
    columns = column_blocks(send.shape[1])
    batches = [[(saved.at[level], value)], []]
    for k, cols in enumerate(columns):
        batches.append([(weight.at[level, :, :, cols], kernel.at[k])])
    arrive = staged(batches, sems)
    for side, start in ((low, 0), (high, halo + rows)):
        act[start : start + halo, :], outside = gelu_parts(side[edge, :].astype(F32))
        if inner and start:
            slope[inner + rows :, :] = outside[:inner].astype(BF16)
        elif inner:
            slope[:inner, :] = outside[halo - inner :].astype(BF16)
    arrive()
    arrive()
    step = 64

    def part_of(k, _):
        start = pl.multiple_of(k * step, step)
        one, two = gelu_parts(value[pl.ds(start, step), :].astype(F32))
        act[pl.ds(pl.multiple_of(start + halo, 16), step), :] = one
        value[pl.ds(start, step), :] = two.astype(BF16)
        return 0

    lax.fori_loop(0, rows // step, part_of, 0)
    slope[inner : inner + rows, :] = value[...]
    for tap in range(taps):
        start = halo - HALO_IN[level] + (tap - 1) * dilation
        shifted[tap] = act[start : start + count, :].astype(BF16)
    for k, cols in enumerate(columns):
        arrive()
        total = None
        for tap in range(taps):
            part = jnp.dot(shifted[tap], kernel[k, tap], preferred_element_type=F32)
            total = part if total is None else total + part
        send[:, cols] = total.astype(BF16)


def pre_partial(level, saved, low, high, weights):
    rows, share = saved.shape[1:]
    count = rows + 2 * HALO_IN[level]
    halo = HALO_SAVED[level]
    _, taps, _, width = weights.shape
    blocks = width // COLS
    return pl.pallas_call(
        functools.partial(pre_kernel, level),
        in_specs=[HBM, VMEM, VMEM, HBM],
        out_specs=[VMEM, VMEM],
        out_shape=[
            jax.ShapeDtypeStruct((count, width), BF16),
            jax.ShapeDtypeStruct((rows + 2 * HALO_IN[level - 1], share), BF16),
        ],
        scratch_shapes=[
            pltpu.VMEM((rows, share), BF16),
            pltpu.VMEM((rows + 2 * halo, share), F32),
            pltpu.VMEM((taps, count, share), BF16),
            pltpu.VMEM((blocks, taps, share, COLS), BF16),
            pltpu.SemaphoreType.DMA((1 + blocks,)),
        ],
        cost_estimate=cost(5e9, 8e6),
        compiler_params=params(),
        name=f"pre_partial_{level}",
    )(in_hbm(saved), low, high, in_hbm(weights))


def pre_slope(level, flags, own, other, rows):
    count, width = own.shape
    blocks = pl.BlockSpec((count, COLS), lambda i, flags: (0, i))
    halo = HALO_IN[level]

    def body(flags, own, other, out):
        slope = gelu_parts(own[...].astype(F32) + other[...].astype(F32))[1]
        at = lax.broadcasted_iota(jnp.int32, slope.shape, 0)
        outside = ((at < halo) & (flags[0] != 0)) | ((at >= halo + rows) & (flags[1] != 0))
        out[...] = jnp.where(outside, 0.0, slope).astype(BF16)

    return pl.pallas_call(
        body,
        grid_spec=pltpu.PrefetchScalarGridSpec(
            num_scalar_prefetch=1, grid=(width // COLS,), in_specs=[blocks, blocks], out_specs=blocks
        ),
        out_shape=jax.ShapeDtypeStruct((count, width), BF16),
        cost_estimate=cost(4e9, 5e6),
        compiler_params=params(),
        name=f"pre_slope_{level}",
    )(flags, own, other)


def top_kernel(spread, vectors, expand, grad, send, matrix, held, kernel, rounded, sems):
    columns = column_blocks(grad.shape[1])
    batches = []
    for half in range(2):
        batches.append([
            (spread.at[half], matrix.at[half]),
            (vectors.at[:, half], held.at[half].reshape(vectors.shape[0], *vectors.shape[2:])),
        ])
    batches.append([(expand.at[expand.shape[0] - 1], kernel)])
    arrive = staged(batches, sems)
    arrive()
    for cols in columns:
        grad[:, cols] = jnp.dot(matrix[0], held[0, :, cols], preferred_element_type=F32)
    arrive()
    for cols in columns:
        top = grad[:, cols] + jnp.dot(
            matrix[1], held[1, :, cols], preferred_element_type=F32
        )
        grad[:, cols] = top
        rounded[:, cols] = top.astype(BF16)
    arrive()
    for cols in column_blocks(send.shape[1]):
        send[:, cols] = lax.dot_general(
            rounded[...], kernel[cols, :], NT, preferred_element_type=F32
        ).astype(BF16)


def top_gradient(spread, vectors, expand):
    _, count, depth = spread.shape
    share = vectors.shape[1]
    width = expand.shape[1]
    vectors = vectors.reshape(depth // SLOTS, 2, SLOTS, share)
    return pl.pallas_call(
        top_kernel,
        in_specs=[HBM] * 3,
        out_specs=[VMEM, VMEM],
        out_shape=[
            jax.ShapeDtypeStruct((count, share), F32),
            jax.ShapeDtypeStruct((count, width), BF16),
        ],
        scratch_shapes=[
            pltpu.VMEM((2, count, depth), BF16),
            pltpu.VMEM((2, depth, share), BF16),
            pltpu.VMEM((width, share), BF16),
            pltpu.VMEM((count, share), BF16),
            pltpu.SemaphoreType.DMA((5,)),
        ],
        cost_estimate=cost(5e9, 14e6),
        compiler_params=params(),
        name="top_gradient",
    )(*[in_hbm(a) for a in (spread, vectors, expand)])


def block_kernel(level, own, other, slope, weight, grad, outer, *rest):
    last = level == 0
    if last:
        out, pre, shifted = rest
    else:
        expand, out, send, pre, shifted = rest
    dilation = BASE_DILATION * 2**level
    count, share = out.shape
    trim = HALO_IN[level] - HALO_IN[level - 1]
    taps = weight.shape[0]
    pre[...] = (own[...].astype(F32) + other[...].astype(F32)) * slope[...].astype(F32)
    for tap in range(taps):
        start = trim - (tap - 1) * dilation
        shifted[tap] = pre[start : start + count, :].astype(BF16)
    middle = None
    for cols in column_blocks(share):
        total = None
        for tap in range(taps):
            part = lax.dot_general(
                shifted[tap], weight[tap, cols, :], NT, preferred_element_type=F32
            )
            total = part if total is None else total + part
        new = grad[trim : trim + count, cols] + total * outer[:, cols].astype(F32)
        if last:
            out[:, cols] = new.astype(BF16)
            continue
        out[:, cols] = new
        part = lax.dot_general(new.astype(BF16), expand[:, cols], NT, preferred_element_type=F32)
        middle = part if middle is None else middle + part
    if not last:
        send[...] = middle.astype(BF16)


def block_step(level, own, other, slope, weight, grad, outer, *expand):
    count_in, width = own.shape
    count, share = outer.shape
    taps = weight.shape[0]
    last = level == 0
    out_shape = [jax.ShapeDtypeStruct((count, share), BF16 if last else F32)]
    if not last:
        out_shape.append(jax.ShapeDtypeStruct((count, width), BF16))
    return pl.pallas_call(
        functools.partial(block_kernel, level),
        in_specs=[VMEM] * (6 + len(expand)),
        out_specs=[VMEM] * len(out_shape),
        out_shape=out_shape,
        scratch_shapes=[
            pltpu.VMEM((count_in, width), F32),
            pltpu.VMEM((taps, count, width), BF16),
        ],
        cost_estimate=cost(5e9, 14e6),
        compiler_params=params(),
        name=f"block_step_{level}",
    )(own, other, slope, weight, grad, outer, *expand)


def after(value, *earlier):
    return lax.optimization_barrier((value, *earlier))[0]


def along_head(vectors, place, first, second):
    count = vectors.shape[0]
    turn = place % 4
    same = lambda steps: [(a * 4 + z, a * 4 + (z - steps) % 4) for a in range(2) for z in range(4)]
    other = lax.ppermute(vectors, "head", [(k, (k + 4) % 8) for k in range(8)])
    both = jnp.concatenate([after(vectors, *first), other], axis=0)
    parts = [lax.ppermute(both, "head", same(k)) for k in (1, 2, 3)]
    parts = [after(both, *second)] + parts
    twice = jnp.concatenate(parts + parts, axis=0)
    return lax.dynamic_slice_in_dim(twice, (4 - turn) % 4 * 2 * count, 8 * count, 0)


def per_device(
    inputs_saved,
    conv_weight,
    expand_weight,
    head_weight,
    batch_of,
    erase_left,
    erase_right,
    bin_gradient,
    cover_bins,
):
    members = lax.axis_size(GROUP_AXES)
    layers, rows, share = inputs_saved.shape
    member = lax.axis_index(GROUP_AXES)
    chan_place = lax.axis_index("chan")
    up = [(k, k + 1) for k in range(members - 1)]
    down = [(k + 1, k) for k in range(members - 1)]
    swap = [(0, 1), (1, 0)]
    levels = list(reversed(range(layers)))

    place = lax.axis_index("head")
    along = place // 4
    vectors = head_vectors(
        chan_place[None].astype(jnp.int32), head_weight, batch_of, erase_left, erase_right, share
    )
    payload = bucket(cover_bins, bin_gradient, members, rows)
    arrived = lax.all_to_all(
        after(payload, vectors), GROUP_AXES, split_axis=0, concat_axis=0, tiled=True
    )
    first, final = cut_edges(after(inputs_saved, payload))
    low = lax.ppermute(final, GROUP_AXES, up)
    high = lax.ppermute(first, GROUP_AXES, down)
    flags = jnp.stack([member == 0, member == members - 1]).astype(jnp.int32)
    sends, outers, others = {}, {}, {}

    def begin(n, *earlier):
        sends[n], outers[n] = pre_partial(
            n, inputs_saved, after(low, *earlier), high, conv_weight
        )

    def exchange(n, *earlier):
        others[n] = lax.ppermute(after(sends[n], *earlier), "chan", swap)

    begin(levels[0])
    exchange(levels[0])
    ring = along_head(vectors, place, (arrived, first), (sends[levels[0]],))
    gathered = lax.all_gather(ring, "pos", tiled=True)
    begin(levels[1], ring)
    exchange(levels[1])
    reach = HALO_IN[layers - 1]
    passed = after(arrived, ring)
    below = lax.ppermute(passed, GROUP_AXES, up)
    above = lax.ppermute(passed, GROUP_AXES, down)
    spread = spread_entries(
        along[None].astype(jnp.int32), after(arrived, sends[levels[1]]), below, above, rows, reach
    )
    begin(levels[2], spread, others[levels[0]])
    gathered = after(gathered, sends[levels[2]], others[levels[1]])
    grad, send = top_gradient(spread, gathered, expand_weight)
    exchange(levels[2])
    send = after(send, others[levels[2]])
    for n in levels:
        other = lax.ppermute(send, "chan", swap)
        slope = pre_slope(n, flags, sends[n], after(others[n], send), rows)
        weights = stage_weights(n, after(conv_weight, slope), expand_weight)
        outs = block_step(n, send, other, slope, weights[0], grad, outers[n], *weights[1:])
        if n:
            grad, send = outs
    return outs[0]


def solution(mesh):
    return jax.shard_map(
        per_device,
        mesh=mesh,
        in_specs=(
            P(None, ("pos", "head"), "chan"),
            P(None, None, "chan", None),
            P(None, None, "chan"),
            P(("pos", "head"), None),
            P(("pos", "head")),
            P(),
            P(),
            P(("pos", "head"), None),
            P(("pos", "head"), None),
        ),
        out_specs=P(("pos", "head"), "chan"),
        check_vma=False,
    )
```

```python
import functools

import jax
import jax.numpy as jnp
from jax import lax
from jax.experimental import pallas as pl
from jax.experimental.pallas import tpu as pltpu
from jax.sharding import PartitionSpec as P

BASE_DILATION = 4
RANK = 8
SLOTS = 64
COLS = 256
GROUP_AXES = ("pos", "head")
HALO_IN = {2: 32, 1: 16, 0: 8, -1: 0}
HALO_SAVED = {2: 48, 1: 32, 0: 16}
EDGE_START = {1: 0, 0: 32, 2: 48}
F32 = jnp.float32
BF16 = jnp.bfloat16
NT = (((1,), (1,)), ((), ()))


def cost(flops, bytes_accessed, transcendentals=0):
    return pl.CostEstimate(
        flops=int(flops / 100), bytes_accessed=int(bytes_accessed / 100), transcendentals=0
    )


def params():
    return pltpu.CompilerParams(vmem_limit_bytes=28 * 2**20)


VMEM = pl.BlockSpec(memory_space=pltpu.VMEM)
HBM = pl.BlockSpec(memory_space=pltpu.HBM)
SMEM = pl.BlockSpec(memory_space=pltpu.SMEM)
ROOT_HALF = 0.7071067811865476
DENSITY = 0.3989422804014327


def in_hbm(value):
    return pltpu.with_memory_space_constraint(value, pltpu.HBM)


def fetch(pairs, sems):
    copies = [pltpu.make_async_copy(a, b, sems.at[k]) for k, (a, b) in enumerate(pairs)]
    for copy in copies:
        copy.start()
    return copies


def staged(batches, sems):
    made, k = [], 0
    for batch in batches:
        made.append([pltpu.make_async_copy(a, b, sems.at[k + i]) for i, (a, b) in enumerate(batch)])
        k += len(batch)
    ahead = iter(made)

    def begin():
        for copy in next(ahead, ()):
            copy.start()

    behind = iter(made)

    def arrive():
        for copy in next(behind):
            copy.wait()
        begin()

    begin()
    begin()
    return arrive


def column_blocks(share):
    return [slice(start, start + COLS) for start in range(0, share, COLS)]


def gelu_parts(value):
    half = 0.5 * (1.0 + lax.erf(value * ROOT_HALF))
    return value * half, half + value * jnp.exp(-0.5 * value * value) * DENSITY


def vectors_kernel(place, weight, share, batch, left, right, out):
    projected = lax.dot_general(left[...], weight[...], NT, preferred_element_type=F32)
    column = lax.broadcasted_iota(jnp.int32, projected.shape, 0) // RANK
    kept = jnp.where(column == batch[...], projected, 0.0)
    removed = lax.dot_general(
        kept, right[...].astype(F32), (((0,), (0,)), ((), ())),
        precision=lax.Precision.HIGHEST, preferred_element_type=F32,
    )
    out[...] = (share[...].astype(F32) - removed).astype(BF16)


def head_vectors(place, head_weight, batch_of, erase_left, erase_right, share):
    count, channels = head_weight.shape
    factors = erase_left.shape[1]
    whole = lambda i, place: (0, 0)
    mine = lambda i, place: (0, place[0])
    return pl.pallas_call(
        vectors_kernel,
        grid_spec=pltpu.PrefetchScalarGridSpec(
            num_scalar_prefetch=1,
            grid=(1,),
            in_specs=[
                pl.BlockSpec((count, channels), whole),
                pl.BlockSpec((count, share), mine),
                pl.BlockSpec((1, count), whole),
                pl.BlockSpec((factors, channels), whole),
                pl.BlockSpec((factors, share), mine),
            ],
            out_specs=pl.BlockSpec((count, share), whole),
        ),
        out_shape=jax.ShapeDtypeStruct((count, share), BF16),
        cost_estimate=cost(1e9, 1e6),
        compiler_params=params(),
        name="head_vectors",
    )(place, *[in_hbm(a) for a in (head_weight, head_weight, batch_of[None, :])],
      in_hbm(erase_left.T), in_hbm(erase_right.T))


def bucket_kernel(rows, bins_at, grads_at, out, bins, grads, sems):
    for copy in fetch([(bins_at, bins), (grads_at, grads)], sems):
        copy.wait()
    cover, experts = bins.shape
    together = 128 // experts
    lanes = together * experts
    chunks = cover // together
    members = out.shape[0]
    before = jnp.where(
        lax.broadcasted_iota(jnp.int32, (lanes, lanes), 0)
        < lax.broadcasted_iota(jnp.int32, (lanes, lanes), 1),
        1.0, 0.0,
    ).astype(BF16)
    index = lax.broadcasted_iota(jnp.int32, (members, lanes), 0)
    slot = lax.broadcasted_iota(jnp.int32, (SLOTS, lanes), 0)
    expert = lax.broadcasted_iota(jnp.int32, (1, lanes), 1) % experts
    side = lambda ref, chunk: jnp.concatenate(
        [ref[chunk * together + k : chunk * together + k + 1, :] for k in range(together)], axis=1
    )
    base = jnp.zeros((members, 1), F32)
    total = jnp.zeros((members, 4 * SLOTS), F32)
    grads = grads[...].astype(F32)
    for chunk in range(chunks):
        place = side(bins, chunk)
        target = place // rows
        offset = place - target * rows
        mine = jnp.where(target == index, 1.0, 0.0)
        mine_low = mine.astype(BF16)
        earlier = jnp.dot(mine_low, before, preferred_element_type=F32) + base
        rank = jnp.sum(mine * earlier, axis=0, keepdims=True).astype(jnp.int32)
        base = base + jnp.sum(mine, axis=1, keepdims=True)
        high = offset // 256
        low = (offset - high * 256).astype(F32)
        code = (expert + high * SLOTS).astype(F32)
        hit = rank == slot
        spread = jnp.concatenate(
            [jnp.where(hit, v, 0.0) for v in (low, code, side(grads, chunk))]
            + [jnp.zeros(hit.shape, F32)],
            axis=0,
        ).astype(BF16)
        total = total + lax.dot_general(mine_low, spread, NT, preferred_element_type=F32)
    for k in range(out.shape[1]):
        out[:, k, :] = total[:, k * 128 : (k + 1) * 128].astype(BF16)


def bucket(cover_bins, bin_gradient, members, rows):
    bins, grads = cover_bins.T, bin_gradient.T
    return pl.pallas_call(
        functools.partial(bucket_kernel, rows),
        in_specs=[HBM, HBM],
        out_shape=jax.ShapeDtypeStruct((members, 4 * SLOTS // 128, 128), BF16),
        scratch_shapes=[
            pltpu.VMEM(bins.shape, bins.dtype),
            pltpu.VMEM(grads.shape, grads.dtype),
            pltpu.SemaphoreType.DMA((2,)),
        ],
        cost_estimate=cost(1e8, 1e5),
        compiler_params=params(),
        name="bucket_entries",
    )(in_hbm(bins), in_hbm(grads))


def spread_kernel(rows, reach, along, *refs):
    arrived, (out, fields) = refs[:3], refs[3:]
    half, group = pl.program_id(0), pl.program_id(1)
    together = COLS // SLOTS
    groups = fields.shape[1]

    @pl.when((half == 0) & (group == 0))
    def _():
        members = arrived[0].shape[0]
        repeat = jnp.where(
            lax.broadcasted_iota(jnp.int32, (SLOTS, COLS), 1) % SLOTS
            == lax.broadcasted_iota(jnp.int32, (SLOTS, COLS), 0),
            1.0, 0.0,
        ).astype(BF16)
        own = (
            lax.broadcasted_iota(jnp.int32, (members, COLS), 1) // SLOTS
            == lax.broadcasted_iota(jnp.int32, (members, COLS), 0) % together
        )
        shape = (groups, members)
        same = jnp.where(
            lax.broadcasted_iota(jnp.int32, shape, 1) // together
            == lax.broadcasted_iota(jnp.int32, shape, 0),
            1.0, 0.0,
        ).astype(BF16)
        for which, payload in enumerate(arrived):
            for k in range(3):
                first = k % 2 * SLOTS
                these = payload[:, k // 2, first : first + SLOTS]
                wide = jnp.dot(these, repeat, preferred_element_type=F32)
                wide = jnp.where(own, wide, 0.0).astype(BF16)
                fields[which, :, k * COLS : (k + 1) * COLS] = jnp.dot(
                    same, wide, preferred_element_type=F32
                )

    width = out.shape[1]
    square = lax.broadcasted_iota(jnp.int32, (width, width), 0)
    parts = ((reach, rows, 0), (0, reach, rows - reach), (reach + rows, reach, 0))
    for which, (start, count, first) in enumerate(parts):
        row = fields[which, pl.ds(group * 2 + (half + along[0]) % 2, 1), :]
        low = row[:, :COLS]
        code = row[:, COLS : 2 * COLS]
        value = row[:, 2 * COLS :]
        high = code >= SLOTS
        offset = (low + jnp.where(high, 256.0, 0.0)).astype(jnp.int32) - first
        slot = lax.broadcasted_iota(jnp.int32, code.shape, 1)
        column = (code - jnp.where(high, 1.0 * SLOTS, 0.0)).astype(jnp.int32)
        column = column + slot // SLOTS * SLOTS
        at_row = jnp.where(
            lax.broadcasted_iota(jnp.int32, (count, width), 0) == offset, 1.0, 0.0
        ).astype(BF16)
        at_column = jnp.where(square == column, value, 0.0).astype(BF16)
        out[start : start + count, :] = lax.dot_general(
            at_row, at_column, NT, preferred_element_type=F32
        ).astype(BF16)


def spread_entries(along, arrived, below, above, rows, reach):
    groups = arrived.shape[0] * SLOTS // COLS
    whole = pl.BlockSpec(arrived.shape, lambda h, i, along: (0, 0, 0))
    return pl.pallas_call(
        functools.partial(spread_kernel, rows, reach),
        grid_spec=pltpu.PrefetchScalarGridSpec(
            num_scalar_prefetch=1,
            grid=(2, groups // 2),
            in_specs=[whole] * 3,
            scratch_shapes=[pltpu.VMEM((3, groups, 3 * COLS), F32)],
            out_specs=pl.BlockSpec((None, rows + 2 * reach, COLS), lambda h, i, along: (h, 0, i)),
        ),
        out_shape=jax.ShapeDtypeStruct((2, rows + 2 * reach, groups // 2 * COLS), BF16),
        cost_estimate=cost(6e9, 8e6),
        compiler_params=params(),
        name="spread_entries",
    )(along, arrived, below, above)


def stage_weights(level, weight, expand):
    last = level == 0
    parts = [(weight, level)] + ([] if last else [(expand, level - 1)])

    def body(*refs):
        sems = refs[-1]
        pairs = [(refs[k].at[n], refs[len(parts) + k]) for k, (_, n) in enumerate(parts)]
        for copy in fetch(pairs, sems):
            copy.wait()

    return pl.pallas_call(
        body,
        in_specs=[HBM] * len(parts),
        out_specs=[VMEM] * len(parts),
        out_shape=[jax.ShapeDtypeStruct(a.shape[1:], a.dtype) for a, _ in parts],
        scratch_shapes=[pltpu.SemaphoreType.DMA((len(parts),))],
        cost_estimate=cost(1e9, 1e6),
        compiler_params=params(),
        name=f"stage_weights_{level}",
    )(*[in_hbm(a) for a, _ in parts])


def cut_edges(saved):
    _, rows, share = saved.shape
    count = sum(HALO_SAVED.values())

    def body(saved, first, last, sems):
        pairs = []
        for level, start in EDGE_START.items():
            size = HALO_SAVED[level]
            to = pl.ds(start, size)
            pairs.append((saved.at[level, pl.ds(0, size), :], first.at[to, :]))
            pairs.append((saved.at[level, pl.ds(rows - size, size), :], last.at[to, :]))
        for copy in fetch(pairs, sems):
            copy.wait()

    return pl.pallas_call(
        body,
        in_specs=[HBM],
        out_specs=[VMEM, VMEM],
        out_shape=[jax.ShapeDtypeStruct((count, share), BF16)] * 2,
        scratch_shapes=[pltpu.SemaphoreType.DMA((2 * len(EDGE_START),))],
        cost_estimate=cost(1e6, 6e5),
        compiler_params=params(),
        name="cut_edges",
    )(in_hbm(saved))


def pre_kernel(level, saved, low, high, weight, send, slope, value, act, shifted, kernel, sems):
    dilation = BASE_DILATION * 2**level
    halo, inner = HALO_SAVED[level], HALO_IN[level - 1]
    rows = value.shape[0]
    edge = slice(EDGE_START[level], EDGE_START[level] + halo)
    count = send.shape[0]
    taps = shifted.shape[0]
    columns = column_blocks(send.shape[1])
    batches = [[(saved.at[level], value)], []]
    for k, cols in enumerate(columns):
        batches.append([(weight.at[level, :, :, cols], kernel.at[k])])
    arrive = staged(batches, sems)
    for side, start in ((low, 0), (high, halo + rows)):
        act[start : start + halo, :], outside = gelu_parts(side[edge, :].astype(F32))
        if inner and start:
            slope[inner + rows :, :] = outside[:inner].astype(BF16)
        elif inner:
            slope[:inner, :] = outside[halo - inner :].astype(BF16)
    arrive()
    arrive()
    step = 64

    def part_of(k, _):
        start = pl.multiple_of(k * step, step)
        one, two = gelu_parts(value[pl.ds(start, step), :].astype(F32))
        act[pl.ds(pl.multiple_of(start + halo, 16), step), :] = one
        value[pl.ds(start, step), :] = two.astype(BF16)
        return 0

    lax.fori_loop(0, rows // step, part_of, 0)
    slope[inner : inner + rows, :] = value[...]
    for tap in range(taps):
        start = halo - HALO_IN[level] + (tap - 1) * dilation
        shifted[tap] = act[start : start + count, :].astype(BF16)
    for k, cols in enumerate(columns):
        arrive()
        total = None
        for tap in range(taps):
            part = jnp.dot(shifted[tap], kernel[k, tap], preferred_element_type=F32)
            total = part if total is None else total + part
        send[:, cols] = total.astype(BF16)


def pre_partial(level, saved, low, high, weights):
    rows, share = saved.shape[1:]
    count = rows + 2 * HALO_IN[level]
    halo = HALO_SAVED[level]
    _, taps, _, width = weights.shape
    blocks = width // COLS
    return pl.pallas_call(
        functools.partial(pre_kernel, level),
        in_specs=[HBM, VMEM, VMEM, HBM],
        out_specs=[VMEM, VMEM],
        out_shape=[
            jax.ShapeDtypeStruct((count, width), BF16),
            jax.ShapeDtypeStruct((rows + 2 * HALO_IN[level - 1], share), BF16),
        ],
        scratch_shapes=[
            pltpu.VMEM((rows, share), BF16),
            pltpu.VMEM((rows + 2 * halo, share), F32),
            pltpu.VMEM((taps, count, share), BF16),
            pltpu.VMEM((blocks, taps, share, COLS), BF16),
            pltpu.SemaphoreType.DMA((1 + blocks,)),
        ],
        cost_estimate=cost(5e9, 8e6),
        compiler_params=params(),
        name=f"pre_partial_{level}",
    )(in_hbm(saved), low, high, in_hbm(weights))


def pre_slope(level, flags, own, other, rows):
    count, width = own.shape
    blocks = pl.BlockSpec((count, COLS), lambda i, flags: (0, i))
    halo = HALO_IN[level]

    def body(flags, own, other, out):
        slope = gelu_parts(own[...].astype(F32) + other[...].astype(F32))[1]
        at = lax.broadcasted_iota(jnp.int32, slope.shape, 0)
        outside = ((at < halo) & (flags[0] != 0)) | ((at >= halo + rows) & (flags[1] != 0))
        out[...] = jnp.where(outside, 0.0, slope).astype(BF16)

    return pl.pallas_call(
        body,
        grid_spec=pltpu.PrefetchScalarGridSpec(
            num_scalar_prefetch=1, grid=(width // COLS,), in_specs=[blocks, blocks], out_specs=blocks
        ),
        out_shape=jax.ShapeDtypeStruct((count, width), BF16),
        cost_estimate=cost(4e9, 5e6),
        compiler_params=params(),
        name=f"pre_slope_{level}",
    )(flags, own, other)


def top_kernel(spread, vectors, expand, grad, send, matrix, held, kernel, rounded, sems):
    columns = column_blocks(grad.shape[1])
    batches = []
    for half in range(2):
        batches.append([
            (spread.at[half], matrix.at[half]),
            (vectors.at[:, half], held.at[half].reshape(vectors.shape[0], *vectors.shape[2:])),
        ])
    batches.append([(expand.at[expand.shape[0] - 1], kernel)])
    arrive = staged(batches, sems)
    arrive()
    for cols in columns:
        grad[:, cols] = jnp.dot(matrix[0], held[0, :, cols], preferred_element_type=F32)
    arrive()
    for cols in columns:
        top = grad[:, cols] + jnp.dot(
            matrix[1], held[1, :, cols], preferred_element_type=F32
        )
        grad[:, cols] = top
        rounded[:, cols] = top.astype(BF16)
    arrive()
    for cols in column_blocks(send.shape[1]):
        send[:, cols] = lax.dot_general(
            rounded[...], kernel[cols, :], NT, preferred_element_type=F32
        ).astype(BF16)


def top_gradient(spread, vectors, expand):
    _, count, depth = spread.shape
    share = vectors.shape[1]
    width = expand.shape[1]
    vectors = vectors.reshape(depth // SLOTS, 2, SLOTS, share)
    return pl.pallas_call(
        top_kernel,
        in_specs=[HBM] * 3,
        out_specs=[VMEM, VMEM],
        out_shape=[
            jax.ShapeDtypeStruct((count, share), F32),
            jax.ShapeDtypeStruct((count, width), BF16),
        ],
        scratch_shapes=[
            pltpu.VMEM((2, count, depth), BF16),
            pltpu.VMEM((2, depth, share), BF16),
            pltpu.VMEM((width, share), BF16),
            pltpu.VMEM((count, share), BF16),
            pltpu.SemaphoreType.DMA((5,)),
        ],
        cost_estimate=cost(5e9, 14e6),
        compiler_params=params(),
        name="top_gradient",
    )(*[in_hbm(a) for a in (spread, vectors, expand)])


def block_kernel(level, own, other, slope, weight, grad, outer, *rest):
    last = level == 0
    if last:
        out, pre, shifted = rest
    else:
        expand, out, send, pre, shifted = rest
    dilation = BASE_DILATION * 2**level
    count, share = out.shape
    trim = HALO_IN[level] - HALO_IN[level - 1]
    taps = weight.shape[0]
    pre[...] = (own[...].astype(F32) + other[...].astype(F32)) * slope[...].astype(F32)
    for tap in range(taps):
        start = trim - (tap - 1) * dilation
        shifted[tap] = pre[start : start + count, :].astype(BF16)
    middle = None
    for cols in column_blocks(share):
        total = None
        for tap in range(taps):
            part = lax.dot_general(
                shifted[tap], weight[tap, cols, :], NT, preferred_element_type=F32
            )
            total = part if total is None else total + part
        new = grad[trim : trim + count, cols] + total * outer[:, cols].astype(F32)
        if last:
            out[:, cols] = new.astype(BF16)
            continue
        out[:, cols] = new
        part = lax.dot_general(new.astype(BF16), expand[:, cols], NT, preferred_element_type=F32)
        middle = part if middle is None else middle + part
    if not last:
        send[...] = middle.astype(BF16)


def block_step(level, own, other, slope, weight, grad, outer, *expand):
    count_in, width = own.shape
    count, share = outer.shape
    taps = weight.shape[0]
    last = level == 0
    out_shape = [jax.ShapeDtypeStruct((count, share), BF16 if last else F32)]
    if not last:
        out_shape.append(jax.ShapeDtypeStruct((count, width), BF16))
    return pl.pallas_call(
        functools.partial(block_kernel, level),
        in_specs=[VMEM] * (6 + len(expand)),
        out_specs=[VMEM] * len(out_shape),
        out_shape=out_shape,
        scratch_shapes=[
            pltpu.VMEM((count_in, width), F32),
            pltpu.VMEM((taps, count, width), BF16),
        ],
        cost_estimate=cost(5e9, 14e6),
        compiler_params=params(),
        name=f"block_step_{level}",
    )(own, other, slope, weight, grad, outer, *expand)


def after(value, *earlier):
    return lax.optimization_barrier((value, *earlier))[0]


def along_head(vectors, place, first, second):
    count = vectors.shape[0]
    turn = place % 4
    same = lambda steps: [(a * 4 + z, a * 4 + (z - steps) % 4) for a in range(2) for z in range(4)]
    other = lax.ppermute(vectors, "head", [(k, (k + 4) % 8) for k in range(8)])
    both = jnp.concatenate([after(vectors, *first), other], axis=0)
    parts = [lax.ppermute(both, "head", same(k)) for k in (1, 2, 3)]
    parts = [after(both, *second)] + parts
    twice = jnp.concatenate(parts + parts, axis=0)
    return lax.dynamic_slice_in_dim(twice, (4 - turn) % 4 * 2 * count, 8 * count, 0)


def per_device(
    inputs_saved,
    conv_weight,
    expand_weight,
    head_weight,
    batch_of,
    erase_left,
    erase_right,
    bin_gradient,
    cover_bins,
):
    members = lax.axis_size(GROUP_AXES)
    layers, rows, share = inputs_saved.shape
    member = lax.axis_index(GROUP_AXES)
    chan_place = lax.axis_index("chan")
    up = [(k, k + 1) for k in range(members - 1)]
    down = [(k + 1, k) for k in range(members - 1)]
    swap = [(0, 1), (1, 0)]
    levels = list(reversed(range(layers)))

    place = lax.axis_index("head")
    along = place // 4
    vectors = head_vectors(
        chan_place[None].astype(jnp.int32), head_weight, batch_of, erase_left, erase_right, share
    )
    payload = bucket(cover_bins, bin_gradient, members, rows)
    arrived = lax.all_to_all(
        after(payload, vectors), GROUP_AXES, split_axis=0, concat_axis=0, tiled=True
    )
    first, final = cut_edges(after(inputs_saved, payload))
    low = lax.ppermute(final, GROUP_AXES, up)
    high = lax.ppermute(first, GROUP_AXES, down)
    flags = jnp.stack([member == 0, member == members - 1]).astype(jnp.int32)
    sends, outers, others = {}, {}, {}

    def begin(n, *earlier):
        sends[n], outers[n] = pre_partial(
            n, inputs_saved, after(low, *earlier), high, conv_weight
        )

    def exchange(n, *earlier):
        others[n] = lax.ppermute(after(sends[n], *earlier), "chan", swap)

    begin(levels[0])
    exchange(levels[0])
    ring = along_head(vectors, place, (arrived, first), (sends[levels[0]],))
    gathered = lax.all_gather(ring, "pos", tiled=True)
    begin(levels[1], ring)
    exchange(levels[1])
    reach = HALO_IN[layers - 1]
    passed = after(arrived, ring)
    below = lax.ppermute(passed, GROUP_AXES, up)
    above = lax.ppermute(passed, GROUP_AXES, down)
    spread = spread_entries(
        along[None].astype(jnp.int32), after(arrived, sends[levels[1]]), below, above, rows, reach
    )
    begin(levels[2], spread, others[levels[0]])
    gathered = after(gathered, sends[levels[2]], others[levels[1]])
    grad, send = top_gradient(spread, gathered, expand_weight)
    exchange(levels[2])
    send = after(send, others[levels[2]])
    for n in levels:
        other = lax.ppermute(send, "chan", swap)
        slope = pre_slope(n, flags, sends[n], after(others[n], send), rows)
        weights = stage_weights(n, after(conv_weight, slope), expand_weight)
        outs = block_step(n, send, other, slope, weights[0], grad, outers[n], *weights[1:])
        if n:
            grad, send = outs
    return outs[0]


def solution(mesh):
    return jax.shard_map(
        per_device,
        mesh=mesh,
        in_specs=(
            P(None, ("pos", "head"), "chan"),
            P(None, None, "chan", None),
            P(None, None, "chan"),
            P(("pos", "head"), None),
            P(("pos", "head")),
            P(),
            P(),
            P(("pos", "head"), None),
            P(("pos", "head"), None),
        ),
        out_specs=P(("pos", "head"), "chan"),
        check_vma=False,
    )
```

```python
import functools

import jax
import jax.numpy as jnp
from jax import lax
from jax.experimental import pallas as pl
from jax.experimental.pallas import tpu as pltpu
from jax.sharding import PartitionSpec as P

BASE_DILATION = 4
RANK = 8
SLOTS = 64
COLS = 256
GROUP_AXES = ("pos", "head")
HALO_IN = {2: 32, 1: 16, 0: 8, -1: 0}
HALO_SAVED = {2: 48, 1: 32, 0: 16}
EDGE_START = {1: 0, 0: 32, 2: 48}
F32 = jnp.float32
BF16 = jnp.bfloat16
NT = (((1,), (1,)), ((), ()))


def cost(flops, bytes_accessed, transcendentals=0):
    return pl.CostEstimate(
        flops=int(flops / 100), bytes_accessed=int(bytes_accessed / 100), transcendentals=0
    )


def params():
    return pltpu.CompilerParams(vmem_limit_bytes=28 * 2**20)


VMEM = pl.BlockSpec(memory_space=pltpu.VMEM)
HBM = pl.BlockSpec(memory_space=pltpu.HBM)
SMEM = pl.BlockSpec(memory_space=pltpu.SMEM)
ROOT_HALF = 0.7071067811865476
DENSITY = 0.3989422804014327


def in_hbm(value):
    return pltpu.with_memory_space_constraint(value, pltpu.HBM)


def fetch(pairs, sems):
    copies = [pltpu.make_async_copy(a, b, sems.at[k]) for k, (a, b) in enumerate(pairs)]
    for copy in copies:
        copy.start()
    return copies


def staged(batches, sems):
    made, k = [], 0
    for batch in batches:
        made.append([pltpu.make_async_copy(a, b, sems.at[k + i]) for i, (a, b) in enumerate(batch)])
        k += len(batch)
    ahead = iter(made)

    def begin():
        for copy in next(ahead, ()):
            copy.start()

    behind = iter(made)

    def arrive():
        for copy in next(behind):
            copy.wait()
        begin()

    begin()
    begin()
    return arrive


def column_blocks(share):
    return [slice(start, start + COLS) for start in range(0, share, COLS)]


def gelu_parts(value):
    half = 0.5 * (1.0 + lax.erf(value * ROOT_HALF))
    return value * half, half + value * jnp.exp(-0.5 * value * value) * DENSITY


def vectors_kernel(place, weight, share, batch, left, right, out):
    projected = lax.dot_general(left[...], weight[...], NT, preferred_element_type=F32)
    column = lax.broadcasted_iota(jnp.int32, projected.shape, 0) // RANK
    kept = jnp.where(column == batch[...], projected, 0.0)
    removed = lax.dot_general(
        kept, right[...].astype(F32), (((0,), (0,)), ((), ())),
        precision=lax.Precision.HIGHEST, preferred_element_type=F32,
    )
    out[...] = (share[...].astype(F32) - removed).astype(BF16)


def head_vectors(place, head_weight, batch_of, erase_left, erase_right, share):
    count, channels = head_weight.shape
    factors = erase_left.shape[1]
    whole = lambda i, place: (0, 0)
    mine = lambda i, place: (0, place[0])
    return pl.pallas_call(
        vectors_kernel,
        grid_spec=pltpu.PrefetchScalarGridSpec(
            num_scalar_prefetch=1,
            grid=(1,),
            in_specs=[
                pl.BlockSpec((count, channels), whole),
                pl.BlockSpec((count, share), mine),
                pl.BlockSpec((1, count), whole),
                pl.BlockSpec((factors, channels), whole),
                pl.BlockSpec((factors, share), mine),
            ],
            out_specs=pl.BlockSpec((count, share), whole),
        ),
        out_shape=jax.ShapeDtypeStruct((count, share), BF16),
        cost_estimate=cost(1e9, 1e6),
        compiler_params=params(),
        name="head_vectors",
    )(place, *[in_hbm(a) for a in (head_weight, head_weight, batch_of[None, :])],
      in_hbm(erase_left.T), in_hbm(erase_right.T))


def bucket_kernel(rows, bins_at, grads_at, out, bins, grads, sems):
    for copy in fetch([(bins_at, bins), (grads_at, grads)], sems):
        copy.wait()
    cover, experts = bins.shape
    together = 128 // experts
    lanes = together * experts
    chunks = cover // together
    members = out.shape[0]
    before = jnp.where(
        lax.broadcasted_iota(jnp.int32, (lanes, lanes), 0)
        < lax.broadcasted_iota(jnp.int32, (lanes, lanes), 1),
        1.0, 0.0,
    ).astype(BF16)
    index = lax.broadcasted_iota(jnp.int32, (members, lanes), 0)
    slot = lax.broadcasted_iota(jnp.int32, (SLOTS, lanes), 0)
    expert = lax.broadcasted_iota(jnp.int32, (1, lanes), 1) % experts
    side = lambda ref, chunk: jnp.concatenate(
        [ref[chunk * together + k : chunk * together + k + 1, :] for k in range(together)], axis=1
    )
    base = jnp.zeros((members, 1), F32)
    total = jnp.zeros((members, 4 * SLOTS), F32)
    grads = grads[...].astype(F32)
    for chunk in range(chunks):
        place = side(bins, chunk)
        target = place // rows
        offset = place - target * rows
        mine = jnp.where(target == index, 1.0, 0.0)
        mine_low = mine.astype(BF16)
        earlier = jnp.dot(mine_low, before, preferred_element_type=F32) + base
        rank = jnp.sum(mine * earlier, axis=0, keepdims=True).astype(jnp.int32)
        base = base + jnp.sum(mine, axis=1, keepdims=True)
        high = offset // 256
        low = (offset - high * 256).astype(F32)
        code = (expert + high * SLOTS).astype(F32)
        hit = rank == slot
        spread = jnp.concatenate(
            [jnp.where(hit, v, 0.0) for v in (low, code, side(grads, chunk))]
            + [jnp.zeros(hit.shape, F32)],
            axis=0,
        ).astype(BF16)
        total = total + lax.dot_general(mine_low, spread, NT, preferred_element_type=F32)
    for k in range(out.shape[1]):
        out[:, k, :] = total[:, k * 128 : (k + 1) * 128].astype(BF16)


def bucket(cover_bins, bin_gradient, members, rows):
    bins, grads = cover_bins.T, bin_gradient.T
    return pl.pallas_call(
        functools.partial(bucket_kernel, rows),
        in_specs=[HBM, HBM],
        out_shape=jax.ShapeDtypeStruct((members, 4 * SLOTS // 128, 128), BF16),
        scratch_shapes=[
            pltpu.VMEM(bins.shape, bins.dtype),
            pltpu.VMEM(grads.shape, grads.dtype),
            pltpu.SemaphoreType.DMA((2,)),
        ],
        cost_estimate=cost(1e8, 1e5),
        compiler_params=params(),
        name="bucket_entries",
    )(in_hbm(bins), in_hbm(grads))


def spread_kernel(rows, reach, along, *refs):
    arrived, (out, fields) = refs[:3], refs[3:]
    half, group = pl.program_id(0), pl.program_id(1)
    together = COLS // SLOTS
    groups = fields.shape[1]

    @pl.when((half == 0) & (group == 0))
    def _():
        members = arrived[0].shape[0]
        repeat = jnp.where(
            lax.broadcasted_iota(jnp.int32, (SLOTS, COLS), 1) % SLOTS
            == lax.broadcasted_iota(jnp.int32, (SLOTS, COLS), 0),
            1.0, 0.0,
        ).astype(BF16)
        own = (
            lax.broadcasted_iota(jnp.int32, (members, COLS), 1) // SLOTS
            == lax.broadcasted_iota(jnp.int32, (members, COLS), 0) % together
        )
        shape = (groups, members)
        same = jnp.where(
            lax.broadcasted_iota(jnp.int32, shape, 1) // together
            == lax.broadcasted_iota(jnp.int32, shape, 0),
            1.0, 0.0,
        ).astype(BF16)
        for which, payload in enumerate(arrived):
            for k in range(3):
                first = k % 2 * SLOTS
                these = payload[:, k // 2, first : first + SLOTS]
                wide = jnp.dot(these, repeat, preferred_element_type=F32)
                wide = jnp.where(own, wide, 0.0).astype(BF16)
                fields[which, :, k * COLS : (k + 1) * COLS] = jnp.dot(
                    same, wide, preferred_element_type=F32
                )

    width = out.shape[1]
    square = lax.broadcasted_iota(jnp.int32, (width, width), 0)
    parts = ((reach, rows, 0), (0, reach, rows - reach), (reach + rows, reach, 0))
    for which, (start, count, first) in enumerate(parts):
        row = fields[which, pl.ds(group * 2 + (half + along[0]) % 2, 1), :]
        low = row[:, :COLS]
        code = row[:, COLS : 2 * COLS]
        value = row[:, 2 * COLS :]
        high = code >= SLOTS
        offset = (low + jnp.where(high, 256.0, 0.0)).astype(jnp.int32) - first
        slot = lax.broadcasted_iota(jnp.int32, code.shape, 1)
        column = (code - jnp.where(high, 1.0 * SLOTS, 0.0)).astype(jnp.int32)
        column = column + slot // SLOTS * SLOTS
        at_row = jnp.where(
            lax.broadcasted_iota(jnp.int32, (count, width), 0) == offset, 1.0, 0.0
        ).astype(BF16)
        at_column = jnp.where(square == column, value, 0.0).astype(BF16)
        out[start : start + count, :] = lax.dot_general(
            at_row, at_column, NT, preferred_element_type=F32
        ).astype(BF16)


def spread_entries(along, arrived, below, above, rows, reach):
    groups = arrived.shape[0] * SLOTS // COLS
    whole = pl.BlockSpec(arrived.shape, lambda h, i, along: (0, 0, 0))
    return pl.pallas_call(
        functools.partial(spread_kernel, rows, reach),
        grid_spec=pltpu.PrefetchScalarGridSpec(
            num_scalar_prefetch=1,
            grid=(2, groups // 2),
            in_specs=[whole] * 3,
            scratch_shapes=[pltpu.VMEM((3, groups, 3 * COLS), F32)],
            out_specs=pl.BlockSpec((None, rows + 2 * reach, COLS), lambda h, i, along: (h, 0, i)),
        ),
        out_shape=jax.ShapeDtypeStruct((2, rows + 2 * reach, groups // 2 * COLS), BF16),
        cost_estimate=cost(6e9, 8e6),
        compiler_params=params(),
        name="spread_entries",
    )(along, arrived, below, above)


def stage_weights(level, weight, expand):
    last = level == 0
    parts = [(weight, level)] + ([] if last else [(expand, level - 1)])

    def body(*refs):
        sems = refs[-1]
        pairs = [(refs[k].at[n], refs[len(parts) + k]) for k, (_, n) in enumerate(parts)]
        for copy in fetch(pairs, sems):
            copy.wait()

    return pl.pallas_call(
        body,
        in_specs=[HBM] * len(parts),
        out_specs=[VMEM] * len(parts),
        out_shape=[jax.ShapeDtypeStruct(a.shape[1:], a.dtype) for a, _ in parts],
        scratch_shapes=[pltpu.SemaphoreType.DMA((len(parts),))],
        cost_estimate=cost(1e9, 1e6),
        compiler_params=params(),
        name=f"stage_weights_{level}",
    )(*[in_hbm(a) for a, _ in parts])


def cut_edges(saved):
    _, rows, share = saved.shape
    count = sum(HALO_SAVED.values())

    def body(saved, first, last, sems):
        pairs = []
        for level, start in EDGE_START.items():
            size = HALO_SAVED[level]
            to = pl.ds(start, size)
            pairs.append((saved.at[level, pl.ds(0, size), :], first.at[to, :]))
            pairs.append((saved.at[level, pl.ds(rows - size, size), :], last.at[to, :]))
        for copy in fetch(pairs, sems):
            copy.wait()

    return pl.pallas_call(
        body,
        in_specs=[HBM],
        out_specs=[VMEM, VMEM],
        out_shape=[jax.ShapeDtypeStruct((count, share), BF16)] * 2,
        scratch_shapes=[pltpu.SemaphoreType.DMA((2 * len(EDGE_START),))],
        cost_estimate=cost(1e6, 6e5),
        compiler_params=params(),
        name="cut_edges",
    )(in_hbm(saved))


def pre_kernel(level, saved, low, high, weight, send, slope, value, act, shifted, kernel, sems):
    dilation = BASE_DILATION * 2**level
    halo, inner = HALO_SAVED[level], HALO_IN[level - 1]
    rows = value.shape[0]
    edge = slice(EDGE_START[level], EDGE_START[level] + halo)
    count = send.shape[0]
    taps = shifted.shape[0]
    columns = column_blocks(send.shape[1])
    batches = [[(saved.at[level], value)], []]
    for k, cols in enumerate(columns):
        batches.append([(weight.at[level, :, :, cols], kernel.at[k])])
    arrive = staged(batches, sems)
    for side, start in ((low, 0), (high, halo + rows)):
        act[start : start + halo, :], outside = gelu_parts(side[edge, :].astype(F32))
        if inner and start:
            slope[inner + rows :, :] = outside[:inner].astype(BF16)
        elif inner:
            slope[:inner, :] = outside[halo - inner :].astype(BF16)
    arrive()
    arrive()
    step = 64

    def part_of(k, _):
        start = pl.multiple_of(k * step, step)
        one, two = gelu_parts(value[pl.ds(start, step), :].astype(F32))
        act[pl.ds(pl.multiple_of(start + halo, 16), step), :] = one
        value[pl.ds(start, step), :] = two.astype(BF16)
        return 0

    lax.fori_loop(0, rows // step, part_of, 0)
    slope[inner : inner + rows, :] = value[...]
    for tap in range(taps):
        start = halo - HALO_IN[level] + (tap - 1) * dilation
        shifted[tap] = act[start : start + count, :].astype(BF16)
    for k, cols in enumerate(columns):
        arrive()
        total = None
        for tap in range(taps):
            part = jnp.dot(shifted[tap], kernel[k, tap], preferred_element_type=F32)
            total = part if total is None else total + part
        send[:, cols] = total.astype(BF16)


def pre_partial(level, saved, low, high, weights):
    rows, share = saved.shape[1:]
    count = rows + 2 * HALO_IN[level]
    halo = HALO_SAVED[level]
    _, taps, _, width = weights.shape
    blocks = width // COLS
    return pl.pallas_call(
        functools.partial(pre_kernel, level),
        in_specs=[HBM, VMEM, VMEM, HBM],
        out_specs=[VMEM, VMEM],
        out_shape=[
            jax.ShapeDtypeStruct((count, width), BF16),
            jax.ShapeDtypeStruct((rows + 2 * HALO_IN[level - 1], share), BF16),
        ],
        scratch_shapes=[
            pltpu.VMEM((rows, share), BF16),
            pltpu.VMEM((rows + 2 * halo, share), F32),
            pltpu.VMEM((taps, count, share), BF16),
            pltpu.VMEM((blocks, taps, share, COLS), BF16),
            pltpu.SemaphoreType.DMA((1 + blocks,)),
        ],
        cost_estimate=cost(5e9, 8e6),
        compiler_params=params(),
        name=f"pre_partial_{level}",
    )(in_hbm(saved), low, high, in_hbm(weights))


def pre_slope(level, flags, own, other, rows):
    count, width = own.shape
    blocks = pl.BlockSpec((count, COLS), lambda i, flags: (0, i))
    halo = HALO_IN[level]

    def body(flags, own, other, out):
        slope = gelu_parts(own[...].astype(F32) + other[...].astype(F32))[1]
        at = lax.broadcasted_iota(jnp.int32, slope.shape, 0)
        outside = ((at < halo) & (flags[0] != 0)) | ((at >= halo + rows) & (flags[1] != 0))
        out[...] = jnp.where(outside, 0.0, slope).astype(BF16)

    return pl.pallas_call(
        body,
        grid_spec=pltpu.PrefetchScalarGridSpec(
            num_scalar_prefetch=1, grid=(width // COLS,), in_specs=[blocks, blocks], out_specs=blocks
        ),
        out_shape=jax.ShapeDtypeStruct((count, width), BF16),
        cost_estimate=cost(4e9, 5e6),
        compiler_params=params(),
        name=f"pre_slope_{level}",
    )(flags, own, other)


def top_kernel(spread, vectors, expand, grad, send, matrix, held, kernel, rounded, sems):
    columns = column_blocks(grad.shape[1])
    batches = []
    for half in range(2):
        batches.append([
            (spread.at[half], matrix.at[half]),
            (vectors.at[:, half], held.at[half].reshape(vectors.shape[0], *vectors.shape[2:])),
        ])
    batches.append([(expand.at[expand.shape[0] - 1], kernel)])
    arrive = staged(batches, sems)
    arrive()
    for cols in columns:
        grad[:, cols] = jnp.dot(matrix[0], held[0, :, cols], preferred_element_type=F32)
    arrive()
    for cols in columns:
        top = grad[:, cols] + jnp.dot(
            matrix[1], held[1, :, cols], preferred_element_type=F32
        )
        grad[:, cols] = top
        rounded[:, cols] = top.astype(BF16)
    arrive()
    for cols in column_blocks(send.shape[1]):
        send[:, cols] = lax.dot_general(
            rounded[...], kernel[cols, :], NT, preferred_element_type=F32
        ).astype(BF16)


def top_gradient(spread, vectors, expand):
    _, count, depth = spread.shape
    share = vectors.shape[1]
    width = expand.shape[1]
    vectors = vectors.reshape(depth // SLOTS, 2, SLOTS, share)
    return pl.pallas_call(
        top_kernel,
        in_specs=[HBM] * 3,
        out_specs=[VMEM, VMEM],
        out_shape=[
            jax.ShapeDtypeStruct((count, share), F32),
            jax.ShapeDtypeStruct((count, width), BF16),
        ],
        scratch_shapes=[
            pltpu.VMEM((2, count, depth), BF16),
            pltpu.VMEM((2, depth, share), BF16),
            pltpu.VMEM((width, share), BF16),
            pltpu.VMEM((count, share), BF16),
            pltpu.SemaphoreType.DMA((5,)),
        ],
        cost_estimate=cost(5e9, 14e6),
        compiler_params=params(),
        name="top_gradient",
    )(*[in_hbm(a) for a in (spread, vectors, expand)])


def block_kernel(level, own, other, slope, weight, grad, outer, *rest):
    last = level == 0
    if last:
        out, pre, shifted = rest
    else:
        expand, out, send, pre, shifted = rest
    dilation = BASE_DILATION * 2**level
    count, share = out.shape
    trim = HALO_IN[level] - HALO_IN[level - 1]
    taps = weight.shape[0]
    pre[...] = (own[...].astype(F32) + other[...].astype(F32)) * slope[...].astype(F32)
    for tap in range(taps):
        start = trim - (tap - 1) * dilation
        shifted[tap] = pre[start : start + count, :].astype(BF16)
    middle = None
    for cols in column_blocks(share):
        total = None
        for tap in range(taps):
            part = lax.dot_general(
                shifted[tap], weight[tap, cols, :], NT, preferred_element_type=F32
            )
            total = part if total is None else total + part
        new = grad[trim : trim + count, cols] + total * outer[:, cols].astype(F32)
        if last:
            out[:, cols] = new.astype(BF16)
            continue
        out[:, cols] = new
        part = lax.dot_general(new.astype(BF16), expand[:, cols], NT, preferred_element_type=F32)
        middle = part if middle is None else middle + part
    if not last:
        send[...] = middle.astype(BF16)


def block_step(level, own, other, slope, weight, grad, outer, *expand):
    count_in, width = own.shape
    count, share = outer.shape
    taps = weight.shape[0]
    last = level == 0
    out_shape = [jax.ShapeDtypeStruct((count, share), BF16 if last else F32)]
    if not last:
        out_shape.append(jax.ShapeDtypeStruct((count, width), BF16))
    return pl.pallas_call(
        functools.partial(block_kernel, level),
        in_specs=[VMEM] * (6 + len(expand)),
        out_specs=[VMEM] * len(out_shape),
        out_shape=out_shape,
        scratch_shapes=[
            pltpu.VMEM((count_in, width), F32),
            pltpu.VMEM((taps, count, width), BF16),
        ],
        cost_estimate=cost(5e9, 14e6),
        compiler_params=params(),
        name=f"block_step_{level}",
    )(own, other, slope, weight, grad, outer, *expand)


def after(value, *earlier):
    return lax.optimization_barrier((value, *earlier))[0]


def along_head(vectors, place, first, second):
    count = vectors.shape[0]
    turn = place % 4
    same = lambda steps: [(a * 4 + z, a * 4 + (z - steps) % 4) for a in range(2) for z in range(4)]
    other = lax.ppermute(vectors, "head", [(k, (k + 4) % 8) for k in range(8)])
    both = jnp.concatenate([after(vectors, *first), other], axis=0)
    parts = [lax.ppermute(both, "head", same(k)) for k in (1, 2, 3)]
    parts = [after(both, *second)] + parts
    twice = jnp.concatenate(parts + parts, axis=0)
    return lax.dynamic_slice_in_dim(twice, (4 - turn) % 4 * 2 * count, 8 * count, 0)


def per_device(
    inputs_saved,
    conv_weight,
    expand_weight,
    head_weight,
    batch_of,
    erase_left,
    erase_right,
    bin_gradient,
    cover_bins,
):
    members = lax.axis_size(GROUP_AXES)
    layers, rows, share = inputs_saved.shape
    member = lax.axis_index(GROUP_AXES)
    chan_place = lax.axis_index("chan")
    up = [(k, k + 1) for k in range(members - 1)]
    down = [(k + 1, k) for k in range(members - 1)]
    swap = [(0, 1), (1, 0)]
    levels = list(reversed(range(layers)))

    place = lax.axis_index("head")
    along = place // 4
    vectors = head_vectors(
        chan_place[None].astype(jnp.int32), head_weight, batch_of, erase_left, erase_right, share
    )
    payload = bucket(cover_bins, bin_gradient, members, rows)
    arrived = lax.all_to_all(
        after(payload, vectors), GROUP_AXES, split_axis=0, concat_axis=0, tiled=True
    )
    first, final = cut_edges(after(inputs_saved, payload))
    low = lax.ppermute(final, GROUP_AXES, up)
    high = lax.ppermute(first, GROUP_AXES, down)
    flags = jnp.stack([member == 0, member == members - 1]).astype(jnp.int32)
    sends, outers, others = {}, {}, {}

    def begin(n, *earlier):
        sends[n], outers[n] = pre_partial(
            n, inputs_saved, after(low, *earlier), high, conv_weight
        )

    def exchange(n, *earlier):
        others[n] = lax.ppermute(after(sends[n], *earlier), "chan", swap)

    begin(levels[0])
    exchange(levels[0])
    ring = along_head(vectors, place, (arrived, first), (sends[levels[0]],))
    gathered = lax.all_gather(ring, "pos", tiled=True)
    passed = after(arrived, sends[levels[0]])
    below = lax.ppermute(passed, GROUP_AXES, up)
    above = lax.ppermute(passed, GROUP_AXES, down)
    begin(levels[1], ring)
    exchange(levels[1])
    reach = HALO_IN[layers - 1]
    begin(levels[2], sends[levels[1]], below, above)
    spread = spread_entries(
        along[None].astype(jnp.int32), after(arrived, sends[levels[2]], others[levels[0]]),
        below, above, rows, reach,
    )
    gathered = after(gathered, sends[levels[2]], others[levels[1]])
    grad, send = top_gradient(spread, gathered, expand_weight)
    exchange(levels[2])
    send = after(send, others[levels[2]])
    for n in levels:
        other = lax.ppermute(send, "chan", swap)
        slope = pre_slope(n, flags, sends[n], after(others[n], send), rows)
        weights = stage_weights(n, after(conv_weight, slope), expand_weight)
        outs = block_step(n, send, other, slope, weights[0], grad, outers[n], *weights[1:])
        if n:
            grad, send = outs
    return outs[0]


def solution(mesh):
    return jax.shard_map(
        per_device,
        mesh=mesh,
        in_specs=(
            P(None, ("pos", "head"), "chan"),
            P(None, None, "chan", None),
            P(None, None, "chan"),
            P(("pos", "head"), None),
            P(("pos", "head")),
            P(),
            P(),
            P(("pos", "head"), None),
            P(("pos", "head"), None),
        ),
        out_specs=P(("pos", "head"), "chan"),
        check_vma=False,
    )
```

```python
import functools

import jax
import jax.numpy as jnp
from jax import lax
from jax.experimental import pallas as pl
from jax.experimental.pallas import tpu as pltpu
from jax.sharding import PartitionSpec as P

BASE_DILATION = 4
RANK = 8
SLOTS = 64
COLS = 256
GROUP_AXES = ("pos", "head")
HALO_IN = {2: 32, 1: 16, 0: 8, -1: 0}
HALO_SAVED = {2: 48, 1: 32, 0: 16}
EDGE_START = {1: 0, 0: 32, 2: 48}
F32 = jnp.float32
BF16 = jnp.bfloat16
NT = (((1,), (1,)), ((), ()))


def cost(flops, bytes_accessed, transcendentals=0):
    return pl.CostEstimate(
        flops=int(flops / 100), bytes_accessed=int(bytes_accessed / 100), transcendentals=0
    )


def params():
    return pltpu.CompilerParams(vmem_limit_bytes=28 * 2**20)


VMEM = pl.BlockSpec(memory_space=pltpu.VMEM)
HBM = pl.BlockSpec(memory_space=pltpu.HBM)
SMEM = pl.BlockSpec(memory_space=pltpu.SMEM)
ROOT_HALF = 0.7071067811865476
DENSITY = 0.3989422804014327


def in_hbm(value):
    return pltpu.with_memory_space_constraint(value, pltpu.HBM)


def fetch(pairs, sems):
    copies = [pltpu.make_async_copy(a, b, sems.at[k]) for k, (a, b) in enumerate(pairs)]
    for copy in copies:
        copy.start()
    return copies


def staged(batches, sems):
    made, k = [], 0
    for batch in batches:
        made.append([pltpu.make_async_copy(a, b, sems.at[k + i]) for i, (a, b) in enumerate(batch)])
        k += len(batch)
    ahead = iter(made)

    def begin():
        for copy in next(ahead, ()):
            copy.start()

    behind = iter(made)

    def arrive():
        for copy in next(behind):
            copy.wait()
        begin()

    begin()
    begin()
    return arrive


def column_blocks(share):
    return [slice(start, start + COLS) for start in range(0, share, COLS)]


def gelu_parts(value):
    half = 0.5 * (1.0 + lax.erf(value * ROOT_HALF))
    return value * half, half + value * jnp.exp(-0.5 * value * value) * DENSITY


def vectors_kernel(place, weight, share, batch, left, right, out):
    projected = lax.dot_general(left[...], weight[...], NT, preferred_element_type=F32)
    column = lax.broadcasted_iota(jnp.int32, projected.shape, 0) // RANK
    kept = jnp.where(column == batch[...], projected, 0.0)
    removed = lax.dot_general(
        kept, right[...].astype(F32), (((0,), (0,)), ((), ())),
        precision=lax.Precision.HIGHEST, preferred_element_type=F32,
    )
    out[...] = (share[...].astype(F32) - removed).astype(BF16)


def head_vectors(place, head_weight, batch_of, erase_left, erase_right, share):
    count, channels = head_weight.shape
    factors = erase_left.shape[1]
    whole = lambda i, place: (0, 0)
    mine = lambda i, place: (0, place[0])
    return pl.pallas_call(
        vectors_kernel,
        grid_spec=pltpu.PrefetchScalarGridSpec(
            num_scalar_prefetch=1,
            grid=(1,),
            in_specs=[
                pl.BlockSpec((count, channels), whole),
                pl.BlockSpec((count, share), mine),
                pl.BlockSpec((1, count), whole),
                pl.BlockSpec((factors, channels), whole),
                pl.BlockSpec((factors, share), mine),
            ],
            out_specs=pl.BlockSpec((count, share), whole),
        ),
        out_shape=jax.ShapeDtypeStruct((count, share), BF16),
        cost_estimate=cost(1e9, 1e6),
        compiler_params=params(),
        name="head_vectors",
    )(place, *[in_hbm(a) for a in (head_weight, head_weight, batch_of[None, :])],
      in_hbm(erase_left.T), in_hbm(erase_right.T))


def bucket_kernel(rows, bins_at, grads_at, out, bins, grads, sems):
    for copy in fetch([(bins_at, bins), (grads_at, grads)], sems):
        copy.wait()
    cover, experts = bins.shape
    together = 128 // experts
    lanes = together * experts
    chunks = cover // together
    members = out.shape[0]
    before = jnp.where(
        lax.broadcasted_iota(jnp.int32, (lanes, lanes), 0)
        < lax.broadcasted_iota(jnp.int32, (lanes, lanes), 1),
        1.0, 0.0,
    ).astype(BF16)
    index = lax.broadcasted_iota(jnp.int32, (members, lanes), 0)
    slot = lax.broadcasted_iota(jnp.int32, (SLOTS, lanes), 0)
    expert = lax.broadcasted_iota(jnp.int32, (1, lanes), 1) % experts
    side = lambda ref, chunk: jnp.concatenate(
        [ref[chunk * together + k : chunk * together + k + 1, :] for k in range(together)], axis=1
    )
    base = jnp.zeros((members, 1), F32)
    total = jnp.zeros((members, 4 * SLOTS), F32)
    grads = grads[...].astype(F32)
    for chunk in range(chunks):
        place = side(bins, chunk)
        target = place // rows
        offset = place - target * rows
        mine = jnp.where(target == index, 1.0, 0.0)
        mine_low = mine.astype(BF16)
        earlier = jnp.dot(mine_low, before, preferred_element_type=F32) + base
        rank = jnp.sum(mine * earlier, axis=0, keepdims=True).astype(jnp.int32)
        base = base + jnp.sum(mine, axis=1, keepdims=True)
        high = offset // 256
        low = (offset - high * 256).astype(F32)
        code = (expert + high * SLOTS).astype(F32)
        hit = rank == slot
        spread = jnp.concatenate(
            [jnp.where(hit, v, 0.0) for v in (low, code, side(grads, chunk))]
            + [jnp.zeros(hit.shape, F32)],
            axis=0,
        ).astype(BF16)
        total = total + lax.dot_general(mine_low, spread, NT, preferred_element_type=F32)
    for k in range(out.shape[1]):
        out[:, k, :] = total[:, k * 128 : (k + 1) * 128].astype(BF16)


def bucket(cover_bins, bin_gradient, members, rows):
    bins, grads = cover_bins.T, bin_gradient.T
    return pl.pallas_call(
        functools.partial(bucket_kernel, rows),
        in_specs=[HBM, HBM],
        out_shape=jax.ShapeDtypeStruct((members, 4 * SLOTS // 128, 128), BF16),
        scratch_shapes=[
            pltpu.VMEM(bins.shape, bins.dtype),
            pltpu.VMEM(grads.shape, grads.dtype),
            pltpu.SemaphoreType.DMA((2,)),
        ],
        cost_estimate=cost(1e8, 1e5),
        compiler_params=params(),
        name="bucket_entries",
    )(in_hbm(bins), in_hbm(grads))


def spread_kernel(rows, reach, along, *refs):
    arrived, (out, fields) = refs[:3], refs[3:]
    half, group = pl.program_id(0), pl.program_id(1)
    together = COLS // SLOTS
    groups = fields.shape[1]

    @pl.when((half == 0) & (group == 0))
    def _():
        members = arrived[0].shape[0]
        repeat = jnp.where(
            lax.broadcasted_iota(jnp.int32, (SLOTS, COLS), 1) % SLOTS
            == lax.broadcasted_iota(jnp.int32, (SLOTS, COLS), 0),
            1.0, 0.0,
        ).astype(BF16)
        own = (
            lax.broadcasted_iota(jnp.int32, (members, COLS), 1) // SLOTS
            == lax.broadcasted_iota(jnp.int32, (members, COLS), 0) % together
        )
        shape = (groups, members)
        same = jnp.where(
            lax.broadcasted_iota(jnp.int32, shape, 1) // together
            == lax.broadcasted_iota(jnp.int32, shape, 0),
            1.0, 0.0,
        ).astype(BF16)
        for which, payload in enumerate(arrived):
            for k in range(3):
                first = k % 2 * SLOTS
                these = payload[:, k // 2, first : first + SLOTS]
                wide = jnp.dot(these, repeat, preferred_element_type=F32)
                wide = jnp.where(own, wide, 0.0).astype(BF16)
                fields[which, :, k * COLS : (k + 1) * COLS] = jnp.dot(
                    same, wide, preferred_element_type=F32
                )

    width = out.shape[1]
    square = lax.broadcasted_iota(jnp.int32, (width, width), 0)
    parts = ((reach, rows, 0), (0, reach, rows - reach), (reach + rows, reach, 0))
    for which, (start, count, first) in enumerate(parts):
        row = fields[which, pl.ds(group * 2 + (half + along[0]) % 2, 1), :]
        low = row[:, :COLS]
        code = row[:, COLS : 2 * COLS]
        value = row[:, 2 * COLS :]
        high = code >= SLOTS
        offset = (low + jnp.where(high, 256.0, 0.0)).astype(jnp.int32) - first
        slot = lax.broadcasted_iota(jnp.int32, code.shape, 1)
        column = (code - jnp.where(high, 1.0 * SLOTS, 0.0)).astype(jnp.int32)
        column = column + slot // SLOTS * SLOTS
        at_row = jnp.where(
            lax.broadcasted_iota(jnp.int32, (count, width), 0) == offset, 1.0, 0.0
        ).astype(BF16)
        at_column = jnp.where(square == column, value, 0.0).astype(BF16)
        out[start : start + count, :] = lax.dot_general(
            at_row, at_column, NT, preferred_element_type=F32
        ).astype(BF16)


def spread_entries(along, arrived, below, above, rows, reach):
    groups = arrived.shape[0] * SLOTS // COLS
    whole = pl.BlockSpec(arrived.shape, lambda h, i, along: (0, 0, 0))
    return pl.pallas_call(
        functools.partial(spread_kernel, rows, reach),
        grid_spec=pltpu.PrefetchScalarGridSpec(
            num_scalar_prefetch=1,
            grid=(2, groups // 2),
            in_specs=[whole] * 3,
            scratch_shapes=[pltpu.VMEM((3, groups, 3 * COLS), F32)],
            out_specs=pl.BlockSpec((None, rows + 2 * reach, COLS), lambda h, i, along: (h, 0, i)),
        ),
        out_shape=jax.ShapeDtypeStruct((2, rows + 2 * reach, groups // 2 * COLS), BF16),
        cost_estimate=cost(6e9, 8e6),
        compiler_params=params(),
        name="spread_entries",
    )(along, arrived, below, above)


def stage_weights(level, weight, expand):
    last = level == 0
    parts = [(weight, level)] + ([] if last else [(expand, level - 1)])

    def body(*refs):
        sems = refs[-1]
        pairs = [(refs[k].at[n], refs[len(parts) + k]) for k, (_, n) in enumerate(parts)]
        for copy in fetch(pairs, sems):
            copy.wait()

    return pl.pallas_call(
        body,
        in_specs=[HBM] * len(parts),
        out_specs=[VMEM] * len(parts),
        out_shape=[jax.ShapeDtypeStruct(a.shape[1:], a.dtype) for a, _ in parts],
        scratch_shapes=[pltpu.SemaphoreType.DMA((len(parts),))],
        cost_estimate=cost(1e9, 1e6),
        compiler_params=params(),
        name=f"stage_weights_{level}",
    )(*[in_hbm(a) for a, _ in parts])


def cut_edges(saved):
    _, rows, share = saved.shape
    count = sum(HALO_SAVED.values())

    def body(saved, first, last, sems):
        pairs = []
        for level, start in EDGE_START.items():
            size = HALO_SAVED[level]
            to = pl.ds(start, size)
            pairs.append((saved.at[level, pl.ds(0, size), :], first.at[to, :]))
            pairs.append((saved.at[level, pl.ds(rows - size, size), :], last.at[to, :]))
        for copy in fetch(pairs, sems):
            copy.wait()

    return pl.pallas_call(
        body,
        in_specs=[HBM],
        out_specs=[VMEM, VMEM],
        out_shape=[jax.ShapeDtypeStruct((count, share), BF16)] * 2,
        scratch_shapes=[pltpu.SemaphoreType.DMA((2 * len(EDGE_START),))],
        cost_estimate=cost(1e6, 6e5),
        compiler_params=params(),
        name="cut_edges",
    )(in_hbm(saved))


def pre_kernel(level, saved, low, high, weight, send, slope, value, act, shifted, kernel, sems):
    dilation = BASE_DILATION * 2**level
    halo, inner = HALO_SAVED[level], HALO_IN[level - 1]
    rows = value.shape[0]
    edge = slice(EDGE_START[level], EDGE_START[level] + halo)
    count = send.shape[0]
    taps = shifted.shape[0]
    columns = column_blocks(send.shape[1])
    batches = [[(saved.at[level], value)], []]
    for k, cols in enumerate(columns):
        batches.append([(weight.at[level, :, :, cols], kernel.at[k])])
    arrive = staged(batches, sems)
    for side, start in ((low, 0), (high, halo + rows)):
        act[start : start + halo, :], outside = gelu_parts(side[edge, :].astype(F32))
        if inner and start:
            slope[inner + rows :, :] = outside[:inner].astype(BF16)
        elif inner:
            slope[:inner, :] = outside[halo - inner :].astype(BF16)
    arrive()
    arrive()
    step = 64

    def part_of(k, _):
        start = pl.multiple_of(k * step, step)
        one, two = gelu_parts(value[pl.ds(start, step), :].astype(F32))
        act[pl.ds(pl.multiple_of(start + halo, 16), step), :] = one
        value[pl.ds(start, step), :] = two.astype(BF16)
        return 0

    lax.fori_loop(0, rows // step, part_of, 0)
    slope[inner : inner + rows, :] = value[...]
    for tap in range(taps):
        start = halo - HALO_IN[level] + (tap - 1) * dilation
        shifted[tap] = act[start : start + count, :].astype(BF16)
    for k, cols in enumerate(columns):
        arrive()
        total = None
        for tap in range(taps):
            part = jnp.dot(shifted[tap], kernel[k, tap], preferred_element_type=F32)
            total = part if total is None else total + part
        send[:, cols] = total.astype(BF16)


def pre_partial(level, saved, low, high, weights):
    rows, share = saved.shape[1:]
    count = rows + 2 * HALO_IN[level]
    halo = HALO_SAVED[level]
    _, taps, _, width = weights.shape
    blocks = width // COLS
    return pl.pallas_call(
        functools.partial(pre_kernel, level),
        in_specs=[HBM, VMEM, VMEM, HBM],
        out_specs=[VMEM, VMEM],
        out_shape=[
            jax.ShapeDtypeStruct((count, width), BF16),
            jax.ShapeDtypeStruct((rows + 2 * HALO_IN[level - 1], share), BF16),
        ],
        scratch_shapes=[
            pltpu.VMEM((rows, share), BF16),
            pltpu.VMEM((rows + 2 * halo, share), F32),
            pltpu.VMEM((taps, count, share), BF16),
            pltpu.VMEM((blocks, taps, share, COLS), BF16),
            pltpu.SemaphoreType.DMA((1 + blocks,)),
        ],
        cost_estimate=cost(5e9, 8e6),
        compiler_params=params(),
        name=f"pre_partial_{level}",
    )(in_hbm(saved), low, high, in_hbm(weights))


def pre_slope(level, flags, own, other, rows):
    count, width = own.shape
    blocks = pl.BlockSpec((count, COLS), lambda i, flags: (0, i))
    halo = HALO_IN[level]

    def body(flags, own, other, out):
        slope = gelu_parts(own[...].astype(F32) + other[...].astype(F32))[1]
        at = lax.broadcasted_iota(jnp.int32, slope.shape, 0)
        outside = ((at < halo) & (flags[0] != 0)) | ((at >= halo + rows) & (flags[1] != 0))
        out[...] = jnp.where(outside, 0.0, slope).astype(BF16)

    return pl.pallas_call(
        body,
        grid_spec=pltpu.PrefetchScalarGridSpec(
            num_scalar_prefetch=1, grid=(width // COLS,), in_specs=[blocks, blocks], out_specs=blocks
        ),
        out_shape=jax.ShapeDtypeStruct((count, width), BF16),
        cost_estimate=cost(4e9, 5e6),
        compiler_params=params(),
        name=f"pre_slope_{level}",
    )(flags, own, other)


def top_kernel(spread, vectors, expand, grad, send, matrix, held, kernel, rounded, sems):
    columns = column_blocks(grad.shape[1])
    batches = []
    for half in range(2):
        batches.append([
            (spread.at[half], matrix.at[half]),
            (vectors.at[:, half], held.at[half].reshape(vectors.shape[0], *vectors.shape[2:])),
        ])
    batches.append([(expand.at[expand.shape[0] - 1], kernel)])
    arrive = staged(batches, sems)
    arrive()
    for cols in columns:
        grad[:, cols] = jnp.dot(matrix[0], held[0, :, cols], preferred_element_type=F32)
    arrive()
    for cols in columns:
        top = grad[:, cols] + jnp.dot(
            matrix[1], held[1, :, cols], preferred_element_type=F32
        )
        grad[:, cols] = top
        rounded[:, cols] = top.astype(BF16)
    arrive()
    for cols in column_blocks(send.shape[1]):
        send[:, cols] = lax.dot_general(
            rounded[...], kernel[cols, :], NT, preferred_element_type=F32
        ).astype(BF16)


def top_gradient(spread, vectors, expand):
    _, count, depth = spread.shape
    share = vectors.shape[1]
    width = expand.shape[1]
    vectors = vectors.reshape(depth // SLOTS, 2, SLOTS, share)
    return pl.pallas_call(
        top_kernel,
        in_specs=[HBM] * 3,
        out_specs=[VMEM, VMEM],
        out_shape=[
            jax.ShapeDtypeStruct((count, share), F32),
            jax.ShapeDtypeStruct((count, width), BF16),
        ],
        scratch_shapes=[
            pltpu.VMEM((2, count, depth), BF16),
            pltpu.VMEM((2, depth, share), BF16),
            pltpu.VMEM((width, share), BF16),
            pltpu.VMEM((count, share), BF16),
            pltpu.SemaphoreType.DMA((5,)),
        ],
        cost_estimate=cost(5e9, 14e6),
        compiler_params=params(),
        name="top_gradient",
    )(*[in_hbm(a) for a in (spread, vectors, expand)])


def block_kernel(level, own, other, slope, weight, grad, outer, *rest):
    last = level == 0
    if last:
        out, pre, shifted = rest
    else:
        expand, out, send, pre, shifted = rest
    dilation = BASE_DILATION * 2**level
    count, share = out.shape
    trim = HALO_IN[level] - HALO_IN[level - 1]
    taps = weight.shape[0]
    pre[...] = (own[...].astype(F32) + other[...].astype(F32)) * slope[...].astype(F32)
    for tap in range(taps):
        start = trim - (tap - 1) * dilation
        shifted[tap] = pre[start : start + count, :].astype(BF16)
    middle = None
    for cols in column_blocks(share):
        total = None
        for tap in range(taps):
            part = lax.dot_general(
                shifted[tap], weight[tap, cols, :], NT, preferred_element_type=F32
            )
            total = part if total is None else total + part
        new = grad[trim : trim + count, cols] + total * outer[:, cols].astype(F32)
        if last:
            out[:, cols] = new.astype(BF16)
            continue
        out[:, cols] = new
        part = lax.dot_general(new.astype(BF16), expand[:, cols], NT, preferred_element_type=F32)
        middle = part if middle is None else middle + part
    if not last:
        send[...] = middle.astype(BF16)


def block_step(level, own, other, slope, weight, grad, outer, *expand):
    count_in, width = own.shape
    count, share = outer.shape
    taps = weight.shape[0]
    last = level == 0
    out_shape = [jax.ShapeDtypeStruct((count, share), BF16 if last else F32)]
    if not last:
        out_shape.append(jax.ShapeDtypeStruct((count, width), BF16))
    return pl.pallas_call(
        functools.partial(block_kernel, level),
        in_specs=[VMEM] * (6 + len(expand)),
        out_specs=[VMEM] * len(out_shape),
        out_shape=out_shape,
        scratch_shapes=[
            pltpu.VMEM((count_in, width), F32),
            pltpu.VMEM((taps, count, width), BF16),
        ],
        cost_estimate=cost(5e9, 14e6),
        compiler_params=params(),
        name=f"block_step_{level}",
    )(own, other, slope, weight, grad, outer, *expand)


def after(value, *earlier):
    return lax.optimization_barrier((value, *earlier))[0]


def along_head(vectors, place, first, second):
    count = vectors.shape[0]
    turn = place % 4
    same = lambda steps: [(a * 4 + z, a * 4 + (z - steps) % 4) for a in range(2) for z in range(4)]
    other = lax.ppermute(vectors, "head", [(k, (k + 4) % 8) for k in range(8)])
    both = jnp.concatenate([after(vectors, *first), other], axis=0)
    parts = [lax.ppermute(both, "head", same(k)) for k in (1, 2, 3)]
    parts = [after(both, *second)] + parts
    twice = jnp.concatenate(parts + parts, axis=0)
    return lax.dynamic_slice_in_dim(twice, (4 - turn) % 4 * 2 * count, 8 * count, 0)


def per_device(
    inputs_saved,
    conv_weight,
    expand_weight,
    head_weight,
    batch_of,
    erase_left,
    erase_right,
    bin_gradient,
    cover_bins,
):
    members = lax.axis_size(GROUP_AXES)
    layers, rows, share = inputs_saved.shape
    member = lax.axis_index(GROUP_AXES)
    chan_place = lax.axis_index("chan")
    up = [(k, k + 1) for k in range(members - 1)]
    down = [(k + 1, k) for k in range(members - 1)]
    swap = [(0, 1), (1, 0)]
    levels = list(reversed(range(layers)))

    place = lax.axis_index("head")
    along = place // 4
    vectors = head_vectors(
        chan_place[None].astype(jnp.int32), head_weight, batch_of, erase_left, erase_right, share
    )
    payload = bucket(cover_bins, bin_gradient, members, rows)
    arrived = lax.all_to_all(
        after(payload, vectors), GROUP_AXES, split_axis=0, concat_axis=0, tiled=True
    )
    first, final = cut_edges(after(inputs_saved, payload))
    low = lax.ppermute(final, GROUP_AXES, up)
    high = lax.ppermute(first, GROUP_AXES, down)
    flags = jnp.stack([member == 0, member == members - 1]).astype(jnp.int32)
    sends, outers, others = {}, {}, {}

    def begin(n, *earlier):
        sends[n], outers[n] = pre_partial(
            n, inputs_saved, after(low, *earlier), high, conv_weight
        )

    def exchange(n, *earlier):
        others[n] = lax.ppermute(after(sends[n], *earlier), "chan", swap)

    below = lax.ppermute(arrived, GROUP_AXES, up)
    above = lax.ppermute(arrived, GROUP_AXES, down)
    begin(levels[0], below, above)
    exchange(levels[0])
    ring = along_head(vectors, place, (arrived, first), (sends[levels[0]],))
    gathered = lax.all_gather(ring, "pos", tiled=True)
    begin(levels[1], ring)
    exchange(levels[1])
    reach = HALO_IN[layers - 1]
    spread = spread_entries(
        along[None].astype(jnp.int32), after(arrived, sends[levels[1]]), below, above, rows, reach
    )
    begin(levels[2], spread, others[levels[0]])
    gathered = after(gathered, sends[levels[2]], others[levels[1]])
    grad, send = top_gradient(spread, gathered, expand_weight)
    exchange(levels[2])
    send = after(send, others[levels[2]])
    for n in levels:
        other = lax.ppermute(send, "chan", swap)
        slope = pre_slope(n, flags, sends[n], after(others[n], send), rows)
        weights = stage_weights(n, after(conv_weight, slope), expand_weight)
        outs = block_step(n, send, other, slope, weights[0], grad, outers[n], *weights[1:])
        if n:
            grad, send = outs
    return outs[0]


def solution(mesh):
    return jax.shard_map(
        per_device,
        mesh=mesh,
        in_specs=(
            P(None, ("pos", "head"), "chan"),
            P(None, None, "chan", None),
            P(None, None, "chan"),
            P(("pos", "head"), None),
            P(("pos", "head")),
            P(),
            P(),
            P(("pos", "head"), None),
            P(("pos", "head"), None),
        ),
        out_specs=P(("pos", "head"), "chan"),
        check_vma=False,
    )
```
